32 devices in a mesh: groups: 1, row: 32 (over z, y, x, core), col: 1.
Axes of the slice: x: 2, y: 2, z: 4, core: 2. Of those that a mesh axis runs over, the one named last changes fastest.
Arguments:
- pair_map: bfloat16 [128, 128, 288], P(('groups', 'col'), 'row'), may hold values from -10 to 10
- row_gain: float32 [288], replicated, may hold values from 0.1 to 1.9
- row_proj: bfloat16 [288, 1152], replicated, may hold values from -0.5 to 0.5
- row_gate_bias: float32 [288], replicated, may hold values from -4 to 4
- row_out: bfloat16 [288, 288], replicated, may hold values from -0.375 to 0.375
- col_gain: float32 [288], replicated, may hold values from 0.1 to 1.9
- col_proj: bfloat16 [288, 1152], replicated, may hold values from -0.5 to 0.5
- col_gate_bias: float32 [288], replicated, may hold values from -4 to 4
- col_out: bfloat16 [288, 288], replicated, may hold values from -0.375 to 0.375
Outputs:
- updated_map: bfloat16 [128, 128, 288], P(('groups', 'col'), 'row')
The draws below stay inside these ranges and needn't reach their ends.
All inputs are finite; a program needn't handle non-finite values.
Results may differ from the reference program's by a relative error of at most 0.006.
Values may be sent and summed in bfloat16 or wider, within the bound.
A program may use at most 64 MiB of HBM per device.

```python
import math
import jax
import jax.numpy as jnp
from jax import lax

WIDTH = 288
HEADS = 8
LENGTH = 128


def drawn_projection(key, salt):
    softmax_weights = jax.random.truncated_normal(jax.random.fold_in(key, salt), -2.5, 2.5, (WIDTH, 4 * WIDTH), jnp.float32)
    softmax_weights = softmax_weights / math.sqrt(WIDTH)
    return softmax_weights


def draw_pair_map(key, part):
    ground = jax.random.truncated_normal(jax.random.fold_in(key, 11), -6.0, 6.0, (LENGTH, LENGTH, WIDTH), jnp.float32)
    return ground.astype(jnp.bfloat16)


def draw_row_proj(key, part):
    return drawn_projection(key, 21).astype(jnp.bfloat16)


def draw_col_proj(key, part):
    return drawn_projection(key, 37).astype(jnp.bfloat16)


def normal_values(key, dims, scale, bound, kind=jnp.bfloat16):
    result = scale * jax.random.normal(key, dims, jnp.float32)
    return jnp.clip(result, min=-bound, max=bound).astype(kind)


def setup_inputs(seed: int = 0, part: int = 0) -> dict:
    seeds = jax.random.split(jax.random.key(seed), 10)
    part_keys = jax.random.split(jax.random.fold_in(seeds[9], part), 10)
    return {
        "pair_map": draw_pair_map(jax.random.fold_in(jax.random.fold_in(seeds[9], part), 71), part),
        "row_gain": jnp.clip(1.0 + 0.18 * jax.random.normal(seeds[1], (WIDTH,), jnp.float32), 0.1, 1.9),
        "row_proj": draw_row_proj(jax.random.fold_in(seeds[9], 71), part),
        "row_gate_bias": normal_values(seeds[3], (WIDTH,), 1.0, 4.0, jnp.float32),
        "row_out": normal_values(seeds[4], (WIDTH, WIDTH), WIDTH ** -0.5, 0.375),
        "col_gain": jnp.clip(1.0 + 0.18 * jax.random.normal(seeds[5], (WIDTH,), jnp.float32), 0.1, 1.9),
        "col_proj": draw_col_proj(jax.random.fold_in(seeds[9], 71), part),
        "col_gate_bias": normal_values(seeds[7], (WIDTH,), 1.0, 4.0, jnp.float32),
        "col_out": normal_values(seeds[8], (WIDTH, WIDTH), WIDTH ** -0.5, 0.375),
    }


def attend_rows(block, gain, w_proj, gate_bias, w_out):
    width = block.shape[-1]
    head_count = HEADS
    per_head_width = width // head_count
    source = block.astype(jnp.float32)
    average = lax.optimization_barrier(jnp.mean(source, -1, keepdims=True))
    centred = source - average
    spread = lax.optimization_barrier(jnp.mean(centred * centred, -1, keepdims=True))
    normed = (centred * lax.rsqrt(spread + 1e-05) * gain).astype(jnp.bfloat16)
    projected = jnp.dot(normed.reshape(-1, width), w_proj, preferred_element_type=jnp.float32)
    projected = projected.reshape(block.shape[:-1] + (4 * width,))
    query_rows = projected[..., :width].astype(jnp.bfloat16).astype(jnp.float32)
    key_rows = projected[..., width:2 * width].astype(jnp.bfloat16).astype(jnp.float32)
    value_rows = projected[..., 2 * width:3 * width].astype(jnp.bfloat16).astype(jnp.float32)
    gating = jax.nn.sigmoid(projected[..., 3 * width:] + gate_bias)
    score_scale_factor = 1.0 / per_head_width ** 0.5
    head_outputs = []
    for head_index in range(head_count):
        lower_start = head_index * per_head_width
        logit_matrix = jnp.einsum('duv,dtv->dut', query_rows[..., lower_start:lower_start + per_head_width], key_rows[..., lower_start:lower_start + per_head_width]) * score_scale_factor
        softmax_weights = jax.nn.softmax(logit_matrix, -1).astype(jnp.bfloat16).astype(jnp.float32)
        head_outputs.append(jnp.einsum('twn,tnl->twl', softmax_weights, value_rows[..., lower_start:lower_start + per_head_width]))
    mixed = jnp.concatenate(head_outputs, -1)
    gated = (mixed * gating).astype(jnp.bfloat16)
    changes = jnp.dot(gated.reshape(-1, width), w_out, preferred_element_type=jnp.float32).reshape(block.shape)
    return (source + changes).astype(jnp.bfloat16)

def axial(pair_map, gain, w_proj, gate_bias, w_out):
    blocks = pair_map.reshape(LENGTH // 16, 16, LENGTH, WIDTH)
    done = lax.map(lambda piece: attend_rows(piece, gain, w_proj, gate_bias, w_out), blocks)
    return done.reshape(LENGTH, LENGTH, WIDTH)

def reference(pair_map, row_gain, row_proj, row_gate_bias, row_out, col_gain, col_proj, col_gate_bias, col_out):
    row_done = axial(pair_map, row_gain, row_proj, row_gate_bias, row_out)
    turned = jnp.transpose(row_done, (1, 0, 2))
    col_done = axial(turned, col_gain, col_proj, col_gate_bias, col_out)
    return jnp.transpose(col_done, (1, 0, 2))
```

```python
import functools
import math

import jax
import jax.numpy as jnp
from jax import lax
from jax.experimental import pallas as pl
from jax.experimental.pallas import tpu as pltpu
from jax.sharding import PartitionSpec as P

HEADS = 8
LANES = 128
VMEM_LIMIT = 32 * 2**20
F32 = jnp.float32
BF16 = jnp.bfloat16
MESH = pl.DeviceIdType.MESH


def ceil_to(value, step):
    return -(-value // step) * step


def nt(a, b):
    return lax.dot_general(a, b, (((1,), (1,)), ((), ())), preferred_element_type=F32)


def tn(a, b):
    return lax.dot_general(a, b, (((0,), (0,)), ((), ())), preferred_element_type=F32)


def nn(a, b):
    return jnp.dot(a, b, preferred_element_type=F32)


class Sizes:
    def __init__(self, width):
        self.width = width
        self.head = width // HEADS
        self.pad_head = ceil_to(self.head + 1, 16)
        self.pad_key = LANES // (LANES // self.head)
        while LANES % self.pad_key:
            self.pad_key += 1
        self.rows = HEADS * self.pad_head
        self.keys = HEADS * self.pad_key
        self.lanes = ceil_to(width, LANES)
        self.chunks = self.lanes // LANES
        self.full = width // LANES
        self.rest = width % LANES
        self.side = LANES // self.rest if self.rest else 1

    def packed_rows(self, block):
        assert self.rest == 0 or (LANES % self.rest == 0 and block % self.side == 0)
        return self.full * block + (block // self.side if self.rest else 0)

    def packed_shapes(self):
        return [
            ((self.keys, self.width), BF16),
            ((self.width, self.keys), BF16),
            ((self.rows, self.width), BF16),
            ((self.rows, self.width), BF16),
            ((self.rows, self.lanes), BF16),
            ((self.rows, 1), F32),
        ]

    def work_scratch(self, tokens, length):
        return [
            pltpu.VMEM((self.chunks, tokens, LANES), F32),
            pltpu.VMEM((self.chunks, tokens, LANES), F32),
            pltpu.VMEM((tokens, self.width), BF16),
            pltpu.VMEM((self.keys, tokens), BF16),
            pltpu.VMEM((tokens, self.keys), BF16),
            pltpu.VMEM((self.rows, tokens), BF16),
            pltpu.VMEM((self.rows, tokens), F32),
            pltpu.VMEM((2, length, HEADS * length), F32),
            pltpu.VMEM((2, length, HEADS * length), BF16),
            pltpu.VMEM((self.rows, tokens), BF16),
        ]


def prepare(sz, weights, packed):
    proj, bias, out = weights
    wqt, wk, wvt, wgt, wo, bias_col = packed

    def window(block):
        start = block * sz.width
        low = start // LANES * LANES
        high = min(ceil_to(start + sz.width, LANES), 4 * sz.width)
        return proj[:, low:high], start - low, high - low

    def hits(shape, axis, pad, shift):
        place = lax.broadcasted_iota(jnp.int32, shape, axis)
        source = lax.broadcasted_iota(jnp.int32, shape, 1 - axis) - shift
        inner = place % pad
        return (inner < sz.head) & (source == place // pad * sz.head + inner)

    def pick(*spec):
        return jnp.where(hits(*spec), 1.0, 0.0).astype(BF16)

    part, shift, size = window(1)
    wk[...] = nn(part, pick((size, sz.keys), 1, sz.pad_key, shift)).astype(BF16)
    for block, ref, pad in ((0, wqt, sz.pad_key), (2, wvt, sz.pad_head), (3, wgt, sz.pad_head)):
        part, shift, size = window(block)
        ref[...] = nt(pick((HEADS * pad, size), 0, pad, shift), part).astype(BF16)
    spec = (sz.rows, sz.width), 0, sz.pad_head, 0
    wo[...] = jnp.zeros(wo.shape, BF16)
    wo[:, : sz.width] = nn(pick(*spec), out[...]).astype(BF16)
    row = bias[...].reshape(1, sz.width)
    bias_col[...] = jnp.sum(jnp.where(hits(*spec), row, 0.0), axis=1, keepdims=True)


def attend(sz, groups, length, start_of, stride, per_group, gain, packed, work, emit=None):
    wqt, wk, wvt, wgt, wo, bias_col = packed
    xs, ys, normed, queries, keys, values, gates, scores, weights, gated = work
    run = length // per_group
    factor = math.log2(math.e) / sz.head**0.5
    lane = lax.broadcasted_iota(jnp.int32, (1, sz.lanes), 1)
    inside = lane < sz.width
    gain_row = gain[...].reshape(1, sz.width)

    def places(group):
        return [pl.ds(start_of(group, c), run, stride=stride) for c in range(per_group)]

    def tokens_of(group):
        parts = [
            jnp.concatenate([xs[k, place, :] for place in places(group)], axis=0)
            for k in range(sz.chunks)
        ]
        return jnp.concatenate(parts, axis=1)

    for group in range(groups):
        x = tokens_of(group)
        mean = jnp.sum(x, axis=1, keepdims=True) * (1.0 / sz.width)
        centred = jnp.where(inside, x - mean, 0.0)
        spread = jnp.sum(centred * centred, axis=1, keepdims=True) * (1.0 / sz.width)
        value = centred[:, : sz.width] * lax.rsqrt(spread + 1e-05) * gain_row
        normed[group * length : (group + 1) * length] = value.astype(BF16)
    z = normed[...]
    feature = lax.broadcasted_iota(jnp.int32, (sz.rows, 1), 0)
    ones_row = jnp.where(feature % sz.pad_head == sz.head, 1.0, 0.0)
    queries[...] = (nt(wqt[...], z) * factor).astype(BF16)
    keys[...] = nn(z, wk[...]).astype(BF16)
    values[...] = (nt(wvt[...], z) + ones_row).astype(BF16)
    gates[...] = jax.nn.sigmoid(nt(wgt[...], z) + bias_col[...])
    pack = LANES // sz.pad_key
    zeros = jnp.zeros((sz.pad_key, length), BF16)

    def score(group):
        mine = slice(group * length, (group + 1) * length)
        for first in range(0, HEADS, pack):
            blocks = []
            for j in range(pack):
                low = (first + j) * sz.pad_key
                own = queries[low : low + sz.pad_key, mine]
                blocks.append(
                    jnp.concatenate([own if i == j else zeros for i in range(pack)], axis=1)
                )
            lanes = slice(first * sz.pad_key, (first + pack) * sz.pad_key)
            scores[group % 2, :, first * length : (first + pack) * length] = nn(
                keys[mine, lanes], jnp.concatenate(blocks, axis=0)
            )

    def soften(group):
        for head in range(HEADS):
            lanes = slice(head * length, (head + 1) * length)
            s = scores[group % 2, :, lanes]
            top = jnp.max(s, axis=0, keepdims=True)
            weights[group % 2, :, lanes] = jnp.exp2(s - top).astype(BF16)

    def mix(group):
        mine = slice(group * length, (group + 1) * length)
        for head in range(HEADS):
            rows = slice(head * sz.pad_head, (head + 1) * sz.pad_head)
            lanes = slice(head * length, (head + 1) * length)
            mixed = nn(values[rows, mine], weights[group % 2, :, lanes])
            total = mixed[sz.head : sz.head + 1]
            gated[rows, mine] = (mixed * (1.0 / total) * gates[rows, mine]).astype(BF16)

    score(0)
    for group in range(groups):
        if group + 1 < groups:
            score(group + 1)
        soften(group)
        mix(group)
    for group in range(groups):
        mine = slice(group * length, (group + 1) * length)
        y = tokens_of(group) + tn(gated[:, mine], wo[...])
        if emit is not None:
            emit(group, y)
            continue
        for k in range(sz.chunks):
            part = y[:, k * LANES : (k + 1) * LANES]
            for c, place in enumerate(places(group)):
                ys[k, place, :] = part[c * run : (c + 1) * run]


def pack_tokens(sz, ys, target):
    tokens = ys.shape[1]
    n = target.shape[0]
    block = tokens // n
    for k in range(sz.full):
        part = ys[k].reshape(n, block, LANES)
        target[:, k * block : (k + 1) * block, :] = part.astype(BF16)
    if sz.rest:
        joined = None
        for q in range(sz.side):
            part = ys[sz.full, pl.ds(q, tokens // sz.side, stride=sz.side), :]
            part = pltpu.roll(part, q * sz.rest, 1) if q else part
            joined = part if joined is None else joined + part
        part = joined.reshape(n, block // sz.side, LANES)
        target[:, sz.full * block :, :] = part.astype(BF16)


def unpack_tokens(sz, source, xs):
    tokens = xs.shape[1]
    n = source.shape[0]
    block = tokens // n
    for k in range(sz.full):
        part = source[:, k * block : (k + 1) * block, :]
        xs[k] = part.astype(F32).reshape(tokens, LANES)
    if sz.rest:
        joined = source[:, sz.full * block :, :].astype(F32).reshape(tokens // sz.side, LANES)
        inside = lax.broadcasted_iota(jnp.int32, (1, LANES), 1) < sz.rest
        for q in range(sz.side):
            part = pltpu.roll(joined, LANES - q * sz.rest, 1) if q else joined
            place = pl.ds(q, tokens // sz.side, stride=sz.side)
            xs[sz.full, place, :] = jnp.where(inside, part, 0.0)


def turn_tokens(sz, n, rows, source, xs, ys):
    cols, width, length = source.shape
    for c in range(cols):
        turned = source[c].astype(F32).T
        for k in range(sz.chunks):
            part = turned[:, k * LANES : min((k + 1) * LANES, width)]
            if part.shape[1] < LANES:
                pad = jnp.zeros((length, LANES - part.shape[1]), F32)
                part = jnp.concatenate([part, pad], axis=1)
            xs[k, c * length : (c + 1) * length] = part
    for k in range(sz.chunks):
        for c in range(cols):
            for r in range(rows):
                part = xs[k, pl.ds(c * length + r, n, stride=rows), :]
                ys[k, pl.ds(r * cols + c, n, stride=rows * cols), :] = part


def row_kernel(sz, n, rows, cols, *refs):
    x_ref, gain, *own_weights = refs[:5]
    next_weights = refs[5:8]
    result, *next_packed = refs[8:15]
    sent, got, back, *rest = refs[15:]
    packed, rest = rest[:6], rest[6:]
    work = rest[:10]
    send_a, recv_a, send_b, recv_b, local_sem = rest[10:]
    me = lax.axis_index("row")
    block = rows * cols

    barrier = pltpu.get_barrier_semaphore()

    def greet(step, carry):
        peer = lax.rem(me + step, n)
        pl.semaphore_signal(barrier, inc=1, device_id={"row": peer}, device_id_type=MESH)
        return carry

    lax.fori_loop(1, n, greet, 0)
    turn_tokens(sz, n, rows, x_ref, work[0], work[1])
    pack_tokens(sz, work[1], sent)
    pl.semaphore_wait(barrier, n - 1)

    def exchange(source, target, send, recv, body):
        def copy(peer, slot):
            return pltpu.make_async_remote_copy(
                src_ref=source.at[peer],
                dst_ref=target.at[slot],
                send_sem=send.at[peer],
                recv_sem=recv.at[slot],
                device_id={"row": peer},
                device_id_type=MESH,
            )

        def start(step, carry):
            copy(lax.rem(me + step, n), me).start()
            return carry

        lax.fori_loop(1, n, start, 0)
        own = pltpu.make_async_copy(source.at[me], target.at[me], local_sem)
        own.start()
        body()
        own.wait()

        def finish(step, carry):
            peer = lax.rem(me + step, n)
            copy(peer, me).wait_send()
            copy(peer, peer).wait_recv()
            return carry

        lax.fori_loop(1, n, finish, 0)

    exchange(
        sent,
        got,
        send_a,
        recv_a,
        lambda: prepare(sz, own_weights, packed),
    )
    unpack_tokens(sz, got, work[0])
    attend(
        sz, rows, n * cols, lambda g, c: g * cols + c, block, cols, gain, packed, work
    )
    pack_tokens(sz, work[1], back)
    exchange(
        back,
        result,
        send_b,
        recv_b,
        lambda: prepare(sz, next_weights, next_packed),
    )


def col_kernel(sz, cols, x_ref, gain, *refs):
    packed, result, work = refs[:6], refs[6], refs[7:]
    unpack_tokens(sz, x_ref, work[0])
    length = work[0].shape[1] // cols

    def emit(group, y):
        result[group] = y[:, : sz.width].T.astype(BF16)

    attend(sz, cols, length, lambda g, c: g, cols, 1, gain, packed, work, emit)


def swap_columns(sz, done, block, rows, cols):
    n = done.shape[0]
    parts = [done[:, k * block : (k + 1) * block] for k in range(sz.full)]
    if sz.rest:
        parts.append(done[:, sz.full * block :].reshape(n, block, sz.rest))
    whole = jnp.concatenate(parts, -1).reshape(rows, cols, sz.width)
    whole = lax.all_to_all(whole, "col", split_axis=1, concat_axis=0, tiled=True)
    whole = whole.reshape(n, block, sz.width)
    parts = [whole[..., k * LANES : (k + 1) * LANES] for k in range(sz.full)]
    if sz.rest:
        parts.append(whole[..., sz.full * LANES :].reshape(n, block // sz.side, LANES))
    return jnp.concatenate(parts, 1)


VMEM = pl.BlockSpec(memory_space=pltpu.VMEM)


def per_device(
    pair_map, row_gain, row_proj, row_gate_bias, row_out, col_gain, col_proj, col_gate_bias, col_out
):
    local_rows, local_cols, width = pair_map.shape
    n = lax.axis_size("row")
    sz = Sizes(width)
    rows = local_rows // n
    tokens = local_rows * local_cols
    block = rows * local_cols
    shape = (n, sz.packed_rows(block), LANES)
    turned = jnp.transpose(pair_map, (1, 2, 0))
    done, *packed = pl.pallas_call(
        functools.partial(row_kernel, sz, n, rows, local_cols),
        out_shape=[jax.ShapeDtypeStruct(shape, BF16)]
        + [jax.ShapeDtypeStruct(*spec) for spec in sz.packed_shapes()],
        in_specs=[VMEM] * 8,
        out_specs=[VMEM] * 7,
        scratch_shapes=[pltpu.VMEM(shape, BF16)] * 3
        + [pltpu.VMEM(*spec) for spec in sz.packed_shapes()]
        + sz.work_scratch(tokens, n * local_cols)
        + [pltpu.SemaphoreType.DMA((n,))] * 4
        + [pltpu.SemaphoreType.DMA],
        compiler_params=pltpu.CompilerParams(
            collective_id=0, has_side_effects=True, vmem_limit_bytes=VMEM_LIMIT
        ),
        name="row_attention",
    )(turned, row_gain, row_proj, row_gate_bias, row_out, col_proj, col_gate_bias, col_out)
    splits = lax.axis_size("col")
    if splits > 1:
        done = swap_columns(sz, done, block, local_rows, local_cols)
    cols = local_cols // splits
    full = tokens // cols
    updated = pl.pallas_call(
        functools.partial(col_kernel, sz, cols),
        out_shape=jax.ShapeDtypeStruct((cols, width, full), BF16),
        in_specs=[VMEM] * 8,
        out_specs=VMEM,
        scratch_shapes=sz.work_scratch(tokens, full),
        compiler_params=pltpu.CompilerParams(vmem_limit_bytes=VMEM_LIMIT),
        name="col_attention",
    )(done, col_gain, *packed)
    updated = jnp.transpose(updated, (2, 0, 1))
    if splits > 1:
        updated = lax.all_to_all(updated, "col", split_axis=0, concat_axis=1, tiled=True)
    return updated


def solution(mesh):
    return jax.shard_map(
        per_device,
        mesh=mesh,
        in_specs=(P(("groups", "col"), "row", None), P(), P(), P(), P(), P(), P(), P(), P()),
        out_specs=P(("groups", "col"), "row", None),
        check_vma=False,
    )
```

```python
import functools
import math

import jax
import jax.numpy as jnp
from jax import lax
from jax.experimental import pallas as pl
from jax.experimental.pallas import tpu as pltpu
from jax.sharding import PartitionSpec as P

HEADS = 8
LANES = 128
FOLD = 4
VMEM_LIMIT = 32 * 2**20
F32 = jnp.float32
BF16 = jnp.bfloat16
MESH = pl.DeviceIdType.MESH


def ceil_to(value, step):
    return -(-value // step) * step


def nt(a, b):
    return lax.dot_general(a, b, (((1,), (1,)), ((), ())), preferred_element_type=F32)


def tn(a, b):
    return lax.dot_general(a, b, (((0,), (0,)), ((), ())), preferred_element_type=F32)


def nn(a, b):
    return jnp.dot(a, b, preferred_element_type=F32)


class Sizes:
    def __init__(self, width):
        self.width = width
        self.head = width // HEADS
        self.pad_head = ceil_to(self.head + 1, 16)
        self.pad_key = LANES // (LANES // self.head)
        while LANES % self.pad_key:
            self.pad_key += 1
        self.rows = HEADS * self.pad_head
        self.keys = HEADS * self.pad_key
        self.lanes = ceil_to(width, LANES)
        self.chunks = self.lanes // LANES
        self.full = width // LANES
        self.rest = width % LANES
        self.side = LANES // self.rest if self.rest else 1

    def packed_rows(self, block):
        assert self.rest == 0 or (LANES % self.rest == 0 and block % self.side == 0)
        return self.full * block + (block // self.side if self.rest else 0)

    def packed_shapes(self):
        return [
            ((self.keys, self.width), BF16),
            ((self.width, self.keys), BF16),
            ((self.rows, self.width), BF16),
            ((self.rows, self.width), BF16),
            ((self.rows, self.lanes), BF16),
            ((self.rows, 1), F32),
        ]

    def work_scratch(self, tokens, length):
        return [
            pltpu.VMEM((self.chunks, tokens, LANES), F32),
            pltpu.VMEM((self.chunks, tokens, LANES), F32),
            pltpu.VMEM((tokens, self.width), BF16),
            pltpu.VMEM((self.keys, tokens), BF16),
            pltpu.VMEM((tokens, self.keys), BF16),
            pltpu.VMEM((self.rows, tokens), BF16),
            pltpu.VMEM((self.rows, tokens), F32),
            pltpu.VMEM((2, length, HEADS * length), F32),
            pltpu.VMEM((2, length, HEADS * length), BF16),
            pltpu.VMEM((self.rows, tokens), BF16),
        ]


def prepare(sz, weights, packed):
    proj, bias, out = weights
    wqt, wk, wvt, wgt, wo, bias_col = packed

    def window(block):
        start = block * sz.width
        low = start // LANES * LANES
        high = min(ceil_to(start + sz.width, LANES), 4 * sz.width)
        return proj[:, low:high], start - low, high - low

    def hits(shape, axis, pad, shift):
        place = lax.broadcasted_iota(jnp.int32, shape, axis)
        source = lax.broadcasted_iota(jnp.int32, shape, 1 - axis) - shift
        inner = place % pad
        return (inner < sz.head) & (source == place // pad * sz.head + inner)

    def pick(*spec):
        return jnp.where(hits(*spec), 1.0, 0.0).astype(BF16)

    part, shift, size = window(1)
    wk[...] = nn(part, pick((size, sz.keys), 1, sz.pad_key, shift)).astype(BF16)
    for block, ref, pad in ((0, wqt, sz.pad_key), (2, wvt, sz.pad_head), (3, wgt, sz.pad_head)):
        part, shift, size = window(block)
        ref[...] = nt(pick((HEADS * pad, size), 0, pad, shift), part).astype(BF16)
    spec = (sz.rows, sz.width), 0, sz.pad_head, 0
    wo[...] = jnp.zeros(wo.shape, BF16)
    wo[:, : sz.width] = nn(pick(*spec), out[...]).astype(BF16)
    row = bias[...].reshape(1, sz.width)
    bias_col[...] = jnp.sum(jnp.where(hits(*spec), row, 0.0), axis=1, keepdims=True)


def attend(sz, groups, length, start_of, stride, per_group, gain, packed, work, emit=None):
    wqt, wk, wvt, wgt, wo, bias_col = packed
    xs, ys, normed, queries, keys, values, gates, scores, weights, gated = work
    run = length // per_group
    factor = math.log2(math.e) / sz.head**0.5
    lane = lax.broadcasted_iota(jnp.int32, (1, sz.lanes), 1)
    inside = lane < sz.width
    gain_row = gain[...].reshape(1, sz.width)

    def places(group):
        return [pl.ds(start_of(group, c), run, stride=stride) for c in range(per_group)]

    def tokens_of(group):
        parts = [
            jnp.concatenate([xs[k, place, :] for place in places(group)], axis=0)
            for k in range(sz.chunks)
        ]
        return jnp.concatenate(parts, axis=1)

    for group in range(groups):
        x = tokens_of(group)
        mean = jnp.sum(x, axis=1, keepdims=True) * (1.0 / sz.width)
        centred = jnp.where(inside, x - mean, 0.0)
        spread = jnp.sum(centred * centred, axis=1, keepdims=True) * (1.0 / sz.width)
        value = centred[:, : sz.width] * lax.rsqrt(spread + 1e-05) * gain_row
        normed[group * length : (group + 1) * length] = value.astype(BF16)
    z = normed[...]
    feature = lax.broadcasted_iota(jnp.int32, (sz.rows, 1), 0)
    ones_row = jnp.where(feature % sz.pad_head == sz.head, 1.0, 0.0)
    queries[...] = (nt(wqt[...], z) * factor).astype(BF16)
    keys[...] = nn(z, wk[...]).astype(BF16)
    values[...] = (nt(wvt[...], z) + ones_row).astype(BF16)
    gates[...] = jax.nn.sigmoid(nt(wgt[...], z) + bias_col[...])
    pack = LANES // sz.pad_key
    zeros = jnp.zeros((sz.pad_key, length), BF16)

    def score(group):
        mine = slice(group * length, (group + 1) * length)
        for first in range(0, HEADS, pack):
            blocks = []
            for j in range(pack):
                low = (first + j) * sz.pad_key
                own = queries[low : low + sz.pad_key, mine]
                blocks.append(
                    jnp.concatenate([own if i == j else zeros for i in range(pack)], axis=1)
                )
            lanes = slice(first * sz.pad_key, (first + pack) * sz.pad_key)
            scores[group % 2, :, first * length : (first + pack) * length] = nn(
                keys[mine, lanes], jnp.concatenate(blocks, axis=0)
            )

    def soften(group):
        for head in range(HEADS):
            lanes = slice(head * length, (head + 1) * length)
            s = scores[group % 2, :, lanes]
            top = jnp.max(s, axis=0, keepdims=True)
            weights[group % 2, :, lanes] = jnp.exp2(s - top).astype(BF16)

    def mix(group):
        mine = slice(group * length, (group + 1) * length)
        for head in range(HEADS):
            rows = slice(head * sz.pad_head, (head + 1) * sz.pad_head)
            lanes = slice(head * length, (head + 1) * length)
            mixed = nn(values[rows, mine], weights[group % 2, :, lanes])
            total = mixed[sz.head : sz.head + 1]
            gated[rows, mine] = (mixed * (1.0 / total) * gates[rows, mine]).astype(BF16)

    score(0)
    for group in range(groups):
        if group + 1 < groups:
            score(group + 1)
        soften(group)
        mix(group)
    for group in range(groups):
        mine = slice(group * length, (group + 1) * length)
        y = tokens_of(group) + tn(gated[:, mine], wo[...])
        if emit is not None:
            emit(group, y)
            continue
        for k in range(sz.chunks):
            part = y[:, k * LANES : (k + 1) * LANES]
            for c, place in enumerate(places(group)):
                ys[k, place, :] = part[c * run : (c + 1) * run]


def pack_tokens(sz, ys, target):
    tokens = ys.shape[1]
    n = target.shape[0]
    block = tokens // n
    tail = target.shape[2:]
    fold = math.prod(tail) // LANES
    for k in range(sz.full):
        part = ys[k].reshape((n, block // fold) + tail)
        target[:, k * block // fold : (k + 1) * block // fold] = part.astype(BF16)
    if sz.rest:
        joined = None
        for q in range(sz.side):
            part = ys[sz.full, pl.ds(q, tokens // sz.side, stride=sz.side), :]
            part = pltpu.roll(part, q * sz.rest, 1) if q else part
            joined = part if joined is None else joined + part
        part = joined.reshape((n, block // sz.side // fold) + tail)
        target[:, sz.full * block // fold :] = part.astype(BF16)


def unpack_tokens(sz, source, xs):
    tokens = xs.shape[1]
    n = source.shape[0]
    block = tokens // n
    fold = math.prod(source.shape[2:]) // LANES
    for k in range(sz.full):
        part = source[:, k * block // fold : (k + 1) * block // fold]
        xs[k] = part.astype(F32).reshape(tokens, LANES)
    if sz.rest:
        joined = source[:, sz.full * block // fold :].astype(F32)
        joined = joined.reshape(tokens // sz.side, LANES)
        inside = lax.broadcasted_iota(jnp.int32, (1, LANES), 1) < sz.rest
        for q in range(sz.side):
            part = pltpu.roll(joined, LANES - q * sz.rest, 1) if q else joined
            place = pl.ds(q, tokens // sz.side, stride=sz.side)
            xs[sz.full, place, :] = jnp.where(inside, part, 0.0)


def turn_tokens(sz, n, rows, source, xs, ys):
    cols, width, length = source.shape
    for c in range(cols):
        turned = source[c].astype(F32).T
        for k in range(sz.chunks):
            part = turned[:, k * LANES : min((k + 1) * LANES, width)]
            if part.shape[1] < LANES:
                pad = jnp.zeros((length, LANES - part.shape[1]), F32)
                part = jnp.concatenate([part, pad], axis=1)
            xs[k, c * length : (c + 1) * length] = part
    for k in range(sz.chunks):
        for c in range(cols):
            for r in range(rows):
                part = xs[k, pl.ds(c * length + r, n, stride=rows), :]
                ys[k, pl.ds(r * cols + c, n, stride=rows * cols), :] = part


def row_kernel(sz, n, rows, cols, *refs):
    x_ref, gain, *own_weights = refs[:5]
    next_weights = refs[5:8]
    result, *next_packed = refs[8:15]
    sent, got, back, *rest = refs[15:]
    packed, rest = rest[:6], rest[6:]
    work = rest[:10]
    send_a, recv_a, send_b, recv_b, local_sem = rest[10:]
    me = lax.axis_index("row")
    block = rows * cols

    barrier = pltpu.get_barrier_semaphore()

    def greet(step, carry):
        peer = lax.rem(me + step, n)
        pl.semaphore_signal(barrier, inc=1, device_id={"row": peer}, device_id_type=MESH)
        return carry

    lax.fori_loop(1, n, greet, 0)
    turn_tokens(sz, n, rows, x_ref, work[0], work[1])
    pack_tokens(sz, work[1], sent)
    pl.semaphore_wait(barrier, n - 1)

    def exchange(source, target, send, recv, body):
        def copy(peer, slot):
            return pltpu.make_async_remote_copy(
                src_ref=source.at[peer],
                dst_ref=target.at[slot],
                send_sem=send.at[peer],
                recv_sem=recv.at[slot],
                device_id={"row": peer},
                device_id_type=MESH,
            )

        def start(step, carry):
            copy(lax.rem(me + step, n), me).start()
            return carry

        lax.fori_loop(1, n, start, 0)
        own = pltpu.make_async_copy(source.at[me], target.at[me], local_sem)
        own.start()
        body()
        own.wait()

        def finish(step, carry):
            peer = lax.rem(me + step, n)
            copy(peer, me).wait_send()
            copy(peer, peer).wait_recv()
            return carry

        lax.fori_loop(1, n, finish, 0)

    exchange(
        sent,
        got,
        send_a,
        recv_a,
        lambda: prepare(sz, own_weights, packed),
    )
    unpack_tokens(sz, got, work[0])
    attend(
        sz, rows, n * cols, lambda g, c: g * cols + c, block, cols, gain, packed, work
    )
    pack_tokens(sz, work[1], back)
    exchange(
        back,
        result,
        send_b,
        recv_b,
        lambda: prepare(sz, next_weights, next_packed),
    )


def col_kernel(sz, cols, x_ref, gain, *refs):
    packed, result, work = refs[:6], refs[6], refs[7:]
    unpack_tokens(sz, x_ref, work[0])
    length = work[0].shape[1] // cols

    def emit(group, y):
        result[group] = y[:, : sz.width].T.astype(BF16)

    attend(sz, cols, length, lambda g, c: g, cols, 1, gain, packed, work, emit)


def axial_kernel(sz, n, rows, cols, *refs):
    outer, result, refs = refs[:9], refs[9], refs[10:]
    local, refs = refs[:9], refs[9:]
    sent, got, back, home, *refs = refs
    packed_row, packed_col, refs = refs[:6], refs[6:12], refs[12:]
    work = refs[:10]
    load_sem, send_a, recv_a, send_b, recv_b, own_sem = refs[10:]
    x_ref, row_gain, *row_weights = local[:5]
    col_gain, *col_weights = local[5:]
    me = lax.axis_index("row")
    block = rows * cols
    length = n * cols

    def partners(body):
        def step(i, carry):
            body(lax.rem(me + i, n))
            return carry

        lax.fori_loop(1, n, step, 0)

    barrier = pltpu.get_barrier_semaphore()

    def greet(peer):
        pl.semaphore_signal(barrier, inc=1, device_id={"row": peer}, device_id_type=MESH)

    partners(greet)
    loads = [
        pltpu.make_async_copy(source, target, load_sem.at[i])
        for i, (source, target) in enumerate(zip(outer, local))
    ]
    for load in loads:
        load.start()

    def exchange(source, target, send, recv, own):
        def copy(peer, slot):
            return pltpu.make_async_remote_copy(
                src_ref=source.at[peer],
                dst_ref=target.at[slot],
                send_sem=send.at[peer],
                recv_sem=recv.at[slot],
                device_id={"row": peer},
                device_id_type=MESH,
            )

        mine = pltpu.make_async_copy(source.at[me], target.at[me], own)

        def start():
            partners(lambda peer: copy(peer, me).start())
            mine.start()

        def arrive():
            mine.wait()
            partners(lambda peer: copy(peer, peer).wait_recv())

        def leave():
            partners(lambda peer: copy(peer, me).wait_send())

        return start, arrive, leave

    start_a, arrive_a, leave_a = exchange(sent, got, send_a, recv_a, own_sem.at[0])
    start_b, arrive_b, leave_b = exchange(back, home, send_b, recv_b, own_sem.at[1])
    loads[0].wait()
    turn_tokens(sz, n, rows, x_ref, work[0], work[1])
    pack_tokens(sz, work[1], sent)
    pl.semaphore_wait(barrier, n - 1)
    start_a()
    for load in loads[1:]:
        load.wait()
    prepare(sz, row_weights, packed_row)
    prepare(sz, col_weights, packed_col)
    arrive_a()
    unpack_tokens(sz, got, work[0])
    attend(
        sz, rows, length, lambda g, c: g * cols + c, block, cols, row_gain, packed_row, work
    )
    pack_tokens(sz, work[1], back)
    start_b()
    leave_a()
    arrive_b()
    unpack_tokens(sz, home, work[0])

    def emit(group, y):
        result[group] = y[:, : sz.width].T.astype(BF16)

    attend(sz, cols, n * rows, lambda g, c: g, cols, 1, col_gain, packed_col, work, emit)
    leave_b()


def swap_columns(sz, done, block, rows, cols):
    n = done.shape[0]
    parts = [done[:, k * block : (k + 1) * block] for k in range(sz.full)]
    if sz.rest:
        parts.append(done[:, sz.full * block :].reshape(n, block, sz.rest))
    whole = jnp.concatenate(parts, -1).reshape(rows, cols, sz.width)
    whole = lax.all_to_all(whole, "col", split_axis=1, concat_axis=0, tiled=True)
    whole = whole.reshape(n, block, sz.width)
    parts = [whole[..., k * LANES : (k + 1) * LANES] for k in range(sz.full)]
    if sz.rest:
        parts.append(whole[..., sz.full * LANES :].reshape(n, block // sz.side, LANES))
    return jnp.concatenate(parts, 1)


VMEM = pl.BlockSpec(memory_space=pltpu.VMEM)


def per_device(
    pair_map, row_gain, row_proj, row_gate_bias, row_out, col_gain, col_proj, col_gate_bias, col_out
):
    local_rows, local_cols, width = pair_map.shape
    n = lax.axis_size("row")
    sz = Sizes(width)
    rows = local_rows // n
    tokens = local_rows * local_cols
    block = rows * local_cols
    shape = (n, sz.packed_rows(block), LANES)
    turned = jnp.transpose(pair_map, (1, 2, 0))
    splits = lax.axis_size("col")
    if splits == 1 and shape[1] % FOLD == 0 and block % (FOLD * sz.side) == 0:
        folded = (n, shape[1] // FOLD, FOLD, LANES)
        operands = (turned, row_gain, row_proj, row_gate_bias, row_out)
        operands += (col_gain, col_proj, col_gate_bias, col_out)
        operands = [pltpu.with_memory_space_constraint(a, pltpu.HBM) for a in operands]
        updated = pl.pallas_call(
            functools.partial(axial_kernel, sz, n, rows, local_cols),
            out_shape=jax.ShapeDtypeStruct(turned.shape, BF16),
            in_specs=[pl.BlockSpec(memory_space=pltpu.HBM)] * len(operands),
            out_specs=VMEM,
            scratch_shapes=[pltpu.VMEM(a.shape, a.dtype) for a in operands]
            + [pltpu.VMEM(folded, BF16)] * 4
            + [pltpu.VMEM(*spec) for spec in sz.packed_shapes()] * 2
            + sz.work_scratch(tokens, max(n * local_cols, local_rows))
            + [pltpu.SemaphoreType.DMA((len(operands),))]
            + [pltpu.SemaphoreType.DMA((n,))] * 4
            + [pltpu.SemaphoreType.DMA((2,))],
            compiler_params=pltpu.CompilerParams(
                collective_id=0, has_side_effects=True, vmem_limit_bytes=VMEM_LIMIT
            ),
            name="axial_attention",
        )(*operands)
        return jnp.transpose(updated, (2, 0, 1))
    done, *packed = pl.pallas_call(
        functools.partial(row_kernel, sz, n, rows, local_cols),
        out_shape=[jax.ShapeDtypeStruct(shape, BF16)]
        + [jax.ShapeDtypeStruct(*spec) for spec in sz.packed_shapes()],
        in_specs=[VMEM] * 8,
        out_specs=[VMEM] * 7,
        scratch_shapes=[pltpu.VMEM(shape, BF16)] * 3
        + [pltpu.VMEM(*spec) for spec in sz.packed_shapes()]
        + sz.work_scratch(tokens, n * local_cols)
        + [pltpu.SemaphoreType.DMA((n,))] * 4
        + [pltpu.SemaphoreType.DMA],
        compiler_params=pltpu.CompilerParams(collective_id=0, has_side_effects=True),
        name="row_attention",
    )(turned, row_gain, row_proj, row_gate_bias, row_out, col_proj, col_gate_bias, col_out)
    if splits > 1:
        done = swap_columns(sz, done, block, local_rows, local_cols)
    cols = local_cols // splits
    full = tokens // cols
    updated = pl.pallas_call(
        functools.partial(col_kernel, sz, cols),
        out_shape=jax.ShapeDtypeStruct((cols, width, full), BF16),
        in_specs=[VMEM] * 8,
        out_specs=VMEM,
        scratch_shapes=sz.work_scratch(tokens, full),
        name="col_attention",
    )(done, col_gain, *packed)
    updated = jnp.transpose(updated, (2, 0, 1))
    if splits > 1:
        updated = lax.all_to_all(updated, "col", split_axis=0, concat_axis=1, tiled=True)
    return updated


def solution(mesh):
    return jax.shard_map(
        per_device,
        mesh=mesh,
        in_specs=(P(("groups", "col"), "row", None), P(), P(), P(), P(), P(), P(), P(), P()),
        out_specs=P(("groups", "col"), "row", None),
        check_vma=False,
    )
```

```python
import functools
import math

import jax
import jax.numpy as jnp
from jax import lax
from jax.experimental import pallas as pl
from jax.experimental.pallas import tpu as pltpu
from jax.sharding import PartitionSpec as P

HEADS = 8
LANES = 128
FOLD = 4
VMEM_LIMIT = 32 * 2**20
F32 = jnp.float32
BF16 = jnp.bfloat16
MESH = pl.DeviceIdType.MESH


def ceil_to(value, step):
    return -(-value // step) * step


def nt(a, b):
    return lax.dot_general(a, b, (((1,), (1,)), ((), ())), preferred_element_type=F32)


def tn(a, b):
    return lax.dot_general(a, b, (((0,), (0,)), ((), ())), preferred_element_type=F32)


def nn(a, b):
    return jnp.dot(a, b, preferred_element_type=F32)


class Sizes:
    def __init__(self, width):
        self.width = width
        self.head = width // HEADS
        self.pad_head = ceil_to(self.head + 1, 16)
        self.pad_key = LANES // (LANES // self.head)
        while LANES % self.pad_key:
            self.pad_key += 1
        self.rows = HEADS * self.pad_head
        self.keys = HEADS * self.pad_key
        self.lanes = ceil_to(width, LANES)
        self.chunks = self.lanes // LANES
        self.full = width // LANES
        self.rest = width % LANES
        self.side = LANES // self.rest if self.rest else 1

    def packed_rows(self, block):
        assert self.rest == 0 or (LANES % self.rest == 0 and block % self.side == 0)
        return self.full * block + (block // self.side if self.rest else 0)

    def packed_shapes(self):
        return [
            ((self.keys, self.width), BF16),
            ((self.width, self.keys), BF16),
            ((self.rows, self.width), BF16),
            ((self.rows, self.width), BF16),
            ((self.rows, self.lanes), BF16),
            ((self.rows, 1), F32),
        ]

    def work_scratch(self, tokens, length):
        return [
            pltpu.VMEM((self.chunks, tokens, LANES), F32),
            pltpu.VMEM((self.chunks, tokens, LANES), F32),
            pltpu.VMEM((tokens, self.width), BF16),
            pltpu.VMEM((self.keys, tokens), BF16),
            pltpu.VMEM((tokens, self.keys), BF16),
            pltpu.VMEM((self.rows, tokens), BF16),
            pltpu.VMEM((self.rows, tokens), F32),
            pltpu.VMEM((2, length, HEADS * length), F32),
            pltpu.VMEM((2, length, HEADS * length), BF16),
            pltpu.VMEM((self.rows, tokens), BF16),
        ]


def prepare(sz, weights, packed):
    proj, bias, out = weights
    wqt, wk, wvt, wgt, wo, bias_col = packed

    def window(block):
        start = block * sz.width
        low = start // LANES * LANES
        high = min(ceil_to(start + sz.width, LANES), 4 * sz.width)
        return proj[:, low:high], start - low, high - low

    def hits(shape, axis, pad, shift):
        place = lax.broadcasted_iota(jnp.int32, shape, axis)
        source = lax.broadcasted_iota(jnp.int32, shape, 1 - axis) - shift
        inner = place % pad
        return (inner < sz.head) & (source == place // pad * sz.head + inner)

    def pick(*spec):
        return jnp.where(hits(*spec), 1.0, 0.0).astype(BF16)

    part, shift, size = window(1)
    wk[...] = nn(part, pick((size, sz.keys), 1, sz.pad_key, shift)).astype(BF16)
    for block, ref, pad in ((0, wqt, sz.pad_key), (2, wvt, sz.pad_head), (3, wgt, sz.pad_head)):
        part, shift, size = window(block)
        ref[...] = nt(pick((HEADS * pad, size), 0, pad, shift), part).astype(BF16)
    spec = (sz.rows, sz.width), 0, sz.pad_head, 0
    wo[...] = jnp.zeros(wo.shape, BF16)
    wo[:, : sz.width] = nn(pick(*spec), out[...]).astype(BF16)
    row = bias[...].reshape(1, sz.width)
    bias_col[...] = jnp.sum(jnp.where(hits(*spec), row, 0.0), axis=1, keepdims=True)


def mix_lines(sz, groups, length, work):
    queries, keys, values, gates, scores, weights, gated = work[3:]
    pack = LANES // sz.pad_key
    zeros = jnp.zeros((sz.pad_key, length), BF16)

    def score(group):
        mine = slice(group * length, (group + 1) * length)
        for first in range(0, HEADS, pack):
            blocks = []
            for j in range(pack):
                low = (first + j) * sz.pad_key
                own = queries[low : low + sz.pad_key, mine]
                blocks.append(
                    jnp.concatenate([own if i == j else zeros for i in range(pack)], axis=1)
                )
            lanes = slice(first * sz.pad_key, (first + pack) * sz.pad_key)
            scores[group % 2, :, first * length : (first + pack) * length] = nn(
                keys[mine, lanes], jnp.concatenate(blocks, axis=0)
            )

    def soften(group):
        for head in range(HEADS):
            lanes = slice(head * length, (head + 1) * length)
            s = scores[group % 2, :, lanes]
            top = jnp.max(s, axis=0, keepdims=True)
            weights[group % 2, :, lanes] = jnp.exp2(s - top).astype(BF16)

    def mix(group):
        mine = slice(group * length, (group + 1) * length)
        for head in range(HEADS):
            rows = slice(head * sz.pad_head, (head + 1) * sz.pad_head)
            lanes = slice(head * length, (head + 1) * length)
            mixed = nn(values[rows, mine], weights[group % 2, :, lanes])
            total = mixed[sz.head : sz.head + 1]
            gated[rows, mine] = (mixed * (1.0 / total) * gates[rows, mine]).astype(BF16)

    score(0)
    for group in range(groups):
        if group + 1 < groups:
            score(group + 1)
        soften(group)
        mix(group)


def attend(sz, groups, length, start_of, stride, per_group, gain, packed, work, emit=None):
    wqt, wk, wvt, wgt, wo, bias_col = packed
    xs, ys, normed, queries, keys, values, gates = work[:7]
    gated = work[9]
    run = length // per_group
    factor = math.log2(math.e) / sz.head**0.5
    lane = lax.broadcasted_iota(jnp.int32, (1, sz.lanes), 1)
    inside = lane < sz.width
    gain_row = gain[...].reshape(1, sz.width)

    def places(group):
        return [pl.ds(start_of(group, c), run, stride=stride) for c in range(per_group)]

    def tokens_of(group):
        parts = [
            jnp.concatenate([xs[k, place, :] for place in places(group)], axis=0)
            for k in range(sz.chunks)
        ]
        return jnp.concatenate(parts, axis=1)

    for group in range(groups):
        x = tokens_of(group)
        mean = jnp.sum(x, axis=1, keepdims=True) * (1.0 / sz.width)
        centred = jnp.where(inside, x - mean, 0.0)
        spread = jnp.sum(centred * centred, axis=1, keepdims=True) * (1.0 / sz.width)
        value = centred[:, : sz.width] * lax.rsqrt(spread + 1e-05) * gain_row
        normed[group * length : (group + 1) * length] = value.astype(BF16)
    z = normed[...]
    feature = lax.broadcasted_iota(jnp.int32, (sz.rows, 1), 0)
    ones_row = jnp.where(feature % sz.pad_head == sz.head, 1.0, 0.0)
    queries[...] = (nt(wqt[...], z) * factor).astype(BF16)
    keys[...] = nn(z, wk[...]).astype(BF16)
    values[...] = (nt(wvt[...], z) + ones_row).astype(BF16)
    gates[...] = jax.nn.sigmoid(nt(wgt[...], z) + bias_col[...])
    mix_lines(sz, groups, length, work)
    for group in range(groups):
        mine = slice(group * length, (group + 1) * length)
        y = tokens_of(group) + tn(gated[:, mine], wo[...])
        if emit is not None:
            emit(group, y)
            continue
        for k in range(sz.chunks):
            part = y[:, k * LANES : (k + 1) * LANES]
            for c, place in enumerate(places(group)):
                ys[k, place, :] = part[c * run : (c + 1) * run]


class Lines:
    def __init__(self, sz, groups, length, start_of, stride, per_group, gain, packed, work):
        self.sz, self.groups, self.length = sz, groups, length
        self.gain, self.packed, self.work = gain, packed, work
        self.half = length // 2
        self.part = groups * self.half
        self.start_of, self.stride, self.per_group = start_of, stride, per_group
        self.run = self.half // per_group

    def order(self, line):
        return (0, 1) if line % 2 == 0 else (1, 0)

    def base(self, part):
        return (1 - part) * self.part

    def places(self, line, part):
        return [
            pl.ds(self.base(part) + self.start_of(line, c), self.run, stride=self.stride)
            for c in range(self.per_group)
        ]

    def gather(self, spots):
        xs = self.work[0]
        parts = [
            jnp.concatenate([xs[k, place, :] for place in spots], axis=0)
            for k in range(self.sz.chunks)
        ]
        return jnp.concatenate(parts, axis=1)

    def tile(self, index, part):
        lines = (2 * index, 2 * index + 1)
        return lines if part == 0 else lines[::-1]

    def absorb(self, part, source):
        sz, length, half = self.sz, self.length, self.half
        wqt, wk, wvt, wgt, _, bias_col = self.packed
        xs, _, normed, queries, keys, values, gates = self.work[:7]
        unpack_tokens(sz, source, xs, self.base(part), self.part)
        factor = math.log2(math.e) / sz.head**0.5
        inside = lax.broadcasted_iota(jnp.int32, (1, sz.lanes), 1) < sz.width
        gain_row = self.gain[...].reshape(1, sz.width)
        for index in range(self.groups // 2):
            first, second = self.tile(index, part)
            x = self.gather(self.places(first, part) + self.places(second, part))
            mean = jnp.sum(x, axis=1, keepdims=True) * (1.0 / sz.width)
            centred = jnp.where(inside, x - mean, 0.0)
            spread = jnp.sum(centred * centred, axis=1, keepdims=True) * (1.0 / sz.width)
            value = centred[:, : sz.width] * lax.rsqrt(spread + 1e-05) * gain_row
            normed[index * length : (index + 1) * length] = value.astype(BF16)
        z = normed[: self.part]
        made = nn(z, wk[...]).astype(BF16)
        for index in range(self.groups // 2):
            for place, line in enumerate(self.tile(index, part)):
                low = index * length + place * half
                spot = line * length + place * half
                keys[spot : spot + half] = made[low : low + half]
        feature = lax.broadcasted_iota(jnp.int32, (sz.rows, 1), 0)
        ones_row = jnp.where(feature % sz.pad_head == sz.head, 1.0, 0.0)
        self.settle(part, queries, (nt(wqt[...], z) * factor).astype(BF16))
        self.settle(part, values, (nt(wvt[...], z) + ones_row).astype(BF16))
        self.settle(part, gates, jax.nn.sigmoid(nt(wgt[...], z) + bias_col[...]))

    def settle(self, part, ref, value):
        length = self.length
        lane = lax.broadcasted_iota(jnp.int32, (ref.shape[0], length), 1)
        for index in range(self.groups // 2):
            new = value[:, index * length : (index + 1) * length]
            even = slice(2 * index * length, (2 * index + 1) * length)
            odd = slice((2 * index + 1) * length, (2 * index + 2) * length)
            if part == 0:
                ref[:, even] = new
                continue
            old = ref[:, even]
            ref[:, even] = jnp.where(lane < self.half, old, new)
            ref[:, odd] = jnp.where(lane < self.half, new, old)

    def finish(self, emit=None):
        sz, length, run = self.sz, self.length, self.run
        wo = self.packed[4]
        ys, gated = self.work[1], self.work[9]
        mix_lines(sz, self.groups, length, self.work)
        for line in range(self.groups):
            mine = slice(line * length, (line + 1) * length)
            spots = [place for part in self.order(line) for place in self.places(line, part)]
            y = self.gather(spots) + tn(gated[:, mine], wo[...])
            if emit is not None:
                emit(line, y)
                continue
            for k in range(sz.chunks):
                piece = y[:, k * LANES : (k + 1) * LANES]
                for i, place in enumerate(spots):
                    ys[k, place, :] = piece[i * run : (i + 1) * run]


def pack_tokens(sz, ys, target):
    tokens = ys.shape[1]
    n = target.shape[0]
    block = tokens // n
    tail = target.shape[2:]
    fold = math.prod(tail) // LANES
    for k in range(sz.full):
        part = ys[k].reshape((n, block // fold) + tail)
        target[:, k * block // fold : (k + 1) * block // fold] = part.astype(BF16)
    if sz.rest:
        joined = None
        for q in range(sz.side):
            part = ys[sz.full, pl.ds(q, tokens // sz.side, stride=sz.side), :]
            part = pltpu.roll(part, q * sz.rest, 1) if q else part
            joined = part if joined is None else joined + part
        part = joined.reshape((n, block // sz.side // fold) + tail)
        target[:, sz.full * block // fold :] = part.astype(BF16)


def unpack_tokens(sz, source, xs, base=0, tokens=None):
    tokens = tokens or xs.shape[1]
    n = source.shape[0]
    block = tokens // n
    fold = math.prod(source.shape[2:]) // LANES
    for k in range(sz.full):
        part = source[:, k * block // fold : (k + 1) * block // fold]
        xs[k, base : base + tokens] = part.astype(F32).reshape(tokens, LANES)
    if sz.rest:
        joined = source[:, sz.full * block // fold :].astype(F32)
        joined = joined.reshape(tokens // sz.side, LANES)
        inside = lax.broadcasted_iota(jnp.int32, (1, LANES), 1) < sz.rest
        for q in range(sz.side):
            part = pltpu.roll(joined, LANES - q * sz.rest, 1) if q else joined
            place = pl.ds(base + q, tokens // sz.side, stride=sz.side)
            xs[sz.full, place, :] = jnp.where(inside, part, 0.0)


def turn_tokens(sz, n, rows, source, xs, ys):
    cols, width, length = source.shape
    for c in range(cols):
        turned = source[c].astype(F32).T
        for k in range(sz.chunks):
            part = turned[:, k * LANES : min((k + 1) * LANES, width)]
            if part.shape[1] < LANES:
                pad = jnp.zeros((length, LANES - part.shape[1]), F32)
                part = jnp.concatenate([part, pad], axis=1)
            xs[k, c * length : (c + 1) * length] = part
    for k in range(sz.chunks):
        for c in range(cols):
            for r in range(rows):
                part = xs[k, pl.ds(c * length + r, n, stride=rows), :]
                ys[k, pl.ds(r * cols + c, n, stride=rows * cols), :] = part


def row_kernel(sz, n, rows, cols, *refs):
    x_ref, gain, *own_weights = refs[:5]
    next_weights = refs[5:8]
    result, *next_packed = refs[8:15]
    sent, got, back, *rest = refs[15:]
    packed, rest = rest[:6], rest[6:]
    work = rest[:10]
    send_a, recv_a, send_b, recv_b, local_sem = rest[10:]
    me = lax.axis_index("row")
    block = rows * cols

    barrier = pltpu.get_barrier_semaphore()

    def greet(step, carry):
        peer = lax.rem(me + step, n)
        pl.semaphore_signal(barrier, inc=1, device_id={"row": peer}, device_id_type=MESH)
        return carry

    lax.fori_loop(1, n, greet, 0)
    turn_tokens(sz, n, rows, x_ref, work[0], work[1])
    pack_tokens(sz, work[1], sent)
    pl.semaphore_wait(barrier, n - 1)

    def exchange(source, target, send, recv, body):
        def copy(peer, slot):
            return pltpu.make_async_remote_copy(
                src_ref=source.at[peer],
                dst_ref=target.at[slot],
                send_sem=send.at[peer],
                recv_sem=recv.at[slot],
                device_id={"row": peer},
                device_id_type=MESH,
            )

        def start(step, carry):
            copy(lax.rem(me + step, n), me).start()
            return carry

        lax.fori_loop(1, n, start, 0)
        own = pltpu.make_async_copy(source.at[me], target.at[me], local_sem)
        own.start()
        body()
        own.wait()

        def finish(step, carry):
            peer = lax.rem(me + step, n)
            copy(peer, me).wait_send()
            copy(peer, peer).wait_recv()
            return carry

        lax.fori_loop(1, n, finish, 0)

    exchange(
        sent,
        got,
        send_a,
        recv_a,
        lambda: prepare(sz, own_weights, packed),
    )
    unpack_tokens(sz, got, work[0])
    attend(
        sz, rows, n * cols, lambda g, c: g * cols + c, block, cols, gain, packed, work
    )
    pack_tokens(sz, work[1], back)
    exchange(
        back,
        result,
        send_b,
        recv_b,
        lambda: prepare(sz, next_weights, next_packed),
    )


def col_kernel(sz, cols, x_ref, gain, *refs):
    packed, result, work = refs[:6], refs[6], refs[7:]
    unpack_tokens(sz, x_ref, work[0])
    length = work[0].shape[1] // cols

    def emit(group, y):
        result[group] = y[:, : sz.width].T.astype(BF16)

    attend(sz, cols, length, lambda g, c: g, cols, 1, gain, packed, work, emit)


def axial_kernel(sz, n, rows, cols, *refs):
    outer, result, refs = refs[:9], refs[9], refs[10:]
    local, refs = refs[:9], refs[9:]
    sent, got, back, home, *refs = refs
    packed_row, packed_col, refs = refs[:6], refs[6:12], refs[12:]
    work = refs[:10]
    load_sem, send_a, recv_a, send_b, recv_b, own_sem = refs[10:]
    x_ref, row_gain, *row_weights = local[:5]
    col_gain, *col_weights = local[5:]
    me = lax.axis_index("row")
    block = rows * cols
    length = n * cols

    half = n // 2

    def steps(low, high, body):
        def step(i, carry):
            body(i)
            return carry

        lax.fori_loop(low, high, step, 0)

    def partner(i):
        return lax.rem(me + i, n)

    barrier = pltpu.get_barrier_semaphore()

    def greet(i):
        peer = partner(i)
        pl.semaphore_signal(barrier, inc=1, device_id={"row": peer}, device_id_type=MESH)

    steps(1, n, greet)
    loads = [
        pltpu.make_async_copy(source, target, load_sem.at[i])
        for i, (source, target) in enumerate(zip(outer, local))
    ]
    for load in loads:
        load.start()

    class Exchange:
        def __init__(self, source, target, send, recv, own, index):
            self.source, self.target, self.index = source, target, index
            self.send, self.recv = send, recv
            self.own = pltpu.make_async_copy(source.at[index(0)], target.at[0], own)

        def copy(self, i, slot):
            return pltpu.make_async_remote_copy(
                src_ref=self.source.at[self.index(i)],
                dst_ref=self.target.at[slot],
                send_sem=self.send.at[i],
                recv_sem=self.recv.at[slot],
                device_id={"row": partner(i)},
                device_id_type=MESH,
            )

        def start(self):
            steps(1, n, lambda i: self.copy(i, n - i).start())
            self.own.start()

        def arrive(self, part):
            if part == 0:
                steps(1, half + 1, lambda i: self.copy(i, n - i).wait_recv())
                return self.target.at[half:]
            steps(half + 1, n, lambda i: self.copy(i, n - i).wait_recv())
            self.own.wait()
            return self.target.at[:half]

        def leave(self):
            steps(1, n, lambda i: self.copy(i, n - i).wait_send())

    first = Exchange(sent, got, send_a, recv_a, own_sem.at[0], partner)
    second = Exchange(back, home, send_b, recv_b, own_sem.at[1], lambda i: i)
    loads[0].wait()
    turn_tokens(sz, n, rows, x_ref, work[0], work[1])
    pack_tokens(sz, work[1], sent)
    pl.semaphore_wait(barrier, n - 1)
    first.start()
    for load in loads[1:]:
        load.wait()
    prepare(sz, row_weights, packed_row)
    prepare(sz, col_weights, packed_col)
    along_rows = Lines(
        sz, rows, length, lambda g, c: g * cols + c, block, cols, row_gain, packed_row, work
    )
    along_rows.absorb(0, first.arrive(0))
    along_rows.absorb(1, first.arrive(1))
    along_rows.finish()
    pack_tokens(sz, work[1], back)
    second.start()
    first.leave()
    height = n * rows
    along_cols = Lines(
        sz, cols, height, lambda g, c: g, cols, 1, col_gain, packed_col, work
    )
    along_cols.absorb(0, second.arrive(0))
    along_cols.absorb(1, second.arrive(1))

    def emit(line, y):
        shift = me * rows + (height // 2 if line % 2 == 0 else 0)
        turned = pltpu.roll(y[:, : sz.width].T, lax.rem(shift, height), 1)
        result[line] = turned.astype(BF16)

    along_cols.finish(emit)
    second.leave()


def swap_columns(sz, done, block, rows, cols):
    n = done.shape[0]
    parts = [done[:, k * block : (k + 1) * block] for k in range(sz.full)]
    if sz.rest:
        parts.append(done[:, sz.full * block :].reshape(n, block, sz.rest))
    whole = jnp.concatenate(parts, -1).reshape(rows, cols, sz.width)
    whole = lax.all_to_all(whole, "col", split_axis=1, concat_axis=0, tiled=True)
    whole = whole.reshape(n, block, sz.width)
    parts = [whole[..., k * LANES : (k + 1) * LANES] for k in range(sz.full)]
    if sz.rest:
        parts.append(whole[..., sz.full * LANES :].reshape(n, block // sz.side, LANES))
    return jnp.concatenate(parts, 1)


VMEM = pl.BlockSpec(memory_space=pltpu.VMEM)


def per_device(
    pair_map, row_gain, row_proj, row_gate_bias, row_out, col_gain, col_proj, col_gate_bias, col_out
):
    local_rows, local_cols, width = pair_map.shape
    n = lax.axis_size("row")
    sz = Sizes(width)
    rows = local_rows // n
    tokens = local_rows * local_cols
    block = rows * local_cols
    shape = (n, sz.packed_rows(block), LANES)
    turned = jnp.transpose(pair_map, (1, 2, 0))
    splits = lax.axis_size("col")
    folds = shape[1] % FOLD == 0 and block % (FOLD * sz.side) == 0
    even = rows % 2 == 0 and local_cols % 2 == 0 and n % 2 == 0
    if splits == 1 and folds and even and n * local_cols == local_rows == LANES:
        folded = (n, shape[1] // FOLD, FOLD, LANES)
        operands = (turned, row_gain, row_proj, row_gate_bias, row_out)
        operands += (col_gain, col_proj, col_gate_bias, col_out)
        operands = [pltpu.with_memory_space_constraint(a, pltpu.HBM) for a in operands]
        updated = pl.pallas_call(
            functools.partial(axial_kernel, sz, n, rows, local_cols),
            out_shape=jax.ShapeDtypeStruct(turned.shape, BF16),
            in_specs=[pl.BlockSpec(memory_space=pltpu.HBM)] * len(operands),
            out_specs=VMEM,
            scratch_shapes=[pltpu.VMEM(a.shape, a.dtype) for a in operands]
            + [pltpu.VMEM(folded, BF16)] * 4
            + [pltpu.VMEM(*spec) for spec in sz.packed_shapes()] * 2
            + sz.work_scratch(tokens, max(n * local_cols, local_rows))
            + [pltpu.SemaphoreType.DMA((len(operands),))]
            + [pltpu.SemaphoreType.DMA((n,))] * 4
            + [pltpu.SemaphoreType.DMA((2,))],
            compiler_params=pltpu.CompilerParams(
                collective_id=0, has_side_effects=True, vmem_limit_bytes=VMEM_LIMIT
            ),
            name="axial_attention",
        )(*operands)
        return jnp.transpose(updated, (2, 0, 1))
    done, *packed = pl.pallas_call(
        functools.partial(row_kernel, sz, n, rows, local_cols),
        out_shape=[jax.ShapeDtypeStruct(shape, BF16)]
        + [jax.ShapeDtypeStruct(*spec) for spec in sz.packed_shapes()],
        in_specs=[VMEM] * 8,
        out_specs=[VMEM] * 7,
        scratch_shapes=[pltpu.VMEM(shape, BF16)] * 3
        + [pltpu.VMEM(*spec) for spec in sz.packed_shapes()]
        + sz.work_scratch(tokens, n * local_cols)
        + [pltpu.SemaphoreType.DMA((n,))] * 4
        + [pltpu.SemaphoreType.DMA],
        compiler_params=pltpu.CompilerParams(collective_id=0, has_side_effects=True),
        name="row_attention",
    )(turned, row_gain, row_proj, row_gate_bias, row_out, col_proj, col_gate_bias, col_out)
    if splits > 1:
        done = swap_columns(sz, done, block, local_rows, local_cols)
    cols = local_cols // splits
    full = tokens // cols
    updated = pl.pallas_call(
        functools.partial(col_kernel, sz, cols),
        out_shape=jax.ShapeDtypeStruct((cols, width, full), BF16),
        in_specs=[VMEM] * 8,
        out_specs=VMEM,
        scratch_shapes=sz.work_scratch(tokens, full),
        name="col_attention",
    )(done, col_gain, *packed)
    updated = jnp.transpose(updated, (2, 0, 1))
    if splits > 1:
        updated = lax.all_to_all(updated, "col", split_axis=0, concat_axis=1, tiled=True)
    return updated


def solution(mesh):
    return jax.shard_map(
        per_device,
        mesh=mesh,
        in_specs=(P(("groups", "col"), "row", None), P(), P(), P(), P(), P(), P(), P(), P()),
        out_specs=P(("groups", "col"), "row", None),
        check_vma=False,
    )
```

```python
import functools
import math

import jax
import jax.numpy as jnp
from jax import lax
from jax.experimental import pallas as pl
from jax.experimental.pallas import tpu as pltpu
from jax.sharding import PartitionSpec as P

HEADS = 8
LANES = 128
FOLD = 4
VMEM_LIMIT = 32 * 2**20
F32 = jnp.float32
BF16 = jnp.bfloat16
MESH = pl.DeviceIdType.MESH


def ceil_to(value, step):
    return -(-value // step) * step


def nt(a, b):
    return lax.dot_general(a, b, (((1,), (1,)), ((), ())), preferred_element_type=F32)


def tn(a, b):
    return lax.dot_general(a, b, (((0,), (0,)), ((), ())), preferred_element_type=F32)


def nn(a, b):
    return jnp.dot(a, b, preferred_element_type=F32)


class Sizes:
    def __init__(self, width):
        self.width = width
        self.head = width // HEADS
        self.pad_head = ceil_to(self.head + 1, 16)
        self.pad_key = LANES // (LANES // self.head)
        while LANES % self.pad_key:
            self.pad_key += 1
        self.rows = HEADS * self.pad_head
        self.keys = HEADS * self.pad_key
        self.lanes = ceil_to(width, LANES)
        self.chunks = self.lanes // LANES
        self.full = width // LANES
        self.rest = width % LANES
        self.side = LANES // self.rest if self.rest else 1

    def packed_rows(self, block):
        assert self.rest == 0 or (LANES % self.rest == 0 and block % self.side == 0)
        return self.full * block + (block // self.side if self.rest else 0)

    def packed_shapes(self):
        return [
            ((self.keys, self.width), BF16),
            ((self.width, self.keys), BF16),
            ((self.rows, self.width), BF16),
            ((self.rows, self.width), BF16),
            ((self.rows, self.lanes), BF16),
            ((self.rows, 1), F32),
        ]

    def work_scratch(self, tokens, length):
        return [
            pltpu.VMEM((self.chunks, tokens, LANES), F32),
            pltpu.VMEM((self.chunks, tokens, LANES), F32),
            pltpu.VMEM((tokens, self.width), BF16),
            pltpu.VMEM((self.keys, tokens), BF16),
            pltpu.VMEM((tokens, self.keys), BF16),
            pltpu.VMEM((self.rows, tokens), BF16),
            pltpu.VMEM((self.rows, tokens), F32),
            pltpu.VMEM((2, length, HEADS * length), F32),
            pltpu.VMEM((2, length, HEADS * length), BF16),
            pltpu.VMEM((self.rows, tokens), BF16),
        ]


def prepare(sz, weights, packed):
    proj, bias, out = weights
    wqt, wk, wvt, wgt, wo, bias_col = packed

    def window(block):
        start = block * sz.width
        low = start // LANES * LANES
        high = min(ceil_to(start + sz.width, LANES), 4 * sz.width)
        return proj[:, low:high], start - low, high - low

    def hits(shape, axis, pad, shift):
        place = lax.broadcasted_iota(jnp.int32, shape, axis)
        source = lax.broadcasted_iota(jnp.int32, shape, 1 - axis) - shift
        inner = place % pad
        return (inner < sz.head) & (source == place // pad * sz.head + inner)

    def pick(*spec):
        return jnp.where(hits(*spec), 1.0, 0.0).astype(BF16)

    part, shift, size = window(1)
    wk[...] = nn(part, pick((size, sz.keys), 1, sz.pad_key, shift)).astype(BF16)
    for block, ref, pad in ((0, wqt, sz.pad_key), (2, wvt, sz.pad_head), (3, wgt, sz.pad_head)):
        part, shift, size = window(block)
        ref[...] = nt(pick((HEADS * pad, size), 0, pad, shift), part).astype(BF16)
    spec = (sz.rows, sz.width), 0, sz.pad_head, 0
    wo[...] = jnp.zeros(wo.shape, BF16)
    wo[:, : sz.width] = nn(pick(*spec), out[...]).astype(BF16)
    row = bias[...].reshape(1, sz.width)
    bias_col[...] = jnp.sum(jnp.where(hits(*spec), row, 0.0), axis=1, keepdims=True)


def mix_lines(sz, groups, length, work):
    queries, keys, values, gates, scores, weights, gated = work[3:]
    pack = LANES // sz.pad_key
    zeros = jnp.zeros((sz.pad_key, length), BF16)

    def score(group):
        mine = slice(group * length, (group + 1) * length)
        for first in range(0, HEADS, pack):
            blocks = []
            for j in range(pack):
                low = (first + j) * sz.pad_key
                own = queries[low : low + sz.pad_key, mine]
                blocks.append(
                    jnp.concatenate([own if i == j else zeros for i in range(pack)], axis=1)
                )
            lanes = slice(first * sz.pad_key, (first + pack) * sz.pad_key)
            scores[group % 2, :, first * length : (first + pack) * length] = nn(
                keys[mine, lanes], jnp.concatenate(blocks, axis=0)
            )

    def soften(group):
        for head in range(HEADS):
            lanes = slice(head * length, (head + 1) * length)
            s = scores[group % 2, :, lanes]
            top = jnp.max(s, axis=0, keepdims=True)
            weights[group % 2, :, lanes] = jnp.exp2(s - top).astype(BF16)

    def mix(group):
        mine = slice(group * length, (group + 1) * length)
        for head in range(HEADS):
            rows = slice(head * sz.pad_head, (head + 1) * sz.pad_head)
            lanes = slice(head * length, (head + 1) * length)
            mixed = nn(values[rows, mine], weights[group % 2, :, lanes])
            total = mixed[sz.head : sz.head + 1]
            gated[rows, mine] = (mixed * (1.0 / total) * gates[rows, mine]).astype(BF16)

    score(0)
    for group in range(groups):
        if group + 1 < groups:
            score(group + 1)
        soften(group)
        mix(group)


def attend(sz, groups, length, start_of, stride, per_group, gain, packed, work, emit=None):
    wqt, wk, wvt, wgt, wo, bias_col = packed
    xs, ys, normed, queries, keys, values, gates = work[:7]
    gated = work[9]
    run = length // per_group
    factor = math.log2(math.e) / sz.head**0.5
    lane = lax.broadcasted_iota(jnp.int32, (1, sz.lanes), 1)
    inside = lane < sz.width
    gain_row = gain[...].reshape(1, sz.width)

    def places(group):
        return [pl.ds(start_of(group, c), run, stride=stride) for c in range(per_group)]

    def tokens_of(group):
        parts = [
            jnp.concatenate([xs[k, place, :] for place in places(group)], axis=0)
            for k in range(sz.chunks)
        ]
        return jnp.concatenate(parts, axis=1)

    for group in range(groups):
        x = tokens_of(group)
        mean = jnp.sum(x, axis=1, keepdims=True) * (1.0 / sz.width)
        centred = jnp.where(inside, x - mean, 0.0)
        spread = jnp.sum(centred * centred, axis=1, keepdims=True) * (1.0 / sz.width)
        value = centred[:, : sz.width] * lax.rsqrt(spread + 1e-05) * gain_row
        normed[group * length : (group + 1) * length] = value.astype(BF16)
    z = normed[...]
    feature = lax.broadcasted_iota(jnp.int32, (sz.rows, 1), 0)
    ones_row = jnp.where(feature % sz.pad_head == sz.head, 1.0, 0.0)
    queries[...] = (nt(wqt[...], z) * factor).astype(BF16)
    keys[...] = nn(z, wk[...]).astype(BF16)
    values[...] = (nt(wvt[...], z) + ones_row).astype(BF16)
    gates[...] = jax.nn.sigmoid(nt(wgt[...], z) + bias_col[...])
    mix_lines(sz, groups, length, work)
    for group in range(groups):
        mine = slice(group * length, (group + 1) * length)
        y = tokens_of(group) + tn(gated[:, mine], wo[...])
        if emit is not None:
            emit(group, y)
            continue
        for k in range(sz.chunks):
            part = y[:, k * LANES : (k + 1) * LANES]
            for c, place in enumerate(places(group)):
                ys[k, place, :] = part[c * run : (c + 1) * run]


class Lines:
    def __init__(self, sz, groups, length, start_of, stride, per_group, gain, packed, work, quarters):
        self.sz, self.groups, self.length = sz, groups, length
        self.quarters = quarters
        self.gain, self.packed, self.work = gain, packed, work
        self.half = length // 2
        self.part = groups * self.half
        self.start_of, self.stride, self.per_group = start_of, stride, per_group
        self.run = self.half // 2 // per_group

    def order(self, line):
        return (0, 1) if line % 2 == 0 else (1, 0)

    def base(self, quarter):
        size = self.part // 2
        return pl.multiple_of(quarter * size, size)

    def places(self, line, part):
        return [
            pl.ds(self.base(quarter) + self.start_of(line, c), self.run, stride=self.stride)
            for quarter in self.quarters[part]
            for c in range(self.per_group)
        ]

    def gather(self, spots):
        xs = self.work[0]
        parts = [
            jnp.concatenate([xs[k, place, :] for place in spots], axis=0)
            for k in range(self.sz.chunks)
        ]
        return jnp.concatenate(parts, axis=1)

    def tile(self, index, part):
        lines = (2 * index, 2 * index + 1)
        return lines if part == 0 else lines[::-1]

    def absorb(self, part, source):
        sz, length, half = self.sz, self.length, self.half
        wqt, wk, wvt, wgt, _, bias_col = self.packed
        xs, _, normed, queries, keys, values, gates = self.work[:7]
        count = source.shape[0] // 4
        for quarter in self.quarters[part]:
            blocks = source.at[pl.ds(quarter * count, count)]
            unpack_tokens(sz, blocks, xs, self.base(quarter), self.part // 2)
        factor = math.log2(math.e) / sz.head**0.5
        inside = lax.broadcasted_iota(jnp.int32, (1, sz.lanes), 1) < sz.width
        gain_row = self.gain[...].reshape(1, sz.width)
        for index in range(self.groups // 2):
            first, second = self.tile(index, part)
            x = self.gather(self.places(first, part) + self.places(second, part))
            mean = jnp.sum(x, axis=1, keepdims=True) * (1.0 / sz.width)
            centred = jnp.where(inside, x - mean, 0.0)
            spread = jnp.sum(centred * centred, axis=1, keepdims=True) * (1.0 / sz.width)
            value = centred[:, : sz.width] * lax.rsqrt(spread + 1e-05) * gain_row
            normed[index * length : (index + 1) * length] = value.astype(BF16)
        z = normed[: self.part]
        made = nn(z, wk[...]).astype(BF16)
        for index in range(self.groups // 2):
            for place, line in enumerate(self.tile(index, part)):
                low = index * length + place * half
                spot = line * length + place * half
                keys[spot : spot + half] = made[low : low + half]
        feature = lax.broadcasted_iota(jnp.int32, (sz.rows, 1), 0)
        ones_row = jnp.where(feature % sz.pad_head == sz.head, 1.0, 0.0)
        self.settle(part, queries, (nt(wqt[...], z) * factor).astype(BF16))
        self.settle(part, values, (nt(wvt[...], z) + ones_row).astype(BF16))
        self.settle(part, gates, jax.nn.sigmoid(nt(wgt[...], z) + bias_col[...]))

    def settle(self, part, ref, value):
        length = self.length
        lane = lax.broadcasted_iota(jnp.int32, (ref.shape[0], length), 1)
        for index in range(self.groups // 2):
            new = value[:, index * length : (index + 1) * length]
            even = slice(2 * index * length, (2 * index + 1) * length)
            odd = slice((2 * index + 1) * length, (2 * index + 2) * length)
            if part == 0:
                ref[:, even] = new
                continue
            old = ref[:, even]
            ref[:, even] = jnp.where(lane < self.half, old, new)
            ref[:, odd] = jnp.where(lane < self.half, new, old)

    def finish(self, emit=None):
        sz, length, run = self.sz, self.length, self.run
        wo = self.packed[4]
        ys, gated = self.work[1], self.work[9]
        mix_lines(sz, self.groups, length, self.work)
        for line in range(self.groups):
            mine = slice(line * length, (line + 1) * length)
            spots = [place for part in self.order(line) for place in self.places(line, part)]
            y = self.gather(spots) + tn(gated[:, mine], wo[...])
            if emit is not None:
                emit(line, y, [q for part in self.order(line) for q in self.quarters[part]])
                continue
            for k in range(sz.chunks):
                piece = y[:, k * LANES : (k + 1) * LANES]
                for i, place in enumerate(spots):
                    ys[k, place, :] = piece[i * run : (i + 1) * run]


def pack_tokens(sz, ys, target):
    tokens = ys.shape[1]
    n = target.shape[0]
    block = tokens // n
    tail = target.shape[2:]
    fold = math.prod(tail) // LANES
    for k in range(sz.full):
        part = ys[k].reshape((n, block // fold) + tail)
        target[:, k * block // fold : (k + 1) * block // fold] = part.astype(BF16)
    if sz.rest:
        joined = None
        for q in range(sz.side):
            part = ys[sz.full, pl.ds(q, tokens // sz.side, stride=sz.side), :]
            part = pltpu.roll(part, q * sz.rest, 1) if q else part
            joined = part if joined is None else joined + part
        part = joined.reshape((n, block // sz.side // fold) + tail)
        target[:, sz.full * block // fold :] = part.astype(BF16)


def unpack_tokens(sz, source, xs, base=0, tokens=None):
    tokens = tokens or xs.shape[1]
    n = source.shape[0]
    block = tokens // n
    fold = math.prod(source.shape[2:]) // LANES
    for k in range(sz.full):
        part = source[:, k * block // fold : (k + 1) * block // fold]
        xs[k, pl.ds(base, tokens), :] = part.astype(F32).reshape(tokens, LANES)
    if sz.rest:
        joined = source[:, sz.full * block // fold :].astype(F32)
        joined = joined.reshape(tokens // sz.side, LANES)
        inside = lax.broadcasted_iota(jnp.int32, (1, LANES), 1) < sz.rest
        for q in range(sz.side):
            part = pltpu.roll(joined, LANES - q * sz.rest, 1) if q else joined
            place = pl.ds(base + q, tokens // sz.side, stride=sz.side)
            xs[sz.full, place, :] = jnp.where(inside, part, 0.0)


def turn_tokens(sz, n, rows, source, xs, ys):
    cols, width, length = source.shape
    for c in range(cols):
        turned = source[c].astype(F32).T
        for k in range(sz.chunks):
            part = turned[:, k * LANES : min((k + 1) * LANES, width)]
            if part.shape[1] < LANES:
                pad = jnp.zeros((length, LANES - part.shape[1]), F32)
                part = jnp.concatenate([part, pad], axis=1)
            xs[k, c * length : (c + 1) * length] = part
    for k in range(sz.chunks):
        for c in range(cols):
            for r in range(rows):
                part = xs[k, pl.ds(c * length + r, n, stride=rows), :]
                ys[k, pl.ds(r * cols + c, n, stride=rows * cols), :] = part


def row_kernel(sz, n, rows, cols, *refs):
    x_ref, gain, *own_weights = refs[:5]
    next_weights = refs[5:8]
    result, *next_packed = refs[8:15]
    sent, got, back, *rest = refs[15:]
    packed, rest = rest[:6], rest[6:]
    work = rest[:10]
    send_a, recv_a, send_b, recv_b, local_sem = rest[10:]
    me = lax.axis_index("row")
    block = rows * cols

    barrier = pltpu.get_barrier_semaphore()

    def greet(step, carry):
        peer = lax.rem(me + step, n)
        pl.semaphore_signal(barrier, inc=1, device_id={"row": peer}, device_id_type=MESH)
        return carry

    lax.fori_loop(1, n, greet, 0)
    turn_tokens(sz, n, rows, x_ref, work[0], work[1])
    pack_tokens(sz, work[1], sent)
    pl.semaphore_wait(barrier, n - 1)

    def exchange(source, target, send, recv, body):
        def copy(peer, slot):
            return pltpu.make_async_remote_copy(
                src_ref=source.at[peer],
                dst_ref=target.at[slot],
                send_sem=send.at[peer],
                recv_sem=recv.at[slot],
                device_id={"row": peer},
                device_id_type=MESH,
            )

        def start(step, carry):
            copy(lax.rem(me + step, n), me).start()
            return carry

        lax.fori_loop(1, n, start, 0)
        own = pltpu.make_async_copy(source.at[me], target.at[me], local_sem)
        own.start()
        body()
        own.wait()

        def finish(step, carry):
            peer = lax.rem(me + step, n)
            copy(peer, me).wait_send()
            copy(peer, peer).wait_recv()
            return carry

        lax.fori_loop(1, n, finish, 0)

    exchange(
        sent,
        got,
        send_a,
        recv_a,
        lambda: prepare(sz, own_weights, packed),
    )
    unpack_tokens(sz, got, work[0])
    attend(
        sz, rows, n * cols, lambda g, c: g * cols + c, block, cols, gain, packed, work
    )
    pack_tokens(sz, work[1], back)
    exchange(
        back,
        result,
        send_b,
        recv_b,
        lambda: prepare(sz, next_weights, next_packed),
    )


def col_kernel(sz, cols, x_ref, gain, *refs):
    packed, result, work = refs[:6], refs[6], refs[7:]
    unpack_tokens(sz, x_ref, work[0])
    length = work[0].shape[1] // cols

    def emit(group, y):
        result[group] = y[:, : sz.width].T.astype(BF16)

    attend(sz, cols, length, lambda g, c: g, cols, 1, gain, packed, work, emit)


def axial_kernel(sz, n, rows, cols, *refs):
    outer, result, refs = refs[:9], refs[9], refs[10:]
    local, refs = refs[:9], refs[9:]
    sent, got, back, home, *refs = refs
    packed_row, packed_col, refs = refs[:6], refs[6:12], refs[12:]
    work = refs[:10]
    load_sem, send_a, recv_a, send_b, recv_b, own_sem = refs[10:]
    x_ref, row_gain, *row_weights = local[:5]
    col_gain, *col_weights = local[5:]
    me = lax.axis_index("row")
    block = rows * cols
    length = n * cols

    def steps(low, high, body):
        def step(i, carry):
            body(i)
            return carry

        lax.fori_loop(low, high, step, 0)

    def partner(i):
        return lax.rem(me + i, n)

    barrier = pltpu.get_barrier_semaphore()

    def greet(i):
        peer = partner(i)
        pl.semaphore_signal(barrier, inc=1, device_id={"row": peer}, device_id_type=MESH)

    steps(1, n, greet)
    loads = [
        pltpu.make_async_copy(source, target, load_sem.at[i])
        for i, (source, target) in enumerate(zip(outer, local))
    ]
    for load in loads:
        load.start()

    fourth = n // 4
    layer = me // fourth

    class Exchange:
        def __init__(self, source, target, send, recv, own):
            self.source, self.target = source, target
            self.send, self.recv = send, recv
            self.own = pltpu.make_async_copy(source.at[me], target.at[me], own)

        def copy(self, peer, slot):
            return pltpu.make_async_remote_copy(
                src_ref=self.source.at[peer],
                dst_ref=self.target.at[slot],
                send_sem=self.send.at[peer],
                recv_sem=self.recv.at[slot],
                device_id={"row": peer},
                device_id_type=MESH,
            )

        def start(self):
            steps(1, n, lambda i: self.copy(partner(i), me).start())
            self.own.start()

        def arrive(self, quarters):
            for quarter in quarters:
                own = quarter is layer
                if own:
                    self.own.wait()

                def wait(i):
                    peer = quarter * fourth + lax.rem(me + i, fourth)
                    self.copy(peer, peer).wait_recv()

                steps(1 if own else 0, fourth, wait)
            return self.target

        def leave(self):
            steps(1, n, lambda i: self.copy(partner(i), me).wait_send())

    def ahead(i):
        return lax.rem(layer + i, 4)

    def choose(*table):
        return sum(jnp.where(layer == i, value, 0) for i, value in enumerate(table))

    first = Exchange(sent, got, send_a, recv_a, own_sem.at[0])
    second = Exchange(back, home, send_b, recv_b, own_sem.at[1])
    early = ((layer, ahead(3)), (ahead(1), ahead(2)))
    late = ((layer, choose(2, 0, 0, 2)), (choose(1, 2, 1, 0), choose(3, 3, 3, 1)))
    loads[0].wait()
    turn_tokens(sz, n, rows, x_ref, work[0], work[1])
    pack_tokens(sz, work[1], sent)
    pl.semaphore_wait(barrier, n - 1)
    first.start()
    for load in loads[1:]:
        load.wait()
    prepare(sz, row_weights, packed_row)
    prepare(sz, col_weights, packed_col)
    place = lambda g, c: g * cols + c
    lines = Lines(sz, rows, length, place, block, cols, row_gain, packed_row, work, early)
    for part in range(2):
        lines.absorb(part, first.arrive(early[part]))
    lines.finish()
    pack_tokens(sz, work[1], back)
    second.start()
    first.leave()
    height = n * rows
    place = lambda g, c: g
    lines = Lines(sz, cols, height, place, cols, 1, col_gain, packed_col, work, late)
    for part in range(2):
        lines.absorb(part, second.arrive(late[part]))
    ys = work[1]
    size = height // 4

    def emit(line, y, quarters):
        low = line * height
        for i, quarter in enumerate(quarters):
            spot = pl.multiple_of(low + quarter * size, size)
            for k in range(sz.chunks):
                piece = y[i * size : (i + 1) * size, k * LANES : (k + 1) * LANES]
                ys[k, pl.ds(spot, size), :] = piece
        y = jnp.concatenate([ys[k, low : low + height] for k in range(sz.chunks)], axis=1)
        result[line] = y[:, : sz.width].T.astype(BF16)

    lines.finish(emit)
    second.leave()


def swap_columns(sz, done, block, rows, cols):
    n = done.shape[0]
    parts = [done[:, k * block : (k + 1) * block] for k in range(sz.full)]
    if sz.rest:
        parts.append(done[:, sz.full * block :].reshape(n, block, sz.rest))
    whole = jnp.concatenate(parts, -1).reshape(rows, cols, sz.width)
    whole = lax.all_to_all(whole, "col", split_axis=1, concat_axis=0, tiled=True)
    whole = whole.reshape(n, block, sz.width)
    parts = [whole[..., k * LANES : (k + 1) * LANES] for k in range(sz.full)]
    if sz.rest:
        parts.append(whole[..., sz.full * LANES :].reshape(n, block // sz.side, LANES))
    return jnp.concatenate(parts, 1)


VMEM = pl.BlockSpec(memory_space=pltpu.VMEM)


def per_device(
    pair_map, row_gain, row_proj, row_gate_bias, row_out, col_gain, col_proj, col_gate_bias, col_out
):
    local_rows, local_cols, width = pair_map.shape
    n = lax.axis_size("row")
    sz = Sizes(width)
    rows = local_rows // n
    tokens = local_rows * local_cols
    block = rows * local_cols
    shape = (n, sz.packed_rows(block), LANES)
    turned = jnp.transpose(pair_map, (1, 2, 0))
    splits = lax.axis_size("col")
    folds = shape[1] % FOLD == 0 and block % (FOLD * sz.side) == 0
    even = rows % 2 == 0 and local_cols % 2 == 0 and n % 4 == 0
    if splits == 1 and folds and even and n * local_cols == local_rows == LANES:
        folded = (n, shape[1] // FOLD, FOLD, LANES)
        operands = (turned, row_gain, row_proj, row_gate_bias, row_out)
        operands += (col_gain, col_proj, col_gate_bias, col_out)
        operands = [pltpu.with_memory_space_constraint(a, pltpu.HBM) for a in operands]
        updated = pl.pallas_call(
            functools.partial(axial_kernel, sz, n, rows, local_cols),
            out_shape=jax.ShapeDtypeStruct(turned.shape, BF16),
            in_specs=[pl.BlockSpec(memory_space=pltpu.HBM)] * len(operands),
            out_specs=VMEM,
            scratch_shapes=[pltpu.VMEM(a.shape, a.dtype) for a in operands]
            + [pltpu.VMEM(folded, BF16)] * 4
            + [pltpu.VMEM(*spec) for spec in sz.packed_shapes()] * 2
            + sz.work_scratch(tokens, max(n * local_cols, local_rows))
            + [pltpu.SemaphoreType.DMA((len(operands),))]
            + [pltpu.SemaphoreType.DMA((n,))] * 4
            + [pltpu.SemaphoreType.DMA((2,))],
            compiler_params=pltpu.CompilerParams(
                collective_id=0, has_side_effects=True, vmem_limit_bytes=VMEM_LIMIT
            ),
            name="axial_attention",
        )(*operands)
        return jnp.transpose(updated, (2, 0, 1))
    done, *packed = pl.pallas_call(
        functools.partial(row_kernel, sz, n, rows, local_cols),
        out_shape=[jax.ShapeDtypeStruct(shape, BF16)]
        + [jax.ShapeDtypeStruct(*spec) for spec in sz.packed_shapes()],
        in_specs=[VMEM] * 8,
        out_specs=[VMEM] * 7,
        scratch_shapes=[pltpu.VMEM(shape, BF16)] * 3
        + [pltpu.VMEM(*spec) for spec in sz.packed_shapes()]
        + sz.work_scratch(tokens, n * local_cols)
        + [pltpu.SemaphoreType.DMA((n,))] * 4
        + [pltpu.SemaphoreType.DMA],
        compiler_params=pltpu.CompilerParams(collective_id=0, has_side_effects=True),
        name="row_attention",
    )(turned, row_gain, row_proj, row_gate_bias, row_out, col_proj, col_gate_bias, col_out)
    if splits > 1:
        done = swap_columns(sz, done, block, local_rows, local_cols)
    cols = local_cols // splits
    full = tokens // cols
    updated = pl.pallas_call(
        functools.partial(col_kernel, sz, cols),
        out_shape=jax.ShapeDtypeStruct((cols, width, full), BF16),
        in_specs=[VMEM] * 8,
        out_specs=VMEM,
        scratch_shapes=sz.work_scratch(tokens, full),
        name="col_attention",
    )(done, col_gain, *packed)
    updated = jnp.transpose(updated, (2, 0, 1))
    if splits > 1:
        updated = lax.all_to_all(updated, "col", split_axis=0, concat_axis=1, tiled=True)
    return updated


def solution(mesh):
    return jax.shard_map(
        per_device,
        mesh=mesh,
        in_specs=(P(("groups", "col"), "row", None), P(), P(), P(), P(), P(), P(), P(), P()),
        out_specs=P(("groups", "col"), "row", None),
        check_vma=False,
    )
```

```python
import functools
import math

import jax
import jax.numpy as jnp
from jax import lax
from jax.experimental import pallas as pl
from jax.experimental.pallas import tpu as pltpu
from jax.sharding import PartitionSpec as P

HEADS = 8
LANES = 128
FOLD = 4
VMEM_LIMIT = 32 * 2**20
F32 = jnp.float32
BF16 = jnp.bfloat16
MESH = pl.DeviceIdType.MESH


def ceil_to(value, step):
    return -(-value // step) * step


def nt(a, b):
    return lax.dot_general(a, b, (((1,), (1,)), ((), ())), preferred_element_type=F32)


def tn(a, b):
    return lax.dot_general(a, b, (((0,), (0,)), ((), ())), preferred_element_type=F32)


def nn(a, b):
    return jnp.dot(a, b, preferred_element_type=F32)


class Sizes:
    def __init__(self, width):
        self.width = width
        self.head = width // HEADS
        self.pad_head = ceil_to(self.head + 1, 16)
        self.pad_key = LANES // (LANES // self.head)
        while LANES % self.pad_key:
            self.pad_key += 1
        self.rows = HEADS * self.pad_head
        self.keys = HEADS * self.pad_key
        assert self.pad_head <= self.pad_key
        self.lanes = ceil_to(width, LANES)
        self.chunks = self.lanes // LANES
        self.full = width // LANES
        self.rest = width % LANES
        self.side = LANES // self.rest if self.rest else 1

    def packed_rows(self, block):
        assert self.rest == 0 or (LANES % self.rest == 0 and block % self.side == 0)
        return self.full * block + (block // self.side if self.rest else 0)

    def packed_shapes(self):
        return [
            ((self.rows, self.width), BF16),
            ((self.width, self.keys), BF16),
            ((self.rows, self.width), BF16),
            ((self.rows, self.width), BF16),
            ((self.rows, self.lanes), BF16),
            ((self.rows, 1), F32),
        ]

    def work_scratch(self, tokens, length):
        return [
            pltpu.VMEM((self.chunks, tokens, LANES), F32),
            pltpu.VMEM((self.chunks, tokens, LANES), F32),
            pltpu.VMEM((tokens, self.width), BF16),
            pltpu.VMEM((self.rows, tokens), BF16),
            pltpu.VMEM((tokens, self.keys), BF16),
            pltpu.VMEM((self.rows, tokens), BF16),
            pltpu.VMEM((self.rows, tokens), F32),
            pltpu.VMEM((2, length, HEADS * length), F32),
            pltpu.VMEM((2, length, HEADS * length), BF16),
            pltpu.VMEM((self.rows, tokens), BF16),
        ]


def prepare(sz, weights, packed):
    proj, bias, out = weights
    wqt, wk, wvt, wgt, wo, bias_col = packed

    def window(block):
        start = block * sz.width
        low = start // LANES * LANES
        high = min(ceil_to(start + sz.width, LANES), 4 * sz.width)
        return proj[:, low:high], start - low, high - low

    def hits(shape, axis, pad, shift):
        place = lax.broadcasted_iota(jnp.int32, shape, axis)
        source = lax.broadcasted_iota(jnp.int32, shape, 1 - axis) - shift
        inner = place % pad
        return (inner < sz.head) & (source == place // pad * sz.head + inner)

    def pick(*spec):
        return jnp.where(hits(*spec), 1.0, 0.0).astype(BF16)

    part, shift, size = window(1)
    wk[...] = nn(part, pick((size, sz.keys), 1, sz.pad_key, shift)).astype(BF16)
    for block, ref, pad in ((0, wqt, sz.pad_head), (2, wvt, sz.pad_head), (3, wgt, sz.pad_head)):
        part, shift, size = window(block)
        ref[...] = nt(pick((HEADS * pad, size), 0, pad, shift), part).astype(BF16)
    spec = (sz.rows, sz.width), 0, sz.pad_head, 0
    wo[...] = jnp.zeros(wo.shape, BF16)
    wo[:, : sz.width] = nn(pick(*spec), out[...]).astype(BF16)
    row = bias[...].reshape(1, sz.width)
    bias_col[...] = jnp.sum(jnp.where(hits(*spec), row, 0.0), axis=1, keepdims=True)


def mix_lines(sz, groups, length, work):
    queries, keys, values, gates, scores, weights, gated = work[3:]
    pack = LANES // sz.pad_key
    spare = sz.pad_key - sz.pad_head
    zeros = jnp.zeros((sz.pad_key, length), BF16)

    def score(group):
        mine = slice(group * length, (group + 1) * length)
        for first in range(0, HEADS, pack):
            blocks = []
            for j in range(pack):
                low = (first + j) * sz.pad_head
                own = queries[low : low + sz.pad_head, mine]
                if spare:
                    gap = jnp.zeros((spare, length), BF16)
                    own = jnp.concatenate([own, gap], axis=0)
                blocks.append(
                    jnp.concatenate([own if i == j else zeros for i in range(pack)], axis=1)
                )
            lanes = slice(first * sz.pad_key, (first + pack) * sz.pad_key)
            scores[group % 2, :, first * length : (first + pack) * length] = nn(
                keys[mine, lanes], jnp.concatenate(blocks, axis=0)
            )

    def soften(group):
        for head in range(HEADS):
            lanes = slice(head * length, (head + 1) * length)
            s = scores[group % 2, :, lanes]
            top = jnp.max(s, axis=0, keepdims=True)
            weights[group % 2, :, lanes] = jnp.exp2(s - top).astype(BF16)

    def mix(group):
        mine = slice(group * length, (group + 1) * length)
        for head in range(HEADS):
            rows = slice(head * sz.pad_head, (head + 1) * sz.pad_head)
            lanes = slice(head * length, (head + 1) * length)
            mixed = nn(values[rows, mine], weights[group % 2, :, lanes])
            total = mixed[sz.head : sz.head + 1]
            gated[rows, mine] = (mixed * (1.0 / total) * gates[rows, mine]).astype(BF16)

    score(0)
    for group in range(groups):
        if group + 1 < groups:
            score(group + 1)
        soften(group)
        if group > 0:
            mix(group - 1)
    mix(groups - 1)


def attend(sz, groups, length, start_of, stride, per_group, gain, packed, work, emit=None):
    wqt, wk, wvt, wgt, wo, bias_col = packed
    xs, ys, normed, queries, keys, values, gates = work[:7]
    gated = work[9]
    run = length // per_group
    factor = math.log2(math.e) / sz.head**0.5
    lane = lax.broadcasted_iota(jnp.int32, (1, sz.lanes), 1)
    inside = lane < sz.width
    gain_row = gain[...].reshape(1, sz.width)

    def places(group):
        return [pl.ds(start_of(group, c), run, stride=stride) for c in range(per_group)]

    def tokens_of(group):
        parts = [
            jnp.concatenate([xs[k, place, :] for place in places(group)], axis=0)
            for k in range(sz.chunks)
        ]
        return jnp.concatenate(parts, axis=1)

    for group in range(groups):
        x = tokens_of(group)
        mean = jnp.sum(x, axis=1, keepdims=True) * (1.0 / sz.width)
        centred = jnp.where(inside, x - mean, 0.0)
        spread = jnp.sum(centred * centred, axis=1, keepdims=True) * (1.0 / sz.width)
        value = centred[:, : sz.width] * lax.rsqrt(spread + 1e-05) * gain_row
        normed[group * length : (group + 1) * length] = value.astype(BF16)
    z = normed[...]
    feature = lax.broadcasted_iota(jnp.int32, (sz.rows, 1), 0)
    ones_row = jnp.where(feature % sz.pad_head == sz.head, 1.0, 0.0)
    queries[...] = (nt(wqt[...], z) * factor).astype(BF16)
    keys[...] = nn(z, wk[...]).astype(BF16)
    values[...] = (nt(wvt[...], z) + ones_row).astype(BF16)
    gates[...] = jax.nn.sigmoid(nt(wgt[...], z) + bias_col[...])
    mix_lines(sz, groups, length, work)
    for group in range(groups):
        mine = slice(group * length, (group + 1) * length)
        y = tokens_of(group) + tn(gated[:, mine], wo[...])
        if emit is not None:
            emit(group, y)
            continue
        for k in range(sz.chunks):
            part = y[:, k * LANES : (k + 1) * LANES]
            for c, place in enumerate(places(group)):
                ys[k, place, :] = part[c * run : (c + 1) * run]


class Lines:
    def __init__(self, sz, groups, length, start_of, stride, per_group, gain, packed, work, quarters):
        self.sz, self.groups, self.length = sz, groups, length
        self.quarters = quarters
        self.gain, self.packed, self.work = gain, packed, work
        self.half = length // 2
        self.part = groups * self.half
        self.start_of, self.stride, self.per_group = start_of, stride, per_group
        self.run = self.half // 2 // per_group

    def order(self, line):
        return (0, 1) if line % 2 == 0 else (1, 0)

    def base(self, quarter):
        size = self.part // 2
        return pl.multiple_of(quarter * size, size)

    def places(self, line, part):
        return [
            pl.ds(self.base(quarter) + self.start_of(line, c), self.run, stride=self.stride)
            for quarter in self.quarters[part]
            for c in range(self.per_group)
        ]

    def gather(self, spots):
        xs = self.work[0]
        parts = [
            jnp.concatenate([xs[k, place, :] for place in spots], axis=0)
            for k in range(self.sz.chunks)
        ]
        return jnp.concatenate(parts, axis=1)

    def tile(self, index, part):
        lines = (2 * index, 2 * index + 1)
        return lines if part == 0 else lines[::-1]

    def absorb(self, part, source):
        sz, length, half = self.sz, self.length, self.half
        wqt, wk, wvt, wgt, _, bias_col = self.packed
        xs, _, normed, queries, keys, values, gates = self.work[:7]
        count = source.shape[0] // 4
        for quarter in self.quarters[part]:
            blocks = source.at[pl.ds(quarter * count, count)]
            unpack_tokens(sz, blocks, xs, self.base(quarter), self.part // 2)
        factor = math.log2(math.e) / sz.head**0.5
        inside = lax.broadcasted_iota(jnp.int32, (1, sz.lanes), 1) < sz.width
        gain_row = self.gain[...].reshape(1, sz.width)
        for index in range(self.groups // 2):
            first, second = self.tile(index, part)
            x = self.gather(self.places(first, part) + self.places(second, part))
            mean = jnp.sum(x, axis=1, keepdims=True) * (1.0 / sz.width)
            centred = jnp.where(inside, x - mean, 0.0)
            spread = jnp.sum(centred * centred, axis=1, keepdims=True) * (1.0 / sz.width)
            value = centred[:, : sz.width] * lax.rsqrt(spread + 1e-05) * gain_row
            normed[index * length : (index + 1) * length] = value.astype(BF16)
        z = normed[: self.part]
        made = nn(z, wk[...]).astype(BF16)
        for index in range(self.groups // 2):
            for place, line in enumerate(self.tile(index, part)):
                low = index * length + place * half
                spot = line * length + place * half
                keys[spot : spot + half] = made[low : low + half]
        feature = lax.broadcasted_iota(jnp.int32, (sz.rows, 1), 0)
        ones_row = jnp.where(feature % sz.pad_head == sz.head, 1.0, 0.0)
        self.settle(part, queries, (nt(wqt[...], z) * factor).astype(BF16))
        self.settle(part, values, (nt(wvt[...], z) + ones_row).astype(BF16))
        self.settle(part, gates, jax.nn.sigmoid(nt(wgt[...], z) + bias_col[...]))

    def settle(self, part, ref, value):
        length = self.length
        lane = lax.broadcasted_iota(jnp.int32, (ref.shape[0], length), 1)
        for index in range(self.groups // 2):
            new = value[:, index * length : (index + 1) * length]
            even = slice(2 * index * length, (2 * index + 1) * length)
            odd = slice((2 * index + 1) * length, (2 * index + 2) * length)
            if part == 0:
                ref[:, even] = new
                continue
            old = ref[:, even]
            ref[:, even] = jnp.where(lane < self.half, old, new)
            ref[:, odd] = jnp.where(lane < self.half, new, old)

    def finish(self, emit=None):
        sz, length, run = self.sz, self.length, self.run
        wo = self.packed[4]
        ys, gated = self.work[1], self.work[9]
        mix_lines(sz, self.groups, length, self.work)
        for line in range(self.groups):
            mine = slice(line * length, (line + 1) * length)
            spots = [place for part in self.order(line) for place in self.places(line, part)]
            y = self.gather(spots) + tn(gated[:, mine], wo[...])
            if emit is not None:
                emit(line, y, [q for part in self.order(line) for q in self.quarters[part]])
                continue
            for k in range(sz.chunks):
                piece = y[:, k * LANES : (k + 1) * LANES]
                for i, place in enumerate(spots):
                    ys[k, place, :] = piece[i * run : (i + 1) * run]


def pack_tokens(sz, ys, target):
    tokens = ys.shape[1]
    n = target.shape[0]
    block = tokens // n
    tail = target.shape[2:]
    fold = math.prod(tail) // LANES
    for k in range(sz.full):
        part = ys[k].reshape((n, block // fold) + tail)
        target[:, k * block // fold : (k + 1) * block // fold] = part.astype(BF16)
    if sz.rest:
        joined = None
        for q in range(sz.side):
            part = ys[sz.full, pl.ds(q, tokens // sz.side, stride=sz.side), :]
            part = pltpu.roll(part, q * sz.rest, 1) if q else part
            joined = part if joined is None else joined + part
        part = joined.reshape((n, block // sz.side // fold) + tail)
        target[:, sz.full * block // fold :] = part.astype(BF16)


def unpack_tokens(sz, source, xs, base=0, tokens=None):
    tokens = tokens or xs.shape[1]
    n = source.shape[0]
    block = tokens // n
    fold = math.prod(source.shape[2:]) // LANES
    for k in range(sz.full):
        part = source[:, k * block // fold : (k + 1) * block // fold]
        xs[k, pl.ds(base, tokens), :] = part.astype(F32).reshape(tokens, LANES)
    if sz.rest:
        joined = source[:, sz.full * block // fold :].astype(F32)
        joined = joined.reshape(tokens // sz.side, LANES)
        inside = lax.broadcasted_iota(jnp.int32, (1, LANES), 1) < sz.rest
        for q in range(sz.side):
            part = pltpu.roll(joined, LANES - q * sz.rest, 1) if q else joined
            place = pl.ds(base + q, tokens // sz.side, stride=sz.side)
            xs[sz.full, place, :] = jnp.where(inside, part, 0.0)


def turn_tokens(sz, n, rows, source, xs, ys):
    cols, width, length = source.shape
    for c in range(cols):
        turned = source[c].astype(F32).T
        for k in range(sz.chunks):
            part = turned[:, k * LANES : min((k + 1) * LANES, width)]
            if part.shape[1] < LANES:
                pad = jnp.zeros((length, LANES - part.shape[1]), F32)
                part = jnp.concatenate([part, pad], axis=1)
            xs[k, c * length : (c + 1) * length] = part
    for k in range(sz.chunks):
        for c in range(cols):
            for r in range(rows):
                part = xs[k, pl.ds(c * length + r, n, stride=rows), :]
                ys[k, pl.ds(r * cols + c, n, stride=rows * cols), :] = part


def row_kernel(sz, n, rows, cols, *refs):
    x_ref, gain, *own_weights = refs[:5]
    next_weights = refs[5:8]
    result, *next_packed = refs[8:15]
    sent, got, back, *rest = refs[15:]
    packed, rest = rest[:6], rest[6:]
    work = rest[:10]
    send_a, recv_a, send_b, recv_b, local_sem = rest[10:]
    me = lax.axis_index("row")
    block = rows * cols

    barrier = pltpu.get_barrier_semaphore()

    def greet(step, carry):
        peer = lax.rem(me + step, n)
        pl.semaphore_signal(barrier, inc=1, device_id={"row": peer}, device_id_type=MESH)
        return carry

    lax.fori_loop(1, n, greet, 0)
    turn_tokens(sz, n, rows, x_ref, work[0], work[1])
    pack_tokens(sz, work[1], sent)
    pl.semaphore_wait(barrier, n - 1)

    def exchange(source, target, send, recv, body):
        def copy(peer, slot):
            return pltpu.make_async_remote_copy(
                src_ref=source.at[peer],
                dst_ref=target.at[slot],
                send_sem=send.at[peer],
                recv_sem=recv.at[slot],
                device_id={"row": peer},
                device_id_type=MESH,
            )

        def start(step, carry):
            copy(lax.rem(me + step, n), me).start()
            return carry

        lax.fori_loop(1, n, start, 0)
        own = pltpu.make_async_copy(source.at[me], target.at[me], local_sem)
        own.start()
        body()
        own.wait()

        def finish(step, carry):
            peer = lax.rem(me + step, n)
            copy(peer, me).wait_send()
            copy(peer, peer).wait_recv()
            return carry

        lax.fori_loop(1, n, finish, 0)

    exchange(
        sent,
        got,
        send_a,
        recv_a,
        lambda: prepare(sz, own_weights, packed),
    )
    unpack_tokens(sz, got, work[0])
    attend(
        sz, rows, n * cols, lambda g, c: g * cols + c, block, cols, gain, packed, work
    )
    pack_tokens(sz, work[1], back)
    exchange(
        back,
        result,
        send_b,
        recv_b,
        lambda: prepare(sz, next_weights, next_packed),
    )


def col_kernel(sz, cols, x_ref, gain, *refs):
    packed, result, work = refs[:6], refs[6], refs[7:]
    unpack_tokens(sz, x_ref, work[0])
    length = work[0].shape[1] // cols

    def emit(group, y):
        result[group] = y[:, : sz.width].T.astype(BF16)

    attend(sz, cols, length, lambda g, c: g, cols, 1, gain, packed, work, emit)


def axial_kernel(sz, n, rows, cols, *refs):
    outer, result, refs = refs[:9], refs[9], refs[10:]
    local, refs = refs[:9], refs[9:]
    sent, got, back, home, *refs = refs
    packed_row, packed_col, refs = refs[:6], refs[6:12], refs[12:]
    work = refs[:10]
    load_sem, send_a, recv_a, send_b, recv_b, own_sem = refs[10:]
    x_ref, row_gain, *row_weights = local[:5]
    col_gain, *col_weights = local[5:]
    me = lax.axis_index("row")
    block = rows * cols
    length = n * cols

    def steps(low, high, body):
        def step(i, carry):
            body(i)
            return carry

        lax.fori_loop(low, high, step, 0)

    def partner(i):
        return lax.rem(me + i, n)

    barrier = pltpu.get_barrier_semaphore()

    def greet(i):
        peer = partner(i)
        pl.semaphore_signal(barrier, inc=1, device_id={"row": peer}, device_id_type=MESH)

    steps(1, n, greet)
    loads = [
        pltpu.make_async_copy(source, target, load_sem.at[i])
        for i, (source, target) in enumerate(zip(outer, local))
    ]
    for load in loads:
        load.start()

    fourth = n // 4
    layer = me // fourth

    class Exchange:
        def __init__(self, source, target, send, recv, own):
            self.source, self.target = source, target
            self.send, self.recv = send, recv
            self.own = pltpu.make_async_copy(source.at[me], target.at[me], own)

        def copy(self, peer, slot):
            return pltpu.make_async_remote_copy(
                src_ref=self.source.at[peer],
                dst_ref=self.target.at[slot],
                send_sem=self.send.at[peer],
                recv_sem=self.recv.at[slot],
                device_id={"row": peer},
                device_id_type=MESH,
            )

        def start(self):
            steps(1, n, lambda i: self.copy(partner(i), me).start())
            self.own.start()

        def arrive(self, quarters):
            for quarter in quarters:
                own = quarter is layer
                if own:
                    self.own.wait()

                def wait(i):
                    peer = quarter * fourth + lax.rem(me + i, fourth)
                    self.copy(peer, peer).wait_recv()

                steps(1 if own else 0, fourth, wait)
            return self.target

        def leave(self):
            steps(1, n, lambda i: self.copy(partner(i), me).wait_send())

    def ahead(i):
        return lax.rem(layer + i, 4)

    def choose(*table):
        return sum(jnp.where(layer == i, value, 0) for i, value in enumerate(table))

    first = Exchange(sent, got, send_a, recv_a, own_sem.at[0])
    second = Exchange(back, home, send_b, recv_b, own_sem.at[1])
    early = ((layer, ahead(3)), (ahead(1), ahead(2)))
    late = ((layer, choose(2, 0, 0, 2)), (choose(1, 2, 1, 0), choose(3, 3, 3, 1)))
    loads[0].wait()
    turn_tokens(sz, n, rows, x_ref, work[0], work[1])
    pack_tokens(sz, work[1], sent)
    pl.semaphore_wait(barrier, n - 1)
    first.start()
    for load in loads[1:]:
        load.wait()
    prepare(sz, row_weights, packed_row)
    prepare(sz, col_weights, packed_col)
    place = lambda g, c: g * cols + c
    lines = Lines(sz, rows, length, place, block, cols, row_gain, packed_row, work, early)
    for part in range(2):
        lines.absorb(part, first.arrive(early[part]))
    lines.finish()
    pack_tokens(sz, work[1], back)
    second.start()
    first.leave()
    height = n * rows
    place = lambda g, c: g
    lines = Lines(sz, cols, height, place, cols, 1, col_gain, packed_col, work, late)
    for part in range(2):
        lines.absorb(part, second.arrive(late[part]))
    ys = work[1]
    size = height // 4

    def emit(line, y, quarters):
        low = line * height
        for i, quarter in enumerate(quarters):
            spot = pl.multiple_of(low + quarter * size, size)
            for k in range(sz.chunks):
                piece = y[i * size : (i + 1) * size, k * LANES : (k + 1) * LANES]
                ys[k, pl.ds(spot, size), :] = piece
        y = jnp.concatenate([ys[k, low : low + height] for k in range(sz.chunks)], axis=1)
        result[line] = y[:, : sz.width].T.astype(BF16)

    lines.finish(emit)
    second.leave()


def swap_columns(sz, done, block, rows, cols):
    n = done.shape[0]
    parts = [done[:, k * block : (k + 1) * block] for k in range(sz.full)]
    if sz.rest:
        parts.append(done[:, sz.full * block :].reshape(n, block, sz.rest))
    whole = jnp.concatenate(parts, -1).reshape(rows, cols, sz.width)
    whole = lax.all_to_all(whole, "col", split_axis=1, concat_axis=0, tiled=True)
    whole = whole.reshape(n, block, sz.width)
    parts = [whole[..., k * LANES : (k + 1) * LANES] for k in range(sz.full)]
    if sz.rest:
        parts.append(whole[..., sz.full * LANES :].reshape(n, block // sz.side, LANES))
    return jnp.concatenate(parts, 1)


VMEM = pl.BlockSpec(memory_space=pltpu.VMEM)


def per_device(
    pair_map, row_gain, row_proj, row_gate_bias, row_out, col_gain, col_proj, col_gate_bias, col_out
):
    local_rows, local_cols, width = pair_map.shape
    n = lax.axis_size("row")
    sz = Sizes(width)
    rows = local_rows // n
    tokens = local_rows * local_cols
    block = rows * local_cols
    shape = (n, sz.packed_rows(block), LANES)
    turned = jnp.transpose(pair_map, (1, 2, 0))
    splits = lax.axis_size("col")
    folds = shape[1] % FOLD == 0 and block % (FOLD * sz.side) == 0
    even = rows % 2 == 0 and local_cols % 2 == 0 and n % 4 == 0
    if splits == 1 and folds and even and n * local_cols == local_rows == LANES:
        folded = (n, shape[1] // FOLD, FOLD, LANES)
        operands = (turned, row_gain, row_proj, row_gate_bias, row_out)
        operands += (col_gain, col_proj, col_gate_bias, col_out)
        operands = [pltpu.with_memory_space_constraint(a, pltpu.HBM) for a in operands]
        updated = pl.pallas_call(
            functools.partial(axial_kernel, sz, n, rows, local_cols),
            out_shape=jax.ShapeDtypeStruct(turned.shape, BF16),
            in_specs=[pl.BlockSpec(memory_space=pltpu.HBM)] * len(operands),
            out_specs=VMEM,
            scratch_shapes=[pltpu.VMEM(a.shape, a.dtype) for a in operands]
            + [pltpu.VMEM(folded, BF16)] * 4
            + [pltpu.VMEM(*spec) for spec in sz.packed_shapes()] * 2
            + sz.work_scratch(tokens, max(n * local_cols, local_rows))
            + [pltpu.SemaphoreType.DMA((len(operands),))]
            + [pltpu.SemaphoreType.DMA((n,))] * 4
            + [pltpu.SemaphoreType.DMA((2,))],
            compiler_params=pltpu.CompilerParams(
                collective_id=0, has_side_effects=True, vmem_limit_bytes=VMEM_LIMIT
            ),
            name="axial_attention",
        )(*operands)
        return jnp.transpose(updated, (2, 0, 1))
    done, *packed = pl.pallas_call(
        functools.partial(row_kernel, sz, n, rows, local_cols),
        out_shape=[jax.ShapeDtypeStruct(shape, BF16)]
        + [jax.ShapeDtypeStruct(*spec) for spec in sz.packed_shapes()],
        in_specs=[VMEM] * 8,
        out_specs=[VMEM] * 7,
        scratch_shapes=[pltpu.VMEM(shape, BF16)] * 3
        + [pltpu.VMEM(*spec) for spec in sz.packed_shapes()]
        + sz.work_scratch(tokens, n * local_cols)
        + [pltpu.SemaphoreType.DMA((n,))] * 4
        + [pltpu.SemaphoreType.DMA],
        compiler_params=pltpu.CompilerParams(collective_id=0, has_side_effects=True),
        name="row_attention",
    )(turned, row_gain, row_proj, row_gate_bias, row_out, col_proj, col_gate_bias, col_out)
    if splits > 1:
        done = swap_columns(sz, done, block, local_rows, local_cols)
    cols = local_cols // splits
    full = tokens // cols
    updated = pl.pallas_call(
        functools.partial(col_kernel, sz, cols),
        out_shape=jax.ShapeDtypeStruct((cols, width, full), BF16),
        in_specs=[VMEM] * 8,
        out_specs=VMEM,
        scratch_shapes=sz.work_scratch(tokens, full),
        name="col_attention",
    )(done, col_gain, *packed)
    updated = jnp.transpose(updated, (2, 0, 1))
    if splits > 1:
        updated = lax.all_to_all(updated, "col", split_axis=0, concat_axis=1, tiled=True)
    return updated


def solution(mesh):
    return jax.shard_map(
        per_device,
        mesh=mesh,
        in_specs=(P(("groups", "col"), "row", None), P(), P(), P(), P(), P(), P(), P(), P()),
        out_specs=P(("groups", "col"), "row", None),
        check_vma=False,
    )
```

```python
import functools
import math

import jax
import jax.numpy as jnp
from jax import lax
from jax.experimental import pallas as pl
from jax.experimental.pallas import tpu as pltpu
from jax.sharding import PartitionSpec as P

HEADS = 8
LANES = 128
FOLD = 4
VMEM_LIMIT = 32 * 2**20
F32 = jnp.float32
BF16 = jnp.bfloat16
MESH = pl.DeviceIdType.MESH


def ceil_to(value, step):
    return -(-value // step) * step


def nt(a, b):
    return lax.dot_general(a, b, (((1,), (1,)), ((), ())), preferred_element_type=F32)


def tn(a, b):
    return lax.dot_general(a, b, (((0,), (0,)), ((), ())), preferred_element_type=F32)


def nn(a, b):
    return jnp.dot(a, b, preferred_element_type=F32)


class Sizes:
    def __init__(self, width):
        self.width = width
        self.head = width // HEADS
        self.pad_head = ceil_to(self.head + 1, 16)
        self.pad_key = LANES // (LANES // self.head)
        while LANES % self.pad_key:
            self.pad_key += 1
        self.rows = HEADS * self.pad_head
        self.keys = HEADS * self.pad_key
        assert self.pad_head <= self.pad_key
        self.lanes = ceil_to(width, LANES)
        self.chunks = self.lanes // LANES
        self.full = width // LANES
        self.rest = width % LANES
        self.side = LANES // self.rest if self.rest else 1

    def packed_rows(self, block):
        assert self.rest == 0 or (LANES % self.rest == 0 and block % self.side == 0)
        return self.full * block + (block // self.side if self.rest else 0)

    def packed_shapes(self):
        return [
            ((self.rows, self.width), BF16),
            ((self.width, self.keys), BF16),
            ((self.rows, self.width), BF16),
            ((self.rows, self.width), BF16),
            ((self.rows, self.lanes), BF16),
            ((self.rows, 1), F32),
        ]

    def work_scratch(self, tokens, length):
        return [
            pltpu.VMEM((self.chunks, tokens, LANES), F32),
            pltpu.VMEM((self.chunks, tokens, LANES), F32),
            pltpu.VMEM((tokens, self.width), BF16),
            pltpu.VMEM((self.rows, tokens), BF16),
            pltpu.VMEM((tokens, self.keys), BF16),
            pltpu.VMEM((self.rows, tokens), BF16),
            pltpu.VMEM((self.rows, tokens), F32),
            pltpu.VMEM((2, length, HEADS * length), F32),
            pltpu.VMEM((2, length, HEADS * length), BF16),
            pltpu.VMEM((self.rows, tokens), BF16),
        ]


def prepare(sz, weights, packed):
    proj, bias, out = weights
    wqt, wk, wvt, wgt, wo, bias_col = packed

    def window(block):
        start = block * sz.width
        low = start // LANES * LANES
        high = min(ceil_to(start + sz.width, LANES), 4 * sz.width)
        return proj[:, low:high], start - low, high - low

    def hits(shape, axis, pad, shift):
        place = lax.broadcasted_iota(jnp.int32, shape, axis)
        source = lax.broadcasted_iota(jnp.int32, shape, 1 - axis) - shift
        inner = place % pad
        return (inner < sz.head) & (source == place // pad * sz.head + inner)

    def pick(*spec):
        return jnp.where(hits(*spec), 1.0, 0.0).astype(BF16)

    part, shift, size = window(1)
    wk[...] = nn(part, pick((size, sz.keys), 1, sz.pad_key, shift)).astype(BF16)
    for block, ref, pad in ((0, wqt, sz.pad_head), (2, wvt, sz.pad_head), (3, wgt, sz.pad_head)):
        part, shift, size = window(block)
        ref[...] = nt(pick((HEADS * pad, size), 0, pad, shift), part).astype(BF16)
    spec = (sz.rows, sz.width), 0, sz.pad_head, 0
    wo[...] = jnp.zeros(wo.shape, BF16)
    wo[:, : sz.width] = nn(pick(*spec), out[...]).astype(BF16)
    row = bias[...].reshape(1, sz.width)
    bias_col[...] = jnp.sum(jnp.where(hits(*spec), row, 0.0), axis=1, keepdims=True)


def mix_lines(sz, groups, length, work):
    queries, keys, values, gates, scores, weights, gated = work[3:]
    pack = LANES // sz.pad_key
    spare = sz.pad_key - sz.pad_head
    zeros = jnp.zeros((sz.pad_key, length), BF16)

    def score(group):
        mine = slice(group * length, (group + 1) * length)
        for first in range(0, HEADS, pack):
            blocks = []
            for j in range(pack):
                low = (first + j) * sz.pad_head
                own = queries[low : low + sz.pad_head, mine]
                if spare:
                    gap = jnp.zeros((spare, length), BF16)
                    own = jnp.concatenate([own, gap], axis=0)
                blocks.append(
                    jnp.concatenate([own if i == j else zeros for i in range(pack)], axis=1)
                )
            lanes = slice(first * sz.pad_key, (first + pack) * sz.pad_key)
            scores[group % 2, :, first * length : (first + pack) * length] = nn(
                keys[mine, lanes], jnp.concatenate(blocks, axis=0)
            )

    def soften(group):
        for head in range(HEADS):
            lanes = slice(head * length, (head + 1) * length)
            s = scores[group % 2, :, lanes]
            top = jnp.max(s, axis=0, keepdims=True)
            weights[group % 2, :, lanes] = jnp.exp2(s - top).astype(BF16)

    def mix(group):
        mine = slice(group * length, (group + 1) * length)
        for head in range(HEADS):
            rows = slice(head * sz.pad_head, (head + 1) * sz.pad_head)
            lanes = slice(head * length, (head + 1) * length)
            mixed = nn(values[rows, mine], weights[group % 2, :, lanes])
            total = mixed[sz.head : sz.head + 1]
            gated[rows, mine] = (mixed * (1.0 / total) * gates[rows, mine]).astype(BF16)

    score(0)
    for group in range(groups):
        if group + 1 < groups:
            score(group + 1)
        soften(group)
        if group > 0:
            mix(group - 1)
    mix(groups - 1)


def attend(sz, groups, length, start_of, stride, per_group, gain, packed, work, emit=None):
    wqt, wk, wvt, wgt, wo, bias_col = packed
    xs, ys, normed, queries, keys, values, gates = work[:7]
    gated = work[9]
    run = length // per_group
    factor = math.log2(math.e) / sz.head**0.5
    lane = lax.broadcasted_iota(jnp.int32, (1, sz.lanes), 1)
    inside = lane < sz.width
    gain_row = gain[...].reshape(1, sz.width)

    def places(group):
        return [pl.ds(start_of(group, c), run, stride=stride) for c in range(per_group)]

    def tokens_of(group):
        parts = [
            jnp.concatenate([xs[k, place, :] for place in places(group)], axis=0)
            for k in range(sz.chunks)
        ]
        return jnp.concatenate(parts, axis=1)

    for group in range(groups):
        x = tokens_of(group)
        mean = jnp.sum(x, axis=1, keepdims=True) * (1.0 / sz.width)
        centred = jnp.where(inside, x - mean, 0.0)
        spread = jnp.sum(centred * centred, axis=1, keepdims=True) * (1.0 / sz.width)
        value = centred[:, : sz.width] * lax.rsqrt(spread + 1e-05) * gain_row
        normed[group * length : (group + 1) * length] = value.astype(BF16)
    z = normed[...]
    feature = lax.broadcasted_iota(jnp.int32, (sz.rows, 1), 0)
    ones_row = jnp.where(feature % sz.pad_head == sz.head, 1.0, 0.0)
    queries[...] = (nt(wqt[...], z) * factor).astype(BF16)
    keys[...] = nn(z, wk[...]).astype(BF16)
    values[...] = (nt(wvt[...], z) + ones_row).astype(BF16)
    gates[...] = jax.nn.sigmoid(nt(wgt[...], z) + bias_col[...])
    mix_lines(sz, groups, length, work)
    for group in range(groups):
        mine = slice(group * length, (group + 1) * length)
        y = tokens_of(group) + tn(gated[:, mine], wo[...])
        if emit is not None:
            emit(group, y)
            continue
        for k in range(sz.chunks):
            part = y[:, k * LANES : (k + 1) * LANES]
            for c, place in enumerate(places(group)):
                ys[k, place, :] = part[c * run : (c + 1) * run]


class Lines:
    def __init__(self, sz, groups, length, start_of, stride, per_group, gain, packed, work, quarters):
        self.sz, self.groups, self.length = sz, groups, length
        self.quarters = quarters
        self.gain, self.packed, self.work = gain, packed, work
        self.half = length // 2
        self.part = groups * self.half
        self.start_of, self.stride, self.per_group = start_of, stride, per_group
        self.run = self.half // 2 // per_group

    def order(self, line):
        return (0, 1) if line % 2 == 0 else (1, 0)

    def base(self, quarter):
        size = self.part // 2
        return pl.multiple_of(quarter * size, size)

    def places(self, line, part):
        return [
            pl.ds(self.base(quarter) + self.start_of(line, c), self.run, stride=self.stride)
            for quarter in self.quarters[part]
            for c in range(self.per_group)
        ]

    def gather(self, spots):
        xs = self.work[0]
        parts = [
            jnp.concatenate([xs[k, place, :] for place in spots], axis=0)
            for k in range(self.sz.chunks)
        ]
        return jnp.concatenate(parts, axis=1)

    def tile(self, index, part):
        lines = (2 * index, 2 * index + 1)
        return lines if part == 0 else lines[::-1]

    def absorb(self, part, source):
        sz, length, half = self.sz, self.length, self.half
        wqt, wk, wvt, wgt, _, bias_col = self.packed
        xs, _, normed, queries, keys, values, gates = self.work[:7]
        count = source.shape[0] // 4
        for quarter in self.quarters[part]:
            blocks = source.at[pl.ds(quarter * count, count)]
            unpack_tokens(sz, blocks, xs, self.base(quarter), self.part // 2)
        factor = math.log2(math.e) / sz.head**0.5
        inside = lax.broadcasted_iota(jnp.int32, (1, sz.lanes), 1) < sz.width
        gain_row = self.gain[...].reshape(1, sz.width)
        for index in range(self.groups // 2):
            first, second = self.tile(index, part)
            x = self.gather(self.places(first, part) + self.places(second, part))
            mean = jnp.sum(x, axis=1, keepdims=True) * (1.0 / sz.width)
            centred = jnp.where(inside, x - mean, 0.0)
            spread = jnp.sum(centred * centred, axis=1, keepdims=True) * (1.0 / sz.width)
            value = centred[:, : sz.width] * lax.rsqrt(spread + 1e-05) * gain_row
            normed[index * length : (index + 1) * length] = value.astype(BF16)
        z = normed[: self.part]
        made = nn(z, wk[...]).astype(BF16)
        for index in range(self.groups // 2):
            for place, line in enumerate(self.tile(index, part)):
                low = index * length + place * half
                spot = line * length + place * half
                keys[spot : spot + half] = made[low : low + half]
        feature = lax.broadcasted_iota(jnp.int32, (sz.rows, 1), 0)
        ones_row = jnp.where(feature % sz.pad_head == sz.head, 1.0, 0.0)
        self.settle(part, queries, (nt(wqt[...], z) * factor).astype(BF16))
        self.settle(part, values, (nt(wvt[...], z) + ones_row).astype(BF16))
        self.settle(part, gates, jax.nn.sigmoid(nt(wgt[...], z) + bias_col[...]))

    def settle(self, part, ref, value):
        length = self.length
        lane = lax.broadcasted_iota(jnp.int32, (ref.shape[0], length), 1)
        for index in range(self.groups // 2):
            new = value[:, index * length : (index + 1) * length]
            even = slice(2 * index * length, (2 * index + 1) * length)
            odd = slice((2 * index + 1) * length, (2 * index + 2) * length)
            if part == 0:
                ref[:, even] = new
                continue
            old = ref[:, even]
            ref[:, even] = jnp.where(lane < self.half, old, new)
            ref[:, odd] = jnp.where(lane < self.half, new, old)

    def finish(self, emit=None):
        sz, length, run = self.sz, self.length, self.run
        wo = self.packed[4]
        ys, gated = self.work[1], self.work[9]
        mix_lines(sz, self.groups, length, self.work)
        for line in range(self.groups):
            mine = slice(line * length, (line + 1) * length)
            spots = [place for part in self.order(line) for place in self.places(line, part)]
            y = self.gather(spots) + tn(gated[:, mine], wo[...])
            if emit is not None:
                emit(line, y, [q for part in self.order(line) for q in self.quarters[part]])
                continue
            for k in range(sz.chunks):
                piece = y[:, k * LANES : (k + 1) * LANES]
                for i, place in enumerate(spots):
                    ys[k, place, :] = piece[i * run : (i + 1) * run]


def pack_tokens(sz, ys, target):
    tokens = ys.shape[1]
    n = target.shape[0]
    block = tokens // n
    tail = target.shape[2:]
    fold = math.prod(tail) // LANES
    for k in range(sz.full):
        part = ys[k].reshape((n, block // fold) + tail)
        target[:, k * block // fold : (k + 1) * block // fold] = part.astype(BF16)
    if sz.rest:
        joined = None
        for q in range(sz.side):
            part = ys[sz.full, pl.ds(q, tokens // sz.side, stride=sz.side), :]
            part = pltpu.roll(part, q * sz.rest, 1) if q else part
            joined = part if joined is None else joined + part
        part = joined.reshape((n, block // sz.side // fold) + tail)
        target[:, sz.full * block // fold :] = part.astype(BF16)


def unpack_tokens(sz, source, xs, base=0, tokens=None):
    tokens = tokens or xs.shape[1]
    n = source.shape[0]
    block = tokens // n
    fold = math.prod(source.shape[2:]) // LANES
    for k in range(sz.full):
        part = source[:, k * block // fold : (k + 1) * block // fold]
        xs[k, pl.ds(base, tokens), :] = part.astype(F32).reshape(tokens, LANES)
    if sz.rest:
        joined = source[:, sz.full * block // fold :].astype(F32)
        joined = joined.reshape(tokens // sz.side, LANES)
        inside = lax.broadcasted_iota(jnp.int32, (1, LANES), 1) < sz.rest
        for q in range(sz.side):
            part = pltpu.roll(joined, LANES - q * sz.rest, 1) if q else joined
            place = pl.ds(base + q, tokens // sz.side, stride=sz.side)
            xs[sz.full, place, :] = jnp.where(inside, part, 0.0)


def turn_tokens(sz, n, rows, source, xs, ys):
    cols, width, length = source.shape
    for c in range(cols):
        turned = source[c].astype(F32).T
        for k in range(sz.chunks):
            part = turned[:, k * LANES : min((k + 1) * LANES, width)]
            if part.shape[1] < LANES:
                pad = jnp.zeros((length, LANES - part.shape[1]), F32)
                part = jnp.concatenate([part, pad], axis=1)
            xs[k, c * length : (c + 1) * length] = part
    for k in range(sz.chunks):
        for c in range(cols):
            for r in range(rows):
                part = xs[k, pl.ds(c * length + r, n, stride=rows), :]
                ys[k, pl.ds(r * cols + c, n, stride=rows * cols), :] = part


def row_kernel(sz, n, rows, cols, *refs):
    x_ref, gain, *own_weights = refs[:5]
    next_weights = refs[5:8]
    result, *next_packed = refs[8:15]
    sent, got, back, *rest = refs[15:]
    packed, rest = rest[:6], rest[6:]
    work = rest[:10]
    send_a, recv_a, send_b, recv_b, local_sem = rest[10:]
    me = lax.axis_index("row")
    block = rows * cols

    barrier = pltpu.get_barrier_semaphore()

    def greet(step, carry):
        peer = lax.rem(me + step, n)
        pl.semaphore_signal(barrier, inc=1, device_id={"row": peer}, device_id_type=MESH)
        return carry

    lax.fori_loop(1, n, greet, 0)
    turn_tokens(sz, n, rows, x_ref, work[0], work[1])
    pack_tokens(sz, work[1], sent)
    pl.semaphore_wait(barrier, n - 1)

    def exchange(source, target, send, recv, body):
        def copy(peer, slot):
            return pltpu.make_async_remote_copy(
                src_ref=source.at[peer],
                dst_ref=target.at[slot],
                send_sem=send.at[peer],
                recv_sem=recv.at[slot],
                device_id={"row": peer},
                device_id_type=MESH,
            )

        def start(step, carry):
            copy(lax.rem(me + step, n), me).start()
            return carry

        lax.fori_loop(1, n, start, 0)
        own = pltpu.make_async_copy(source.at[me], target.at[me], local_sem)
        own.start()
        body()
        own.wait()

        def finish(step, carry):
            peer = lax.rem(me + step, n)
            copy(peer, me).wait_send()
            copy(peer, peer).wait_recv()
            return carry

        lax.fori_loop(1, n, finish, 0)

    exchange(
        sent,
        got,
        send_a,
        recv_a,
        lambda: prepare(sz, own_weights, packed),
    )
    unpack_tokens(sz, got, work[0])
    attend(
        sz, rows, n * cols, lambda g, c: g * cols + c, block, cols, gain, packed, work
    )
    pack_tokens(sz, work[1], back)
    exchange(
        back,
        result,
        send_b,
        recv_b,
        lambda: prepare(sz, next_weights, next_packed),
    )


def col_kernel(sz, cols, x_ref, gain, *refs):
    packed, result, work = refs[:6], refs[6], refs[7:]
    unpack_tokens(sz, x_ref, work[0])
    length = work[0].shape[1] // cols

    def emit(group, y):
        result[group] = y[:, : sz.width].T.astype(BF16)

    attend(sz, cols, length, lambda g, c: g, cols, 1, gain, packed, work, emit)


def axial_kernel(sz, n, rows, cols, *refs):
    outer, result, refs = refs[:9], refs[9], refs[10:]
    local, refs = refs[:9], refs[9:]
    sent, got, back, home, *refs = refs
    packed_row, packed_col, refs = refs[:6], refs[6:12], refs[12:]
    work = refs[:10]
    load_sem, send_a, recv_a, send_b, recv_b, own_sem = refs[10:]
    x_ref, row_gain, *row_weights = local[:5]
    col_gain, *col_weights = local[5:]
    me = lax.axis_index("row")
    block = rows * cols
    length = n * cols

    def steps(low, high, body):
        def step(i, carry):
            body(i)
            return carry

        lax.fori_loop(low, high, step, 0)

    def partner(i):
        return lax.rem(me + i, n)

    barrier = pltpu.get_barrier_semaphore()

    def greet(i):
        peer = partner(i)
        pl.semaphore_signal(barrier, inc=1, device_id={"row": peer}, device_id_type=MESH)

    steps(1, n, greet)
    loads = [
        pltpu.make_async_copy(source, target, load_sem.at[i])
        for i, (source, target) in enumerate(zip(outer, local))
    ]
    for load in loads:
        load.start()

    fourth = n // 4
    layer = me // fourth

    class Exchange:
        def __init__(self, source, target, send, recv, own):
            self.source, self.target = source, target
            self.send, self.recv = send, recv
            self.own = pltpu.make_async_copy(source.at[me], target.at[me], own)

        def copy(self, peer, slot):
            return pltpu.make_async_remote_copy(
                src_ref=self.source.at[peer],
                dst_ref=self.target.at[slot],
                send_sem=self.send.at[peer],
                recv_sem=self.recv.at[slot],
                device_id={"row": peer},
                device_id_type=MESH,
            )

        def visit(self, quarter, body):
            low = 1 if quarter is layer else 0
            steps(low, fourth, lambda i: body(quarter * fourth + lax.rem(me + i, fourth)))

        def start(self, quarters=None):
            self.own.start()
            if quarters is None:
                steps(1, n, lambda i: self.copy(partner(i), me).start())
                return
            for quarter in quarters:
                self.visit(quarter, lambda peer: self.copy(peer, me).start())

        def arrive(self, quarters):
            for quarter in quarters:
                self.visit(quarter, lambda peer: self.copy(peer, peer).wait_recv())
                if quarter is layer:
                    self.own.wait()
            return self.target

        def leave(self):
            steps(1, n, lambda i: self.copy(partner(i), me).wait_send())

    def choose(*table):
        return sum(jnp.where(layer == i, value, 0) for i, value in enumerate(table))

    first = Exchange(sent, got, send_a, recv_a, own_sem.at[0])
    second = Exchange(back, home, send_b, recv_b, own_sem.at[1])
    early = ((layer, choose(1, 0, 3, 2)), (choose(2, 2, 1, 1), choose(3, 3, 0, 0)))
    late = ((layer, choose(2, 0, 0, 2)), (choose(1, 2, 1, 0), choose(3, 3, 3, 1)))
    loads[0].wait()
    turn_tokens(sz, n, rows, x_ref, work[0], work[1])
    pack_tokens(sz, work[1], sent)
    pl.semaphore_wait(barrier, n - 1)
    first.start(early[0] + early[1])
    for load in loads[1:]:
        load.wait()
    prepare(sz, row_weights, packed_row)
    prepare(sz, col_weights, packed_col)
    place = lambda g, c: g * cols + c
    lines = Lines(sz, rows, length, place, block, cols, row_gain, packed_row, work, early)
    for part in range(2):
        lines.absorb(part, first.arrive(early[part]))
    lines.finish()
    pack_tokens(sz, work[1], back)
    second.start()
    first.leave()
    height = n * rows
    place = lambda g, c: g
    lines = Lines(sz, cols, height, place, cols, 1, col_gain, packed_col, work, late)
    for part in range(2):
        lines.absorb(part, second.arrive(late[part]))
    ys = work[1]
    size = height // 4

    def emit(line, y, quarters):
        low = line * height
        for i, quarter in enumerate(quarters):
            spot = pl.multiple_of(low + quarter * size, size)
            for k in range(sz.chunks):
                piece = y[i * size : (i + 1) * size, k * LANES : (k + 1) * LANES]
                ys[k, pl.ds(spot, size), :] = piece
        y = jnp.concatenate([ys[k, low : low + height] for k in range(sz.chunks)], axis=1)
        result[line] = y[:, : sz.width].T.astype(BF16)

    lines.finish(emit)
    second.leave()


def swap_columns(sz, done, block, rows, cols):
    n = done.shape[0]
    parts = [done[:, k * block : (k + 1) * block] for k in range(sz.full)]
    if sz.rest:
        parts.append(done[:, sz.full * block :].reshape(n, block, sz.rest))
    whole = jnp.concatenate(parts, -1).reshape(rows, cols, sz.width)
    whole = lax.all_to_all(whole, "col", split_axis=1, concat_axis=0, tiled=True)
    whole = whole.reshape(n, block, sz.width)
    parts = [whole[..., k * LANES : (k + 1) * LANES] for k in range(sz.full)]
    if sz.rest:
        parts.append(whole[..., sz.full * LANES :].reshape(n, block // sz.side, LANES))
    return jnp.concatenate(parts, 1)


VMEM = pl.BlockSpec(memory_space=pltpu.VMEM)


def per_device(
    pair_map, row_gain, row_proj, row_gate_bias, row_out, col_gain, col_proj, col_gate_bias, col_out
):
    local_rows, local_cols, width = pair_map.shape
    n = lax.axis_size("row")
    sz = Sizes(width)
    rows = local_rows // n
    tokens = local_rows * local_cols
    block = rows * local_cols
    shape = (n, sz.packed_rows(block), LANES)
    turned = jnp.transpose(pair_map, (1, 2, 0))
    splits = lax.axis_size("col")
    folds = shape[1] % FOLD == 0 and block % (FOLD * sz.side) == 0
    even = rows % 2 == 0 and local_cols % 2 == 0 and n % 4 == 0
    if splits == 1 and folds and even and n * local_cols == local_rows == LANES:
        folded = (n, shape[1] // FOLD, FOLD, LANES)
        operands = (turned, row_gain, row_proj, row_gate_bias, row_out)
        operands += (col_gain, col_proj, col_gate_bias, col_out)
        operands = [pltpu.with_memory_space_constraint(a, pltpu.HBM) for a in operands]
        updated = pl.pallas_call(
            functools.partial(axial_kernel, sz, n, rows, local_cols),
            out_shape=jax.ShapeDtypeStruct(turned.shape, BF16),
            in_specs=[pl.BlockSpec(memory_space=pltpu.HBM)] * len(operands),
            out_specs=VMEM,
            scratch_shapes=[pltpu.VMEM(a.shape, a.dtype) for a in operands]
            + [pltpu.VMEM(folded, BF16)] * 4
            + [pltpu.VMEM(*spec) for spec in sz.packed_shapes()] * 2
            + sz.work_scratch(tokens, max(n * local_cols, local_rows))
            + [pltpu.SemaphoreType.DMA((len(operands),))]
            + [pltpu.SemaphoreType.DMA((n,))] * 4
            + [pltpu.SemaphoreType.DMA((2,))],
            compiler_params=pltpu.CompilerParams(
                collective_id=0, has_side_effects=True, vmem_limit_bytes=VMEM_LIMIT
            ),
            name="axial_attention",
        )(*operands)
        return jnp.transpose(updated, (2, 0, 1))
    done, *packed = pl.pallas_call(
        functools.partial(row_kernel, sz, n, rows, local_cols),
        out_shape=[jax.ShapeDtypeStruct(shape, BF16)]
        + [jax.ShapeDtypeStruct(*spec) for spec in sz.packed_shapes()],
        in_specs=[VMEM] * 8,
        out_specs=[VMEM] * 7,
        scratch_shapes=[pltpu.VMEM(shape, BF16)] * 3
        + [pltpu.VMEM(*spec) for spec in sz.packed_shapes()]
        + sz.work_scratch(tokens, n * local_cols)
        + [pltpu.SemaphoreType.DMA((n,))] * 4
        + [pltpu.SemaphoreType.DMA],
        compiler_params=pltpu.CompilerParams(collective_id=0, has_side_effects=True),
        name="row_attention",
    )(turned, row_gain, row_proj, row_gate_bias, row_out, col_proj, col_gate_bias, col_out)
    if splits > 1:
        done = swap_columns(sz, done, block, local_rows, local_cols)
    cols = local_cols // splits
    full = tokens // cols
    updated = pl.pallas_call(
        functools.partial(col_kernel, sz, cols),
        out_shape=jax.ShapeDtypeStruct((cols, width, full), BF16),
        in_specs=[VMEM] * 8,
        out_specs=VMEM,
        scratch_shapes=sz.work_scratch(tokens, full),
        name="col_attention",
    )(done, col_gain, *packed)
    updated = jnp.transpose(updated, (2, 0, 1))
    if splits > 1:
        updated = lax.all_to_all(updated, "col", split_axis=0, concat_axis=1, tiled=True)
    return updated


def solution(mesh):
    return jax.shard_map(
        per_device,
        mesh=mesh,
        in_specs=(P(("groups", "col"), "row", None), P(), P(), P(), P(), P(), P(), P(), P()),
        out_specs=P(("groups", "col"), "row", None),
        check_vma=False,
    )
```

```python
import functools
import math

import jax
import jax.numpy as jnp
from jax import lax
from jax.experimental import pallas as pl
from jax.experimental.pallas import tpu as pltpu
from jax.sharding import PartitionSpec as P

HEADS = 8
LANES = 128
FOLD = 4
VMEM_LIMIT = 32 * 2**20
F32 = jnp.float32
BF16 = jnp.bfloat16
MESH = pl.DeviceIdType.MESH


def ceil_to(value, step):
    return -(-value // step) * step


def nt(a, b):
    return lax.dot_general(a, b, (((1,), (1,)), ((), ())), preferred_element_type=F32)


def tn(a, b):
    return lax.dot_general(a, b, (((0,), (0,)), ((), ())), preferred_element_type=F32)


def nn(a, b):
    return jnp.dot(a, b, preferred_element_type=F32)


class Sizes:
    def __init__(self, width):
        self.width = width
        self.head = width // HEADS
        self.pad_head = ceil_to(self.head + 1, 16)
        self.pad_key = LANES // (LANES // self.head)
        while LANES % self.pad_key:
            self.pad_key += 1
        self.rows = HEADS * self.pad_head
        self.keys = HEADS * self.pad_key
        assert self.pad_head <= self.pad_key
        self.lanes = ceil_to(width, LANES)
        self.chunks = self.lanes // LANES
        self.full = width // LANES
        self.rest = width % LANES
        self.side = LANES // self.rest if self.rest else 1

    def packed_rows(self, block):
        assert self.rest == 0 or (LANES % self.rest == 0 and block % self.side == 0)
        return self.full * block + (block // self.side if self.rest else 0)

    def packed_shapes(self):
        return [
            ((self.rows, self.width), BF16),
            ((self.width, self.keys), BF16),
            ((self.rows, self.width), BF16),
            ((self.rows, self.width), BF16),
            ((self.rows, self.lanes), BF16),
            ((self.rows, 1), F32),
        ]

    def work_scratch(self, tokens, length):
        return [
            pltpu.VMEM((self.chunks, tokens, LANES), F32),
            pltpu.VMEM((self.chunks, tokens, LANES), F32),
            pltpu.VMEM((tokens, self.width), BF16),
            pltpu.VMEM((self.rows, tokens), BF16),
            pltpu.VMEM((tokens, self.keys), BF16),
            pltpu.VMEM((self.rows, tokens), BF16),
            pltpu.VMEM((self.rows, tokens), F32),
            pltpu.VMEM((2, length, HEADS * length), F32),
            pltpu.VMEM((2, length, HEADS * length), BF16),
            pltpu.VMEM((self.rows, tokens), BF16),
        ]


def prepare(sz, weights, packed):
    proj, bias, out = weights
    wqt, wk, wvt, wgt, wo, bias_col = packed

    def window(block):
        start = block * sz.width
        low = start // LANES * LANES
        high = min(ceil_to(start + sz.width, LANES), 4 * sz.width)
        return proj[:, low:high], start - low, high - low

    def hits(shape, axis, pad, shift):
        place = lax.broadcasted_iota(jnp.int32, shape, axis)
        source = lax.broadcasted_iota(jnp.int32, shape, 1 - axis) - shift
        inner = place % pad
        return (inner < sz.head) & (source == place // pad * sz.head + inner)

    def pick(*spec):
        return jnp.where(hits(*spec), 1.0, 0.0).astype(BF16)

    part, shift, size = window(1)
    wk[...] = nn(part, pick((size, sz.keys), 1, sz.pad_key, shift)).astype(BF16)
    for block, ref, pad in ((0, wqt, sz.pad_head), (2, wvt, sz.pad_head), (3, wgt, sz.pad_head)):
        part, shift, size = window(block)
        ref[...] = nt(pick((HEADS * pad, size), 0, pad, shift), part).astype(BF16)
    spec = (sz.rows, sz.width), 0, sz.pad_head, 0
    wo[...] = jnp.zeros(wo.shape, BF16)
    wo[:, : sz.width] = nn(pick(*spec), out[...]).astype(BF16)
    row = bias[...].reshape(1, sz.width)
    bias_col[...] = jnp.sum(jnp.where(hits(*spec), row, 0.0), axis=1, keepdims=True)


def mix_lines(sz, groups, length, work):
    queries, keys, values, gates, scores, weights, gated = work[3:]
    pack = LANES // sz.pad_key
    spare = sz.pad_key - sz.pad_head
    zeros = jnp.zeros((sz.pad_key, length), BF16)

    def score(group):
        mine = slice(group * length, (group + 1) * length)
        for first in range(0, HEADS, pack):
            blocks = []
            for j in range(pack):
                low = (first + j) * sz.pad_head
                own = queries[low : low + sz.pad_head, mine]
                if spare:
                    gap = jnp.zeros((spare, length), BF16)
                    own = jnp.concatenate([own, gap], axis=0)
                blocks.append(
                    jnp.concatenate([own if i == j else zeros for i in range(pack)], axis=1)
                )
            lanes = slice(first * sz.pad_key, (first + pack) * sz.pad_key)
            scores[group % 2, :, first * length : (first + pack) * length] = nn(
                keys[mine, lanes], jnp.concatenate(blocks, axis=0)
            )

    def soften(group):
        for head in range(HEADS):
            lanes = slice(head * length, (head + 1) * length)
            s = scores[group % 2, :, lanes]
            top = jnp.max(s, axis=0, keepdims=True)
            weights[group % 2, :, lanes] = jnp.exp2(s - top).astype(BF16)

    def mix(group):
        mine = slice(group * length, (group + 1) * length)
        for head in range(HEADS):
            rows = slice(head * sz.pad_head, (head + 1) * sz.pad_head)
            lanes = slice(head * length, (head + 1) * length)
            mixed = nn(values[rows, mine], weights[group % 2, :, lanes])
            total = mixed[sz.head : sz.head + 1]
            gated[rows, mine] = (mixed * (1.0 / total) * gates[rows, mine]).astype(BF16)

    score(0)
    for group in range(groups):
        if group + 1 < groups:
            score(group + 1)
        soften(group)
        if group > 0:
            mix(group - 1)
    mix(groups - 1)


def attend(sz, groups, length, start_of, stride, per_group, gain, packed, work, emit=None):
    wqt, wk, wvt, wgt, wo, bias_col = packed
    xs, ys, normed, queries, keys, values, gates = work[:7]
    gated = work[9]
    run = length // per_group
    factor = math.log2(math.e) / sz.head**0.5
    lane = lax.broadcasted_iota(jnp.int32, (1, sz.lanes), 1)
    inside = lane < sz.width
    gain_row = gain[...].reshape(1, sz.width)

    def places(group):
        return [pl.ds(start_of(group, c), run, stride=stride) for c in range(per_group)]

    def tokens_of(group):
        parts = [
            jnp.concatenate([xs[k, place, :] for place in places(group)], axis=0)
            for k in range(sz.chunks)
        ]
        return jnp.concatenate(parts, axis=1)

    for group in range(groups):
        x = tokens_of(group)
        mean = jnp.sum(x, axis=1, keepdims=True) * (1.0 / sz.width)
        centred = jnp.where(inside, x - mean, 0.0)
        spread = jnp.sum(centred * centred, axis=1, keepdims=True) * (1.0 / sz.width)
        value = centred[:, : sz.width] * lax.rsqrt(spread + 1e-05) * gain_row
        normed[group * length : (group + 1) * length] = value.astype(BF16)
    z = normed[...]
    feature = lax.broadcasted_iota(jnp.int32, (sz.rows, 1), 0)
    ones_row = jnp.where(feature % sz.pad_head == sz.head, 1.0, 0.0)
    queries[...] = (nt(wqt[...], z) * factor).astype(BF16)
    keys[...] = nn(z, wk[...]).astype(BF16)
    values[...] = (nt(wvt[...], z) + ones_row).astype(BF16)
    gates[...] = jax.nn.sigmoid(nt(wgt[...], z) + bias_col[...])
    mix_lines(sz, groups, length, work)
    for group in range(groups):
        mine = slice(group * length, (group + 1) * length)
        y = tokens_of(group) + tn(gated[:, mine], wo[...])
        if emit is not None:
            emit(group, y)
            continue
        for k in range(sz.chunks):
            part = y[:, k * LANES : (k + 1) * LANES]
            for c, place in enumerate(places(group)):
                ys[k, place, :] = part[c * run : (c + 1) * run]


class Lines:
    def __init__(self, sz, groups, length, start_of, stride, per_group, gain, packed, work, quarters):
        self.sz, self.groups, self.length = sz, groups, length
        self.quarters = quarters
        self.gain, self.packed, self.work = gain, packed, work
        self.half = length // 2
        self.part = groups * self.half
        self.start_of, self.stride, self.per_group = start_of, stride, per_group
        self.run = self.half // 2 // per_group

    def order(self, line):
        return (0, 1) if line % 2 == 0 else (1, 0)

    def base(self, quarter):
        size = self.part // 2
        return pl.multiple_of(quarter * size, size)

    def places(self, line, part):
        return [
            pl.ds(self.base(quarter) + self.start_of(line, c), self.run, stride=self.stride)
            for quarter in self.quarters[part]
            for c in range(self.per_group)
        ]

    def gather(self, spots):
        xs = self.work[0]
        parts = [
            jnp.concatenate([xs[k, place, :] for place in spots], axis=0)
            for k in range(self.sz.chunks)
        ]
        return jnp.concatenate(parts, axis=1)

    def tile(self, index, part):
        lines = (2 * index, 2 * index + 1)
        return lines if part == 0 else lines[::-1]

    def absorb(self, part, source):
        sz, length, half = self.sz, self.length, self.half
        wqt, wk, wvt, wgt, _, bias_col = self.packed
        xs, _, normed, queries, keys, values, gates = self.work[:7]
        count = source.shape[0] // 4
        for quarter in self.quarters[part]:
            blocks = source.at[pl.ds(quarter * count, count)]
            unpack_tokens(sz, blocks, xs, self.base(quarter), self.part // 2)
        factor = math.log2(math.e) / sz.head**0.5
        inside = lax.broadcasted_iota(jnp.int32, (1, sz.lanes), 1) < sz.width
        gain_row = self.gain[...].reshape(1, sz.width)
        for index in range(self.groups // 2):
            first, second = self.tile(index, part)
            x = self.gather(self.places(first, part) + self.places(second, part))
            mean = jnp.sum(x, axis=1, keepdims=True) * (1.0 / sz.width)
            centred = jnp.where(inside, x - mean, 0.0)
            spread = jnp.sum(centred * centred, axis=1, keepdims=True) * (1.0 / sz.width)
            value = centred[:, : sz.width] * lax.rsqrt(spread + 1e-05) * gain_row
            normed[index * length : (index + 1) * length] = value.astype(BF16)
        z = normed[: self.part]
        made = nn(z, wk[...]).astype(BF16)
        for index in range(self.groups // 2):
            for place, line in enumerate(self.tile(index, part)):
                low = index * length + place * half
                spot = line * length + place * half
                keys[spot : spot + half] = made[low : low + half]
        feature = lax.broadcasted_iota(jnp.int32, (sz.rows, 1), 0)
        ones_row = jnp.where(feature % sz.pad_head == sz.head, 1.0, 0.0)
        self.settle(part, queries, (nt(wqt[...], z) * factor).astype(BF16))
        self.settle(part, values, (nt(wvt[...], z) + ones_row).astype(BF16))
        self.settle(part, gates, jax.nn.sigmoid(nt(wgt[...], z) + bias_col[...]))

    def settle(self, part, ref, value):
        length = self.length
        lane = lax.broadcasted_iota(jnp.int32, (ref.shape[0], length), 1)
        for index in range(self.groups // 2):
            new = value[:, index * length : (index + 1) * length]
            even = slice(2 * index * length, (2 * index + 1) * length)
            odd = slice((2 * index + 1) * length, (2 * index + 2) * length)
            if part == 0:
                ref[:, even] = new
                continue
            old = ref[:, even]
            ref[:, even] = jnp.where(lane < self.half, old, new)
            ref[:, odd] = jnp.where(lane < self.half, new, old)

    def finish(self, emit=None):
        sz, length, run = self.sz, self.length, self.run
        wo = self.packed[4]
        ys, gated = self.work[1], self.work[9]
        mix_lines(sz, self.groups, length, self.work)
        for line in range(self.groups):
            mine = slice(line * length, (line + 1) * length)
            spots = [place for part in self.order(line) for place in self.places(line, part)]
            y = self.gather(spots) + tn(gated[:, mine], wo[...])
            if emit is not None:
                emit(line, y, [q for part in self.order(line) for q in self.quarters[part]])
                continue
            for k in range(sz.chunks):
                piece = y[:, k * LANES : (k + 1) * LANES]
                for i, place in enumerate(spots):
                    ys[k, place, :] = piece[i * run : (i + 1) * run]


def pack_tokens(sz, ys, target):
    tokens = ys.shape[1]
    n = target.shape[0]
    block = tokens // n
    tail = target.shape[2:]
    fold = math.prod(tail) // LANES
    for k in range(sz.full):
        part = ys[k].reshape((n, block // fold) + tail)
        target[:, k * block // fold : (k + 1) * block // fold] = part.astype(BF16)
    if sz.rest:
        joined = None
        for q in range(sz.side):
            part = ys[sz.full, pl.ds(q, tokens // sz.side, stride=sz.side), :]
            part = pltpu.roll(part, q * sz.rest, 1) if q else part
            joined = part if joined is None else joined + part
        part = joined.reshape((n, block // sz.side // fold) + tail)
        target[:, sz.full * block // fold :] = part.astype(BF16)


def unpack_tokens(sz, source, xs, base=0, tokens=None):
    tokens = tokens or xs.shape[1]
    n = source.shape[0]
    block = tokens // n
    fold = math.prod(source.shape[2:]) // LANES
    for k in range(sz.full):
        part = source[:, k * block // fold : (k + 1) * block // fold]
        xs[k, pl.ds(base, tokens), :] = part.astype(F32).reshape(tokens, LANES)
    if sz.rest:
        joined = source[:, sz.full * block // fold :].astype(F32)
        joined = joined.reshape(tokens // sz.side, LANES)
        inside = lax.broadcasted_iota(jnp.int32, (1, LANES), 1) < sz.rest
        for q in range(sz.side):
            part = pltpu.roll(joined, LANES - q * sz.rest, 1) if q else joined
            place = pl.ds(base + q, tokens // sz.side, stride=sz.side)
            xs[sz.full, place, :] = jnp.where(inside, part, 0.0)


def turn_tokens(sz, n, rows, source, xs, ys):
    cols, width, length = source.shape
    for c in range(cols):
        turned = source[c].astype(F32).T
        for k in range(sz.chunks):
            part = turned[:, k * LANES : min((k + 1) * LANES, width)]
            if part.shape[1] < LANES:
                pad = jnp.zeros((length, LANES - part.shape[1]), F32)
                part = jnp.concatenate([part, pad], axis=1)
            xs[k, c * length : (c + 1) * length] = part
    for k in range(sz.chunks):
        for c in range(cols):
            for r in range(rows):
                part = xs[k, pl.ds(c * length + r, n, stride=rows), :]
                ys[k, pl.ds(r * cols + c, n, stride=rows * cols), :] = part


def row_kernel(sz, n, rows, cols, *refs):
    x_ref, gain, *own_weights = refs[:5]
    next_weights = refs[5:8]
    result, *next_packed = refs[8:15]
    sent, got, back, *rest = refs[15:]
    packed, rest = rest[:6], rest[6:]
    work = rest[:10]
    send_a, recv_a, send_b, recv_b, local_sem = rest[10:]
    me = lax.axis_index("row")
    block = rows * cols

    barrier = pltpu.get_barrier_semaphore()

    def greet(step, carry):
        peer = lax.rem(me + step, n)
        pl.semaphore_signal(barrier, inc=1, device_id={"row": peer}, device_id_type=MESH)
        return carry

    lax.fori_loop(1, n, greet, 0)
    turn_tokens(sz, n, rows, x_ref, work[0], work[1])
    pack_tokens(sz, work[1], sent)
    pl.semaphore_wait(barrier, n - 1)

    def exchange(source, target, send, recv, body):
        def copy(peer, slot):
            return pltpu.make_async_remote_copy(
                src_ref=source.at[peer],
                dst_ref=target.at[slot],
                send_sem=send.at[peer],
                recv_sem=recv.at[slot],
                device_id={"row": peer},
                device_id_type=MESH,
            )

        def start(step, carry):
            copy(lax.rem(me + step, n), me).start()
            return carry

        lax.fori_loop(1, n, start, 0)
        own = pltpu.make_async_copy(source.at[me], target.at[me], local_sem)
        own.start()
        body()
        own.wait()

        def finish(step, carry):
            peer = lax.rem(me + step, n)
            copy(peer, me).wait_send()
            copy(peer, peer).wait_recv()
            return carry

        lax.fori_loop(1, n, finish, 0)

    exchange(
        sent,
        got,
        send_a,
        recv_a,
        lambda: prepare(sz, own_weights, packed),
    )
    unpack_tokens(sz, got, work[0])
    attend(
        sz, rows, n * cols, lambda g, c: g * cols + c, block, cols, gain, packed, work
    )
    pack_tokens(sz, work[1], back)
    exchange(
        back,
        result,
        send_b,
        recv_b,
        lambda: prepare(sz, next_weights, next_packed),
    )


def col_kernel(sz, cols, x_ref, gain, *refs):
    packed, result, work = refs[:6], refs[6], refs[7:]
    unpack_tokens(sz, x_ref, work[0])
    length = work[0].shape[1] // cols

    def emit(group, y):
        result[group] = y[:, : sz.width].T.astype(BF16)

    attend(sz, cols, length, lambda g, c: g, cols, 1, gain, packed, work, emit)


def axial_kernel(sz, n, rows, cols, *refs):
    outer, result, refs = refs[:9], refs[9], refs[10:]
    local, refs = refs[:9], refs[9:]
    sent, got, back, home, *refs = refs
    packed_row, packed_col, refs = refs[:6], refs[6:12], refs[12:]
    work = refs[:10]
    load_sem, send_a, recv_a, send_b, recv_b = refs[10:]
    x_ref, row_gain, *row_weights = local[:5]
    col_gain, *col_weights = local[5:]
    me = lax.axis_index("row")
    block = rows * cols
    length = n * cols

    def steps(low, high, body):
        def step(i, carry):
            body(i)
            return carry

        lax.fori_loop(low, high, step, 0)

    def partner(i):
        return lax.rem(me + i, n)

    barrier = pltpu.get_barrier_semaphore()

    def greet(i):
        peer = partner(i)
        pl.semaphore_signal(barrier, inc=1, device_id={"row": peer}, device_id_type=MESH)

    steps(1, n, greet)
    loads = [
        pltpu.make_async_copy(source, target, load_sem.at[i])
        for i, (source, target) in enumerate(zip(outer, local))
    ]
    for load in loads:
        load.start()

    fourth = n // 4
    layer = me // fourth

    class Exchange:
        def __init__(self, source, target, send, recv):
            self.source, self.target = source, target
            self.send, self.recv = send, recv
            self.own = pltpu.make_async_copy(source.at[me], target.at[me], recv.at[layer])

        def copy(self, peer):
            return pltpu.make_async_remote_copy(
                src_ref=self.source.at[peer],
                dst_ref=self.target.at[me],
                send_sem=self.send,
                recv_sem=self.recv.at[layer],
                device_id={"row": peer},
                device_id_type=MESH,
            )

        def visit(self, quarter, body):
            low = 1 if quarter is layer else 0
            steps(low, fourth, lambda i: body(quarter * fourth + lax.rem(me + i, fourth)))

        def start(self, quarters=None):
            self.own.start()
            if quarters is None:
                steps(1, n, lambda i: self.copy(partner(i)).start())
                return
            for quarter in quarters:
                self.visit(quarter, lambda peer: self.copy(peer).start())

        def arrive(self, quarters):
            for quarter in quarters:
                blocks = self.target.at[pl.ds(quarter * fourth, fourth)]
                pltpu.make_async_copy(blocks, blocks, self.recv.at[quarter]).wait()
            return self.target

        def leave(self):
            blocks = self.source.at[: n - 1]
            pltpu.make_async_copy(blocks, blocks, self.send).wait()

    def choose(*table):
        return sum(jnp.where(layer == i, value, 0) for i, value in enumerate(table))

    first = Exchange(sent, got, send_a, recv_a)
    second = Exchange(back, home, send_b, recv_b)
    early = ((layer, choose(1, 0, 3, 2)), (choose(2, 2, 1, 1), choose(3, 3, 0, 0)))
    late = ((layer, choose(2, 0, 0, 2)), (choose(1, 2, 1, 0), choose(3, 3, 3, 1)))
    loads[0].wait()
    turn_tokens(sz, n, rows, x_ref, work[0], work[1])
    pack_tokens(sz, work[1], sent)
    pl.semaphore_wait(barrier, n - 1)
    first.start(early[0] + early[1])
    for load in loads[1:]:
        load.wait()
    prepare(sz, row_weights, packed_row)
    prepare(sz, col_weights, packed_col)
    place = lambda g, c: g * cols + c
    lines = Lines(sz, rows, length, place, block, cols, row_gain, packed_row, work, early)
    for part in range(2):
        lines.absorb(part, first.arrive(early[part]))
    lines.finish()
    pack_tokens(sz, work[1], back)
    second.start()
    first.leave()
    height = n * rows
    place = lambda g, c: g
    lines = Lines(sz, cols, height, place, cols, 1, col_gain, packed_col, work, late)
    for part in range(2):
        lines.absorb(part, second.arrive(late[part]))
    ys = work[1]
    size = height // 4

    def emit(line, y, quarters):
        low = line * height
        for i, quarter in enumerate(quarters):
            spot = pl.multiple_of(low + quarter * size, size)
            for k in range(sz.chunks):
                piece = y[i * size : (i + 1) * size, k * LANES : (k + 1) * LANES]
                ys[k, pl.ds(spot, size), :] = piece
        y = jnp.concatenate([ys[k, low : low + height] for k in range(sz.chunks)], axis=1)
        result[line] = y[:, : sz.width].T.astype(BF16)

    lines.finish(emit)
    second.leave()


def swap_columns(sz, done, block, rows, cols):
    n = done.shape[0]
    parts = [done[:, k * block : (k + 1) * block] for k in range(sz.full)]
    if sz.rest:
        parts.append(done[:, sz.full * block :].reshape(n, block, sz.rest))
    whole = jnp.concatenate(parts, -1).reshape(rows, cols, sz.width)
    whole = lax.all_to_all(whole, "col", split_axis=1, concat_axis=0, tiled=True)
    whole = whole.reshape(n, block, sz.width)
    parts = [whole[..., k * LANES : (k + 1) * LANES] for k in range(sz.full)]
    if sz.rest:
        parts.append(whole[..., sz.full * LANES :].reshape(n, block // sz.side, LANES))
    return jnp.concatenate(parts, 1)


VMEM = pl.BlockSpec(memory_space=pltpu.VMEM)


def per_device(
    pair_map, row_gain, row_proj, row_gate_bias, row_out, col_gain, col_proj, col_gate_bias, col_out
):
    local_rows, local_cols, width = pair_map.shape
    n = lax.axis_size("row")
    sz = Sizes(width)
    rows = local_rows // n
    tokens = local_rows * local_cols
    block = rows * local_cols
    shape = (n, sz.packed_rows(block), LANES)
    turned = jnp.transpose(pair_map, (1, 2, 0))
    splits = lax.axis_size("col")
    folds = shape[1] % FOLD == 0 and block % (FOLD * sz.side) == 0
    even = rows % 2 == 0 and local_cols % 2 == 0 and n % 4 == 0
    if splits == 1 and folds and even and n * local_cols == local_rows == LANES:
        folded = (n, shape[1] // FOLD, FOLD, LANES)
        operands = (turned, row_gain, row_proj, row_gate_bias, row_out)
        operands += (col_gain, col_proj, col_gate_bias, col_out)
        operands = [pltpu.with_memory_space_constraint(a, pltpu.HBM) for a in operands]
        updated = pl.pallas_call(
            functools.partial(axial_kernel, sz, n, rows, local_cols),
            out_shape=jax.ShapeDtypeStruct(turned.shape, BF16),
            in_specs=[pl.BlockSpec(memory_space=pltpu.HBM)] * len(operands),
            out_specs=VMEM,
            scratch_shapes=[pltpu.VMEM(a.shape, a.dtype) for a in operands]
            + [pltpu.VMEM(folded, BF16)] * 4
            + [pltpu.VMEM(*spec) for spec in sz.packed_shapes()] * 2
            + sz.work_scratch(tokens, max(n * local_cols, local_rows))
            + [pltpu.SemaphoreType.DMA((len(operands),))]
            + [pltpu.SemaphoreType.DMA, pltpu.SemaphoreType.DMA((4,))] * 2,
            compiler_params=pltpu.CompilerParams(
                collective_id=0, has_side_effects=True, vmem_limit_bytes=VMEM_LIMIT
            ),
            name="axial_attention",
        )(*operands)
        return jnp.transpose(updated, (2, 0, 1))
    done, *packed = pl.pallas_call(
        functools.partial(row_kernel, sz, n, rows, local_cols),
        out_shape=[jax.ShapeDtypeStruct(shape, BF16)]
        + [jax.ShapeDtypeStruct(*spec) for spec in sz.packed_shapes()],
        in_specs=[VMEM] * 8,
        out_specs=[VMEM] * 7,
        scratch_shapes=[pltpu.VMEM(shape, BF16)] * 3
        + [pltpu.VMEM(*spec) for spec in sz.packed_shapes()]
        + sz.work_scratch(tokens, n * local_cols)
        + [pltpu.SemaphoreType.DMA((n,))] * 4
        + [pltpu.SemaphoreType.DMA],
        compiler_params=pltpu.CompilerParams(collective_id=0, has_side_effects=True),
        name="row_attention",
    )(turned, row_gain, row_proj, row_gate_bias, row_out, col_proj, col_gate_bias, col_out)
    if splits > 1:
        done = swap_columns(sz, done, block, local_rows, local_cols)
    cols = local_cols // splits
    full = tokens // cols
    updated = pl.pallas_call(
        functools.partial(col_kernel, sz, cols),
        out_shape=jax.ShapeDtypeStruct((cols, width, full), BF16),
        in_specs=[VMEM] * 8,
        out_specs=VMEM,
        scratch_shapes=sz.work_scratch(tokens, full),
        name="col_attention",
    )(done, col_gain, *packed)
    updated = jnp.transpose(updated, (2, 0, 1))
    if splits > 1:
        updated = lax.all_to_all(updated, "col", split_axis=0, concat_axis=1, tiled=True)
    return updated


def solution(mesh):
    return jax.shard_map(
        per_device,
        mesh=mesh,
        in_specs=(P(("groups", "col"), "row", None), P(), P(), P(), P(), P(), P(), P(), P()),
        out_specs=P(("groups", "col"), "row", None),
        check_vma=False,
    )
```

```python
import functools
import math

import jax
import jax.numpy as jnp
from jax import lax
from jax.experimental import pallas as pl
from jax.experimental.pallas import tpu as pltpu
from jax.sharding import PartitionSpec as P

HEADS = 8
LANES = 128
FOLD = 4
VMEM_LIMIT = 32 * 2**20
F32 = jnp.float32
BF16 = jnp.bfloat16
MESH = pl.DeviceIdType.MESH


def ceil_to(value, step):
    return -(-value // step) * step


def nt(a, b):
    return lax.dot_general(a, b, (((1,), (1,)), ((), ())), preferred_element_type=F32)


def tn(a, b):
    return lax.dot_general(a, b, (((0,), (0,)), ((), ())), preferred_element_type=F32)


def nn(a, b):
    return jnp.dot(a, b, preferred_element_type=F32)


class Sizes:
    def __init__(self, width):
        self.width = width
        self.head = width // HEADS
        self.pad_head = ceil_to(self.head + 1, 16)
        self.pad_key = LANES // (LANES // self.head)
        while LANES % self.pad_key:
            self.pad_key += 1
        self.rows = HEADS * self.pad_head
        self.keys = HEADS * self.pad_key
        assert self.pad_head <= self.pad_key
        self.lanes = ceil_to(width, LANES)
        self.chunks = self.lanes // LANES
        self.full = width // LANES
        self.rest = width % LANES
        self.side = LANES // self.rest if self.rest else 1

    def packed_rows(self, block):
        assert self.rest == 0 or (LANES % self.rest == 0 and block % self.side == 0)
        return self.full * block + (block // self.side if self.rest else 0)

    def packed_shapes(self):
        return [
            ((self.rows, self.width), BF16),
            ((self.width, self.keys), BF16),
            ((self.rows, self.width), BF16),
            ((self.rows, self.width), BF16),
            ((self.rows, self.lanes), BF16),
            ((self.rows, 1), F32),
        ]

    def work_scratch(self, tokens, length):
        return [
            pltpu.VMEM((self.chunks, tokens, LANES), F32),
            pltpu.VMEM((self.chunks, tokens, LANES), F32),
            pltpu.VMEM((tokens, self.width), BF16),
            pltpu.VMEM((self.rows, tokens), BF16),
            pltpu.VMEM((tokens, self.keys), BF16),
            pltpu.VMEM((self.rows, tokens), BF16),
            pltpu.VMEM((self.rows, tokens), F32),
            pltpu.VMEM((2, length, HEADS * length), F32),
            pltpu.VMEM((2, length, HEADS * length), BF16),
            pltpu.VMEM((self.rows, tokens), BF16),
        ]


def prepare(sz, weights, packed):
    proj, bias, out = weights
    wqt, wk, wvt, wgt, wo, bias_col = packed

    def window(block):
        start = block * sz.width
        low = start // LANES * LANES
        high = min(ceil_to(start + sz.width, LANES), 4 * sz.width)
        return proj[:, low:high], start - low, high - low

    def hits(shape, axis, pad, shift):
        place = lax.broadcasted_iota(jnp.int32, shape, axis)
        source = lax.broadcasted_iota(jnp.int32, shape, 1 - axis) - shift
        inner = place % pad
        return (inner < sz.head) & (source == place // pad * sz.head + inner)

    def pick(*spec):
        return jnp.where(hits(*spec), 1.0, 0.0).astype(BF16)

    part, shift, size = window(1)
    wk[...] = nn(part, pick((size, sz.keys), 1, sz.pad_key, shift)).astype(BF16)
    for block, ref, pad in ((0, wqt, sz.pad_head), (2, wvt, sz.pad_head), (3, wgt, sz.pad_head)):
        part, shift, size = window(block)
        ref[...] = nt(pick((HEADS * pad, size), 0, pad, shift), part).astype(BF16)
    spec = (sz.rows, sz.width), 0, sz.pad_head, 0
    wo[...] = jnp.zeros(wo.shape, BF16)
    wo[:, : sz.width] = nn(pick(*spec), out[...]).astype(BF16)
    row = bias[...].reshape(1, sz.width)
    bias_col[...] = jnp.sum(jnp.where(hits(*spec), row, 0.0), axis=1, keepdims=True)


def mix_lines(sz, groups, length, work):
    queries, keys, values, gates, scores, weights, gated = work[3:]
    pack = LANES // sz.pad_key
    spare = sz.pad_key - sz.pad_head
    zeros = jnp.zeros((sz.pad_key, length), BF16)

    def score(group):
        mine = slice(group * length, (group + 1) * length)
        for first in range(0, HEADS, pack):
            blocks = []
            for j in range(pack):
                low = (first + j) * sz.pad_head
                own = queries[low : low + sz.pad_head, mine]
                if spare:
                    gap = jnp.zeros((spare, length), BF16)
                    own = jnp.concatenate([own, gap], axis=0)
                blocks.append(
                    jnp.concatenate([own if i == j else zeros for i in range(pack)], axis=1)
                )
            lanes = slice(first * sz.pad_key, (first + pack) * sz.pad_key)
            scores[group % 2, :, first * length : (first + pack) * length] = nn(
                keys[mine, lanes], jnp.concatenate(blocks, axis=0)
            )

    def soften(group):
        for head in range(HEADS):
            lanes = slice(head * length, (head + 1) * length)
            s = scores[group % 2, :, lanes]
            top = jnp.max(s, axis=0, keepdims=True)
            weights[group % 2, :, lanes] = jnp.exp2(s - top).astype(BF16)

    def mix(group):
        mine = slice(group * length, (group + 1) * length)
        for head in range(HEADS):
            rows = slice(head * sz.pad_head, (head + 1) * sz.pad_head)
            lanes = slice(head * length, (head + 1) * length)
            mixed = nn(values[rows, mine], weights[group % 2, :, lanes])
            total = mixed[sz.head : sz.head + 1]
            gated[rows, mine] = (mixed * (1.0 / total) * gates[rows, mine]).astype(BF16)

    score(0)
    for group in range(groups):
        if group + 1 < groups:
            score(group + 1)
        soften(group)
        if group > 0:
            mix(group - 1)
    mix(groups - 1)


def attend(sz, groups, length, start_of, stride, per_group, gain, packed, work, emit=None):
    wqt, wk, wvt, wgt, wo, bias_col = packed
    xs, ys, normed, queries, keys, values, gates = work[:7]
    gated = work[9]
    run = length // per_group
    factor = math.log2(math.e) / sz.head**0.5
    lane = lax.broadcasted_iota(jnp.int32, (1, sz.lanes), 1)
    inside = lane < sz.width
    gain_row = gain[...].reshape(1, sz.width)

    def places(group):
        return [pl.ds(start_of(group, c), run, stride=stride) for c in range(per_group)]

    def tokens_of(group):
        parts = [
            jnp.concatenate([xs[k, place, :] for place in places(group)], axis=0)
            for k in range(sz.chunks)
        ]
        return jnp.concatenate(parts, axis=1)

    for group in range(groups):
        x = tokens_of(group)
        mean = jnp.sum(x, axis=1, keepdims=True) * (1.0 / sz.width)
        centred = jnp.where(inside, x - mean, 0.0)
        spread = jnp.sum(centred * centred, axis=1, keepdims=True) * (1.0 / sz.width)
        value = centred[:, : sz.width] * lax.rsqrt(spread + 1e-05) * gain_row
        normed[group * length : (group + 1) * length] = value.astype(BF16)
    z = normed[...]
    feature = lax.broadcasted_iota(jnp.int32, (sz.rows, 1), 0)
    ones_row = jnp.where(feature % sz.pad_head == sz.head, 1.0, 0.0)
    queries[...] = (nt(wqt[...], z) * factor).astype(BF16)
    keys[...] = nn(z, wk[...]).astype(BF16)
    values[...] = (nt(wvt[...], z) + ones_row).astype(BF16)
    gates[...] = jax.nn.sigmoid(nt(wgt[...], z) + bias_col[...])
    mix_lines(sz, groups, length, work)
    for group in range(groups):
        mine = slice(group * length, (group + 1) * length)
        y = tokens_of(group) + tn(gated[:, mine], wo[...])
        if emit is not None:
            emit(group, y)
            continue
        for k in range(sz.chunks):
            part = y[:, k * LANES : (k + 1) * LANES]
            for c, place in enumerate(places(group)):
                ys[k, place, :] = part[c * run : (c + 1) * run]


class Lines:
    def __init__(self, sz, groups, length, start_of, stride, per_group, gain, packed, work, quarters):
        self.sz, self.groups, self.length = sz, groups, length
        self.quarters = quarters
        self.gain, self.packed, self.work = gain, packed, work
        self.half = length // 2
        self.part = groups * self.half
        self.start_of, self.stride, self.per_group = start_of, stride, per_group
        self.run = self.half // 2 // per_group

    def order(self, line):
        return (0, 1) if line % 2 == 0 else (1, 0)

    def base(self, quarter):
        size = self.part // 2
        return pl.multiple_of(quarter * size, size)

    def spots(self, line, quarter):
        return [
            pl.ds(self.base(quarter) + self.start_of(line, c), self.run, stride=self.stride)
            for c in range(self.per_group)
        ]

    def places(self, line, part):
        return [p for quarter in self.quarters[part] for p in self.spots(line, quarter)]

    def gather(self, spots):
        xs = self.work[0]
        parts = [
            jnp.concatenate([xs[k, place, :] for place in spots], axis=0)
            for k in range(self.sz.chunks)
        ]
        return jnp.concatenate(parts, axis=1)

    def tile(self, index, part):
        lines = (2 * index, 2 * index + 1)
        return lines if part == 0 else lines[::-1]

    def absorb(self, part, source, arrive):
        sz, length, half = self.sz, self.length, self.half
        wqt, wk, wvt, wgt, _, bias_col = self.packed
        xs, _, normed, queries, keys, values, gates = self.work[:7]
        factor = math.log2(math.e) / sz.head**0.5
        inside = lax.broadcasted_iota(jnp.int32, (1, sz.lanes), 1) < sz.width
        gain_row = self.gain[...].reshape(1, sz.width)
        count = source.shape[0] // 4
        size = half // 2
        lines = [line for i in range(self.groups // 2) for line in self.tile(i, part)]
        for turn, quarter in enumerate(self.quarters[part]):
            arrive(quarter)
            blocks = source.at[pl.ds(quarter * count, count)]
            unpack_tokens(sz, blocks, xs, self.base(quarter), self.part // 2)
            x = self.gather([p for line in lines for p in self.spots(line, quarter)])
            mean = jnp.sum(x, axis=1, keepdims=True) * (1.0 / sz.width)
            centred = jnp.where(inside, x - mean, 0.0)
            spread = jnp.sum(centred * centred, axis=1, keepdims=True) * (1.0 / sz.width)
            value = centred[:, : sz.width] * lax.rsqrt(spread + 1e-05) * gain_row
            value = value.astype(BF16)
            for i in range(self.groups):
                low = i * half + turn * size
                normed[low : low + size] = value[i * size : (i + 1) * size]
        z = normed[: self.part]
        made = nn(z, wk[...]).astype(BF16)
        for index in range(self.groups // 2):
            for place, line in enumerate(self.tile(index, part)):
                low = index * length + place * half
                spot = line * length + place * half
                keys[spot : spot + half] = made[low : low + half]
        feature = lax.broadcasted_iota(jnp.int32, (sz.rows, 1), 0)
        ones_row = jnp.where(feature % sz.pad_head == sz.head, 1.0, 0.0)
        self.settle(part, queries, (nt(wqt[...], z) * factor).astype(BF16))
        self.settle(part, values, (nt(wvt[...], z) + ones_row).astype(BF16))
        self.settle(part, gates, jax.nn.sigmoid(nt(wgt[...], z) + bias_col[...]))

    def settle(self, part, ref, value):
        length = self.length
        lane = lax.broadcasted_iota(jnp.int32, (ref.shape[0], length), 1)
        for index in range(self.groups // 2):
            new = value[:, index * length : (index + 1) * length]
            even = slice(2 * index * length, (2 * index + 1) * length)
            odd = slice((2 * index + 1) * length, (2 * index + 2) * length)
            if part == 0:
                ref[:, even] = new
                continue
            old = ref[:, even]
            ref[:, even] = jnp.where(lane < self.half, old, new)
            ref[:, odd] = jnp.where(lane < self.half, new, old)

    def finish(self, emit=None):
        sz, length, run = self.sz, self.length, self.run
        wo = self.packed[4]
        ys, gated = self.work[1], self.work[9]
        mix_lines(sz, self.groups, length, self.work)
        for line in range(self.groups):
            mine = slice(line * length, (line + 1) * length)
            spots = [place for part in self.order(line) for place in self.places(line, part)]
            y = self.gather(spots) + tn(gated[:, mine], wo[...])
            if emit is not None:
                emit(line, y, [q for part in self.order(line) for q in self.quarters[part]])
                continue
            for k in range(sz.chunks):
                piece = y[:, k * LANES : (k + 1) * LANES]
                for i, place in enumerate(spots):
                    ys[k, place, :] = piece[i * run : (i + 1) * run]


def pack_tokens(sz, ys, target):
    tokens = ys.shape[1]
    n = target.shape[0]
    block = tokens // n
    tail = target.shape[2:]
    fold = math.prod(tail) // LANES
    for k in range(sz.full):
        part = ys[k].reshape((n, block // fold) + tail)
        target[:, k * block // fold : (k + 1) * block // fold] = part.astype(BF16)
    if sz.rest:
        joined = None
        for q in range(sz.side):
            part = ys[sz.full, pl.ds(q, tokens // sz.side, stride=sz.side), :]
            part = pltpu.roll(part, q * sz.rest, 1) if q else part
            joined = part if joined is None else joined + part
        part = joined.reshape((n, block // sz.side // fold) + tail)
        target[:, sz.full * block // fold :] = part.astype(BF16)


def unpack_tokens(sz, source, xs, base=0, tokens=None):
    tokens = tokens or xs.shape[1]
    n = source.shape[0]
    block = tokens // n
    fold = math.prod(source.shape[2:]) // LANES
    for k in range(sz.full):
        part = source[:, k * block // fold : (k + 1) * block // fold]
        xs[k, pl.ds(base, tokens), :] = part.astype(F32).reshape(tokens, LANES)
    if sz.rest:
        joined = source[:, sz.full * block // fold :].astype(F32)
        joined = joined.reshape(tokens // sz.side, LANES)
        inside = lax.broadcasted_iota(jnp.int32, (1, LANES), 1) < sz.rest
        for q in range(sz.side):
            part = pltpu.roll(joined, LANES - q * sz.rest, 1) if q else joined
            place = pl.ds(base + q, tokens // sz.side, stride=sz.side)
            xs[sz.full, place, :] = jnp.where(inside, part, 0.0)


def turn_tokens(sz, n, rows, source, xs, ys):
    cols, width, length = source.shape
    for c in range(cols):
        turned = source[c].astype(F32).T
        for k in range(sz.chunks):
            part = turned[:, k * LANES : min((k + 1) * LANES, width)]
            if part.shape[1] < LANES:
                pad = jnp.zeros((length, LANES - part.shape[1]), F32)
                part = jnp.concatenate([part, pad], axis=1)
            xs[k, c * length : (c + 1) * length] = part
    for k in range(sz.chunks):
        for c in range(cols):
            for r in range(rows):
                part = xs[k, pl.ds(c * length + r, n, stride=rows), :]
                ys[k, pl.ds(r * cols + c, n, stride=rows * cols), :] = part


def row_kernel(sz, n, rows, cols, *refs):
    x_ref, gain, *own_weights = refs[:5]
    next_weights = refs[5:8]
    result, *next_packed = refs[8:15]
    sent, got, back, *rest = refs[15:]
    packed, rest = rest[:6], rest[6:]
    work = rest[:10]
    send_a, recv_a, send_b, recv_b, local_sem = rest[10:]
    me = lax.axis_index("row")
    block = rows * cols

    barrier = pltpu.get_barrier_semaphore()

    def greet(step, carry):
        peer = lax.rem(me + step, n)
        pl.semaphore_signal(barrier, inc=1, device_id={"row": peer}, device_id_type=MESH)
        return carry

    lax.fori_loop(1, n, greet, 0)
    turn_tokens(sz, n, rows, x_ref, work[0], work[1])
    pack_tokens(sz, work[1], sent)
    pl.semaphore_wait(barrier, n - 1)

    def exchange(source, target, send, recv, body):
        def copy(peer, slot):
            return pltpu.make_async_remote_copy(
                src_ref=source.at[peer],
                dst_ref=target.at[slot],
                send_sem=send.at[peer],
                recv_sem=recv.at[slot],
                device_id={"row": peer},
                device_id_type=MESH,
            )

        def start(step, carry):
            copy(lax.rem(me + step, n), me).start()
            return carry

        lax.fori_loop(1, n, start, 0)
        own = pltpu.make_async_copy(source.at[me], target.at[me], local_sem)
        own.start()
        body()
        own.wait()

        def finish(step, carry):
            peer = lax.rem(me + step, n)
            copy(peer, me).wait_send()
            copy(peer, peer).wait_recv()
            return carry

        lax.fori_loop(1, n, finish, 0)

    exchange(
        sent,
        got,
        send_a,
        recv_a,
        lambda: prepare(sz, own_weights, packed),
    )
    unpack_tokens(sz, got, work[0])
    attend(
        sz, rows, n * cols, lambda g, c: g * cols + c, block, cols, gain, packed, work
    )
    pack_tokens(sz, work[1], back)
    exchange(
        back,
        result,
        send_b,
        recv_b,
        lambda: prepare(sz, next_weights, next_packed),
    )


def col_kernel(sz, cols, x_ref, gain, *refs):
    packed, result, work = refs[:6], refs[6], refs[7:]
    unpack_tokens(sz, x_ref, work[0])
    length = work[0].shape[1] // cols

    def emit(group, y):
        result[group] = y[:, : sz.width].T.astype(BF16)

    attend(sz, cols, length, lambda g, c: g, cols, 1, gain, packed, work, emit)


def axial_kernel(sz, n, rows, cols, *refs):
    outer, result, refs = refs[:9], refs[9], refs[10:]
    local, refs = refs[:9], refs[9:]
    sent, got, back, home, *refs = refs
    packed_row, packed_col, refs = refs[:6], refs[6:12], refs[12:]
    work = refs[:10]
    load_sem, send_a, recv_a, send_b, recv_b = refs[10:]
    x_ref, row_gain, *row_weights = local[:5]
    col_gain, *col_weights = local[5:]
    me = lax.axis_index("row")
    block = rows * cols
    length = n * cols

    def steps(low, high, body):
        def step(i, carry):
            body(i)
            return carry

        lax.fori_loop(low, high, step, 0)

    def partner(i):
        return lax.rem(me + i, n)

    barrier = pltpu.get_barrier_semaphore()

    def greet(i):
        peer = partner(i)
        pl.semaphore_signal(barrier, inc=1, device_id={"row": peer}, device_id_type=MESH)

    steps(1, n, greet)
    loads = [
        pltpu.make_async_copy(source, target, load_sem.at[i])
        for i, (source, target) in enumerate(zip(outer, local))
    ]
    for load in loads:
        load.start()

    fourth = n // 4
    layer = me // fourth

    class Exchange:
        def __init__(self, source, target, send, recv):
            self.source, self.target = source, target
            self.send, self.recv = send, recv
            self.own = pltpu.make_async_copy(source.at[me], target.at[me], recv.at[layer])

        def copy(self, peer):
            return pltpu.make_async_remote_copy(
                src_ref=self.source.at[peer],
                dst_ref=self.target.at[me],
                send_sem=self.send,
                recv_sem=self.recv.at[layer],
                device_id={"row": peer},
                device_id_type=MESH,
            )

        def visit(self, quarter, body):
            low = 1 if quarter is layer else 0
            steps(low, fourth, lambda i: body(quarter * fourth + lax.rem(me + i, fourth)))

        def start(self, quarters=None):
            self.own.start()
            if quarters is None:
                steps(1, n, lambda i: self.copy(partner(i)).start())
                return
            for quarter in quarters:
                self.visit(quarter, lambda peer: self.copy(peer).start())

        def arrive(self, quarter):
            blocks = self.target.at[pl.ds(quarter * fourth, fourth)]
            pltpu.make_async_copy(blocks, blocks, self.recv.at[quarter]).wait()

        def leave(self):
            blocks = self.source.at[: n - 1]
            pltpu.make_async_copy(blocks, blocks, self.send).wait()

    def choose(*table):
        return sum(jnp.where(layer == i, value, 0) for i, value in enumerate(table))

    first = Exchange(sent, got, send_a, recv_a)
    second = Exchange(back, home, send_b, recv_b)
    early = ((layer, choose(1, 0, 3, 2)), (choose(2, 2, 1, 1), choose(3, 3, 0, 0)))
    late = ((layer, choose(2, 0, 0, 2)), (choose(1, 2, 1, 0), choose(3, 3, 3, 1)))
    loads[0].wait()
    turn_tokens(sz, n, rows, x_ref, work[0], work[1])
    pack_tokens(sz, work[1], sent)
    pl.semaphore_wait(barrier, n - 1)
    first.start(early[0] + early[1])
    for load in loads[1:]:
        load.wait()
    prepare(sz, row_weights, packed_row)
    prepare(sz, col_weights, packed_col)
    place = lambda g, c: g * cols + c
    lines = Lines(sz, rows, length, place, block, cols, row_gain, packed_row, work, early)
    for part in range(2):
        lines.absorb(part, got, first.arrive)
    lines.finish()
    pack_tokens(sz, work[1], back)
    second.start()
    first.leave()
    height = n * rows
    place = lambda g, c: g
    lines = Lines(sz, cols, height, place, cols, 1, col_gain, packed_col, work, late)
    for part in range(2):
        lines.absorb(part, home, second.arrive)
    ys = work[1]
    size = height // 4

    def emit(line, y, quarters):
        low = line * height
        for i, quarter in enumerate(quarters):
            spot = pl.multiple_of(low + quarter * size, size)
            for k in range(sz.chunks):
                piece = y[i * size : (i + 1) * size, k * LANES : (k + 1) * LANES]
                ys[k, pl.ds(spot, size), :] = piece
        y = jnp.concatenate([ys[k, low : low + height] for k in range(sz.chunks)], axis=1)
        result[line] = y[:, : sz.width].T.astype(BF16)

    lines.finish(emit)
    second.leave()


def swap_columns(sz, done, block, rows, cols):
    n = done.shape[0]
    parts = [done[:, k * block : (k + 1) * block] for k in range(sz.full)]
    if sz.rest:
        parts.append(done[:, sz.full * block :].reshape(n, block, sz.rest))
    whole = jnp.concatenate(parts, -1).reshape(rows, cols, sz.width)
    whole = lax.all_to_all(whole, "col", split_axis=1, concat_axis=0, tiled=True)
    whole = whole.reshape(n, block, sz.width)
    parts = [whole[..., k * LANES : (k + 1) * LANES] for k in range(sz.full)]
    if sz.rest:
        parts.append(whole[..., sz.full * LANES :].reshape(n, block // sz.side, LANES))
    return jnp.concatenate(parts, 1)


VMEM = pl.BlockSpec(memory_space=pltpu.VMEM)


def per_device(
    pair_map, row_gain, row_proj, row_gate_bias, row_out, col_gain, col_proj, col_gate_bias, col_out
):
    local_rows, local_cols, width = pair_map.shape
    n = lax.axis_size("row")
    sz = Sizes(width)
    rows = local_rows // n
    tokens = local_rows * local_cols
    block = rows * local_cols
    shape = (n, sz.packed_rows(block), LANES)
    turned = jnp.transpose(pair_map, (1, 2, 0))
    splits = lax.axis_size("col")
    folds = shape[1] % FOLD == 0 and block % (FOLD * sz.side) == 0
    even = rows % 2 == 0 and local_cols % 2 == 0 and n % 4 == 0
    if splits == 1 and folds and even and n * local_cols == local_rows == LANES:
        folded = (n, shape[1] // FOLD, FOLD, LANES)
        operands = (turned, row_gain, row_proj, row_gate_bias, row_out)
        operands += (col_gain, col_proj, col_gate_bias, col_out)
        operands = [pltpu.with_memory_space_constraint(a, pltpu.HBM) for a in operands]
        updated = pl.pallas_call(
            functools.partial(axial_kernel, sz, n, rows, local_cols),
            out_shape=jax.ShapeDtypeStruct(turned.shape, BF16),
            in_specs=[pl.BlockSpec(memory_space=pltpu.HBM)] * len(operands),
            out_specs=VMEM,
            scratch_shapes=[pltpu.VMEM(a.shape, a.dtype) for a in operands]
            + [pltpu.VMEM(folded, BF16)] * 4
            + [pltpu.VMEM(*spec) for spec in sz.packed_shapes()] * 2
            + sz.work_scratch(tokens, max(n * local_cols, local_rows))
            + [pltpu.SemaphoreType.DMA((len(operands),))]
            + [pltpu.SemaphoreType.DMA, pltpu.SemaphoreType.DMA((4,))] * 2,
            compiler_params=pltpu.CompilerParams(
                collective_id=0, has_side_effects=True, vmem_limit_bytes=VMEM_LIMIT
            ),
            name="axial_attention",
        )(*operands)
        return jnp.transpose(updated, (2, 0, 1))
    done, *packed = pl.pallas_call(
        functools.partial(row_kernel, sz, n, rows, local_cols),
        out_shape=[jax.ShapeDtypeStruct(shape, BF16)]
        + [jax.ShapeDtypeStruct(*spec) for spec in sz.packed_shapes()],
        in_specs=[VMEM] * 8,
        out_specs=[VMEM] * 7,
        scratch_shapes=[pltpu.VMEM(shape, BF16)] * 3
        + [pltpu.VMEM(*spec) for spec in sz.packed_shapes()]
        + sz.work_scratch(tokens, n * local_cols)
        + [pltpu.SemaphoreType.DMA((n,))] * 4
        + [pltpu.SemaphoreType.DMA],
        compiler_params=pltpu.CompilerParams(collective_id=0, has_side_effects=True),
        name="row_attention",
    )(turned, row_gain, row_proj, row_gate_bias, row_out, col_proj, col_gate_bias, col_out)
    if splits > 1:
        done = swap_columns(sz, done, block, local_rows, local_cols)
    cols = local_cols // splits
    full = tokens // cols
    updated = pl.pallas_call(
        functools.partial(col_kernel, sz, cols),
        out_shape=jax.ShapeDtypeStruct((cols, width, full), BF16),
        in_specs=[VMEM] * 8,
        out_specs=VMEM,
        scratch_shapes=sz.work_scratch(tokens, full),
        name="col_attention",
    )(done, col_gain, *packed)
    updated = jnp.transpose(updated, (2, 0, 1))
    if splits > 1:
        updated = lax.all_to_all(updated, "col", split_axis=0, concat_axis=1, tiled=True)
    return updated


def solution(mesh):
    return jax.shard_map(
        per_device,
        mesh=mesh,
        in_specs=(P(("groups", "col"), "row", None), P(), P(), P(), P(), P(), P(), P(), P()),
        out_specs=P(("groups", "col"), "row", None),
        check_vma=False,
    )
```

```python
import functools
import math

import jax
import jax.numpy as jnp
from jax import lax
from jax.experimental import pallas as pl
from jax.experimental.pallas import tpu as pltpu
from jax.sharding import PartitionSpec as P

HEADS = 8
LANES = 128
FOLD = 4
VMEM_LIMIT = 32 * 2**20
F32 = jnp.float32
BF16 = jnp.bfloat16
MESH = pl.DeviceIdType.MESH


def ceil_to(value, step):
    return -(-value // step) * step


def nt(a, b):
    return lax.dot_general(a, b, (((1,), (1,)), ((), ())), preferred_element_type=F32)


def tn(a, b):
    return lax.dot_general(a, b, (((0,), (0,)), ((), ())), preferred_element_type=F32)


def nn(a, b):
    return jnp.dot(a, b, preferred_element_type=F32)


class Sizes:
    def __init__(self, width):
        self.width = width
        self.head = width // HEADS
        self.pad_head = ceil_to(self.head + 1, 16)
        self.pad_key = LANES // (LANES // self.head)
        while LANES % self.pad_key:
            self.pad_key += 1
        self.rows = HEADS * self.pad_head
        self.keys = HEADS * self.pad_key
        assert self.pad_head <= self.pad_key
        self.lanes = ceil_to(width, LANES)
        self.chunks = self.lanes // LANES
        self.full = width // LANES
        self.rest = width % LANES
        self.side = LANES // self.rest if self.rest else 1

    def packed_rows(self, block):
        assert self.rest == 0 or (LANES % self.rest == 0 and block % self.side == 0)
        return self.full * block + (block // self.side if self.rest else 0)

    def packed_shapes(self):
        return [
            ((self.rows, self.width), BF16),
            ((self.width, self.keys), BF16),
            ((self.rows, self.width), BF16),
            ((self.rows, self.width), BF16),
            ((self.rows, self.lanes), BF16),
            ((self.rows, 1), F32),
        ]

    def work_scratch(self, tokens, length):
        return [
            pltpu.VMEM((self.chunks, tokens, LANES), F32),
            pltpu.VMEM((self.chunks, tokens, LANES), F32),
            pltpu.VMEM((tokens, self.width), BF16),
            pltpu.VMEM((self.rows, tokens), BF16),
            pltpu.VMEM((tokens, self.keys), BF16),
            pltpu.VMEM((self.rows, tokens), BF16),
            pltpu.VMEM((self.rows, tokens), F32),
            pltpu.VMEM((2, length, HEADS * length), F32),
            pltpu.VMEM((2, length, HEADS * length), BF16),
            pltpu.VMEM((self.rows, tokens), BF16),
        ]


def prepare(sz, weights, packed):
    proj, bias, out = weights
    wqt, wk, wvt, wgt, wo, bias_col = packed

    def window(block):
        start = block * sz.width
        low = start // LANES * LANES
        high = min(ceil_to(start + sz.width, LANES), 4 * sz.width)
        return proj[:, low:high], start - low, high - low

    def hits(shape, axis, pad, shift):
        place = lax.broadcasted_iota(jnp.int32, shape, axis)
        source = lax.broadcasted_iota(jnp.int32, shape, 1 - axis) - shift
        inner = place % pad
        return (inner < sz.head) & (source == place // pad * sz.head + inner)

    def pick(*spec):
        return jnp.where(hits(*spec), 1.0, 0.0).astype(BF16)

    part, shift, size = window(1)
    wk[...] = nn(part, pick((size, sz.keys), 1, sz.pad_key, shift)).astype(BF16)
    for block, ref, pad in ((0, wqt, sz.pad_head), (2, wvt, sz.pad_head), (3, wgt, sz.pad_head)):
        part, shift, size = window(block)
        ref[...] = nt(pick((HEADS * pad, size), 0, pad, shift), part).astype(BF16)
    spec = (sz.rows, sz.width), 0, sz.pad_head, 0
    wo[...] = jnp.zeros(wo.shape, BF16)
    wo[:, : sz.width] = nn(pick(*spec), out[...]).astype(BF16)
    row = bias[...].reshape(1, sz.width)
    bias_col[...] = jnp.sum(jnp.where(hits(*spec), row, 0.0), axis=1, keepdims=True)


def mix_lines(sz, groups, length, work):
    queries, keys, values, gates, scores, weights, gated = work[3:]
    pack = LANES // sz.pad_key
    spare = sz.pad_key - sz.pad_head
    zeros = jnp.zeros((sz.pad_key, length), BF16)

    def score(group):
        mine = slice(group * length, (group + 1) * length)
        for first in range(0, HEADS, pack):
            blocks = []
            for j in range(pack):
                low = (first + j) * sz.pad_head
                own = queries[low : low + sz.pad_head, mine]
                if spare:
                    gap = jnp.zeros((spare, length), BF16)
                    own = jnp.concatenate([own, gap], axis=0)
                blocks.append(
                    jnp.concatenate([own if i == j else zeros for i in range(pack)], axis=1)
                )
            lanes = slice(first * sz.pad_key, (first + pack) * sz.pad_key)
            scores[group % 2, :, first * length : (first + pack) * length] = nn(
                keys[mine, lanes], jnp.concatenate(blocks, axis=0)
            )

    def soften(group):
        for head in range(HEADS):
            lanes = slice(head * length, (head + 1) * length)
            s = scores[group % 2, :, lanes]
            top = jnp.max(s, axis=0, keepdims=True)
            weights[group % 2, :, lanes] = jnp.exp2(s - top).astype(BF16)

    def mix(group):
        mine = slice(group * length, (group + 1) * length)
        for head in range(HEADS):
            rows = slice(head * sz.pad_head, (head + 1) * sz.pad_head)
            lanes = slice(head * length, (head + 1) * length)
            mixed = nn(values[rows, mine], weights[group % 2, :, lanes])
            total = mixed[sz.head : sz.head + 1]
            gated[rows, mine] = (mixed * (1.0 / total) * gates[rows, mine]).astype(BF16)

    score(0)
    for group in range(groups):
        if group + 1 < groups:
            score(group + 1)
        soften(group)
        if group > 0:
            mix(group - 1)
    mix(groups - 1)


def attend(sz, groups, length, start_of, stride, per_group, gain, packed, work, emit=None):
    wqt, wk, wvt, wgt, wo, bias_col = packed
    xs, ys, normed, queries, keys, values, gates = work[:7]
    gated = work[9]
    run = length // per_group
    factor = math.log2(math.e) / sz.head**0.5
    lane = lax.broadcasted_iota(jnp.int32, (1, sz.lanes), 1)
    inside = lane < sz.width
    gain_row = gain[...].reshape(1, sz.width)

    def places(group):
        return [pl.ds(start_of(group, c), run, stride=stride) for c in range(per_group)]

    def tokens_of(group):
        parts = [
            jnp.concatenate([xs[k, place, :] for place in places(group)], axis=0)
            for k in range(sz.chunks)
        ]
        return jnp.concatenate(parts, axis=1)

    for group in range(groups):
        x = tokens_of(group)
        mean = jnp.sum(x, axis=1, keepdims=True) * (1.0 / sz.width)
        centred = jnp.where(inside, x - mean, 0.0)
        spread = jnp.sum(centred * centred, axis=1, keepdims=True) * (1.0 / sz.width)
        value = centred[:, : sz.width] * lax.rsqrt(spread + 1e-05) * gain_row
        normed[group * length : (group + 1) * length] = value.astype(BF16)
    z = normed[...]
    feature = lax.broadcasted_iota(jnp.int32, (sz.rows, 1), 0)
    ones_row = jnp.where(feature % sz.pad_head == sz.head, 1.0, 0.0)
    queries[...] = (nt(wqt[...], z) * factor).astype(BF16)
    keys[...] = nn(z, wk[...]).astype(BF16)
    values[...] = (nt(wvt[...], z) + ones_row).astype(BF16)
    gates[...] = jax.nn.sigmoid(nt(wgt[...], z) + bias_col[...])
    mix_lines(sz, groups, length, work)
    for group in range(groups):
        mine = slice(group * length, (group + 1) * length)
        y = tokens_of(group) + tn(gated[:, mine], wo[...])
        if emit is not None:
            emit(group, y)
            continue
        for k in range(sz.chunks):
            part = y[:, k * LANES : (k + 1) * LANES]
            for c, place in enumerate(places(group)):
                ys[k, place, :] = part[c * run : (c + 1) * run]


class Lines:
    def __init__(self, sz, groups, length, start_of, stride, per_group, gain, packed, work, quarters):
        self.sz, self.groups, self.length = sz, groups, length
        self.quarters = quarters
        self.gain, self.packed, self.work = gain, packed, work
        self.half = length // 2
        self.part = groups * self.half
        self.start_of, self.stride, self.per_group = start_of, stride, per_group
        self.run = self.half // 2 // per_group

    def order(self, line):
        return (0, 1) if line % 2 == 0 else (1, 0)

    def base(self, quarter):
        size = self.part // 2
        return pl.multiple_of(quarter * size, size)

    def places(self, line, part):
        return [
            pl.ds(self.base(quarter) + self.start_of(line, c), self.run, stride=self.stride)
            for quarter in self.quarters[part]
            for c in range(self.per_group)
        ]

    def gather(self, spots):
        xs = self.work[0]
        parts = [
            jnp.concatenate([xs[k, place, :] for place in spots], axis=0)
            for k in range(self.sz.chunks)
        ]
        return jnp.concatenate(parts, axis=1)

    def tile(self, index, part):
        lines = (2 * index, 2 * index + 1)
        return lines if part == 0 else lines[::-1]

    def absorb(self, part, source):
        sz, length, half = self.sz, self.length, self.half
        wqt, wk, wvt, wgt, _, bias_col = self.packed
        xs, _, normed, queries, keys, values, gates = self.work[:7]
        count = source.shape[0] // 4
        for quarter in self.quarters[part]:
            blocks = source.at[pl.ds(quarter * count, count)]
            unpack_tokens(sz, blocks, xs, self.base(quarter), self.part // 2)
        factor = math.log2(math.e) / sz.head**0.5
        inside = lax.broadcasted_iota(jnp.int32, (1, sz.lanes), 1) < sz.width
        gain_row = self.gain[...].reshape(1, sz.width)
        for index in range(self.groups // 2):
            first, second = self.tile(index, part)
            x = self.gather(self.places(first, part) + self.places(second, part))
            mean = jnp.sum(x, axis=1, keepdims=True) * (1.0 / sz.width)
            centred = jnp.where(inside, x - mean, 0.0)
            spread = jnp.sum(centred * centred, axis=1, keepdims=True) * (1.0 / sz.width)
            value = centred[:, : sz.width] * lax.rsqrt(spread + 1e-05) * gain_row
            normed[index * length : (index + 1) * length] = value.astype(BF16)
        z = normed[: self.part]
        made = nn(z, wk[...]).astype(BF16)
        for index in range(self.groups // 2):
            for place, line in enumerate(self.tile(index, part)):
                low = index * length + place * half
                spot = line * length + place * half
                keys[spot : spot + half] = made[low : low + half]
        feature = lax.broadcasted_iota(jnp.int32, (sz.rows, 1), 0)
        ones_row = jnp.where(feature % sz.pad_head == sz.head, 1.0, 0.0)
        self.settle(part, queries, (nt(wqt[...], z) * factor).astype(BF16))
        self.settle(part, values, (nt(wvt[...], z) + ones_row).astype(BF16))
        logits = nt(wgt[...], z) + bias_col[...]
        self.settle(part, gates, 0.5 * jnp.tanh(0.5 * logits) + 0.5)

    def settle(self, part, ref, value):
        length = self.length
        lane = lax.broadcasted_iota(jnp.int32, (ref.shape[0], length), 1)
        for index in range(self.groups // 2):
            new = value[:, index * length : (index + 1) * length]
            even = slice(2 * index * length, (2 * index + 1) * length)
            odd = slice((2 * index + 1) * length, (2 * index + 2) * length)
            if part == 0:
                ref[:, even] = new
                continue
            old = ref[:, even]
            ref[:, even] = jnp.where(lane < self.half, old, new)
            ref[:, odd] = jnp.where(lane < self.half, new, old)

    def finish(self, emit=None):
        sz, length, run = self.sz, self.length, self.run
        wo = self.packed[4]
        ys, gated = self.work[1], self.work[9]
        mix_lines(sz, self.groups, length, self.work)
        for line in range(self.groups):
            mine = slice(line * length, (line + 1) * length)
            spots = [place for part in self.order(line) for place in self.places(line, part)]
            y = self.gather(spots) + tn(gated[:, mine], wo[...])
            if emit is not None:
                emit(line, y, [q for part in self.order(line) for q in self.quarters[part]])
                continue
            for k in range(sz.chunks):
                piece = y[:, k * LANES : (k + 1) * LANES]
                for i, place in enumerate(spots):
                    ys[k, place, :] = piece[i * run : (i + 1) * run]


def pack_tokens(sz, ys, target):
    tokens = ys.shape[1]
    n = target.shape[0]
    block = tokens // n
    tail = target.shape[2:]
    fold = math.prod(tail) // LANES
    for k in range(sz.full):
        part = ys[k].reshape((n, block // fold) + tail)
        target[:, k * block // fold : (k + 1) * block // fold] = part.astype(BF16)
    if sz.rest:
        joined = None
        for q in range(sz.side):
            part = ys[sz.full, pl.ds(q, tokens // sz.side, stride=sz.side), :]
            part = pltpu.roll(part, q * sz.rest, 1) if q else part
            joined = part if joined is None else joined + part
        part = joined.reshape((n, block // sz.side // fold) + tail)
        target[:, sz.full * block // fold :] = part.astype(BF16)


def unpack_tokens(sz, source, xs, base=0, tokens=None):
    tokens = tokens or xs.shape[1]
    n = source.shape[0]
    block = tokens // n
    fold = math.prod(source.shape[2:]) // LANES
    for k in range(sz.full):
        part = source[:, k * block // fold : (k + 1) * block // fold]
        xs[k, pl.ds(base, tokens), :] = part.astype(F32).reshape(tokens, LANES)
    if sz.rest:
        joined = source[:, sz.full * block // fold :].astype(F32)
        joined = joined.reshape(tokens // sz.side, LANES)
        inside = lax.broadcasted_iota(jnp.int32, (1, LANES), 1) < sz.rest
        for q in range(sz.side):
            part = pltpu.roll(joined, LANES - q * sz.rest, 1) if q else joined
            place = pl.ds(base + q, tokens // sz.side, stride=sz.side)
            xs[sz.full, place, :] = jnp.where(inside, part, 0.0)


def turn_tokens(sz, n, rows, source, xs, ys):
    cols, width, length = source.shape
    for c in range(cols):
        turned = source[c].astype(F32).T
        for k in range(sz.chunks):
            part = turned[:, k * LANES : min((k + 1) * LANES, width)]
            if part.shape[1] < LANES:
                pad = jnp.zeros((length, LANES - part.shape[1]), F32)
                part = jnp.concatenate([part, pad], axis=1)
            xs[k, c * length : (c + 1) * length] = part
    for k in range(sz.chunks):
        for c in range(cols):
            for r in range(rows):
                part = xs[k, pl.ds(c * length + r, n, stride=rows), :]
                ys[k, pl.ds(r * cols + c, n, stride=rows * cols), :] = part


def row_kernel(sz, n, rows, cols, *refs):
    x_ref, gain, *own_weights = refs[:5]
    next_weights = refs[5:8]
    result, *next_packed = refs[8:15]
    sent, got, back, *rest = refs[15:]
    packed, rest = rest[:6], rest[6:]
    work = rest[:10]
    send_a, recv_a, send_b, recv_b, local_sem = rest[10:]
    me = lax.axis_index("row")
    block = rows * cols

    barrier = pltpu.get_barrier_semaphore()

    def greet(step, carry):
        peer = lax.rem(me + step, n)
        pl.semaphore_signal(barrier, inc=1, device_id={"row": peer}, device_id_type=MESH)
        return carry

    lax.fori_loop(1, n, greet, 0)
    turn_tokens(sz, n, rows, x_ref, work[0], work[1])
    pack_tokens(sz, work[1], sent)
    pl.semaphore_wait(barrier, n - 1)

    def exchange(source, target, send, recv, body):
        def copy(peer, slot):
            return pltpu.make_async_remote_copy(
                src_ref=source.at[peer],
                dst_ref=target.at[slot],
                send_sem=send.at[peer],
                recv_sem=recv.at[slot],
                device_id={"row": peer},
                device_id_type=MESH,
            )

        def start(step, carry):
            copy(lax.rem(me + step, n), me).start()
            return carry

        lax.fori_loop(1, n, start, 0)
        own = pltpu.make_async_copy(source.at[me], target.at[me], local_sem)
        own.start()
        body()
        own.wait()

        def finish(step, carry):
            peer = lax.rem(me + step, n)
            copy(peer, me).wait_send()
            copy(peer, peer).wait_recv()
            return carry

        lax.fori_loop(1, n, finish, 0)

    exchange(
        sent,
        got,
        send_a,
        recv_a,
        lambda: prepare(sz, own_weights, packed),
    )
    unpack_tokens(sz, got, work[0])
    attend(
        sz, rows, n * cols, lambda g, c: g * cols + c, block, cols, gain, packed, work
    )
    pack_tokens(sz, work[1], back)
    exchange(
        back,
        result,
        send_b,
        recv_b,
        lambda: prepare(sz, next_weights, next_packed),
    )


def col_kernel(sz, cols, x_ref, gain, *refs):
    packed, result, work = refs[:6], refs[6], refs[7:]
    unpack_tokens(sz, x_ref, work[0])
    length = work[0].shape[1] // cols

    def emit(group, y):
        result[group] = y[:, : sz.width].T.astype(BF16)

    attend(sz, cols, length, lambda g, c: g, cols, 1, gain, packed, work, emit)


def axial_kernel(sz, n, rows, cols, *refs):
    outer, result, refs = refs[:9], refs[9], refs[10:]
    local, refs = refs[:9], refs[9:]
    sent, got, back, home, *refs = refs
    packed_row, packed_col, refs = refs[:6], refs[6:12], refs[12:]
    work = refs[:10]
    load_sem, send_a, recv_a, send_b, recv_b = refs[10:]
    x_ref, row_gain, *row_weights = local[:5]
    col_gain, *col_weights = local[5:]
    me = lax.axis_index("row")
    block = rows * cols
    length = n * cols

    def steps(low, high, body):
        def step(i, carry):
            body(i)
            return carry

        lax.fori_loop(low, high, step, 0)

    def partner(i):
        return lax.rem(me + i, n)

    barrier = pltpu.get_barrier_semaphore()

    def greet(i):
        peer = partner(i)
        pl.semaphore_signal(barrier, inc=1, device_id={"row": peer}, device_id_type=MESH)

    steps(1, n, greet)
    loads = [
        pltpu.make_async_copy(source, target, load_sem.at[i])
        for i, (source, target) in enumerate(zip(outer, local))
    ]
    for load in loads:
        load.start()

    fourth = n // 4
    layer = me // fourth

    class Exchange:
        def __init__(self, source, target, send, recv):
            self.source, self.target = source, target
            self.send, self.recv = send, recv
            self.own = pltpu.make_async_copy(source.at[me], target.at[me], recv.at[layer])

        def copy(self, peer):
            return pltpu.make_async_remote_copy(
                src_ref=self.source.at[peer],
                dst_ref=self.target.at[me],
                send_sem=self.send,
                recv_sem=self.recv.at[layer],
                device_id={"row": peer},
                device_id_type=MESH,
            )

        def visit(self, quarter, body):
            low = 1 if quarter is layer else 0
            steps(low, fourth, lambda i: body(quarter * fourth + lax.rem(me + i, fourth)))

        def start(self, quarters=None):
            self.own.start()
            if quarters is None:
                steps(1, n, lambda i: self.copy(partner(i)).start())
                return
            for quarter in quarters:
                self.visit(quarter, lambda peer: self.copy(peer).start())

        def arrive(self, quarters):
            for quarter in quarters:
                blocks = self.target.at[pl.ds(quarter * fourth, fourth)]
                pltpu.make_async_copy(blocks, blocks, self.recv.at[quarter]).wait()
            return self.target

        def leave(self):
            blocks = self.source.at[: n - 1]
            pltpu.make_async_copy(blocks, blocks, self.send).wait()

    def choose(*table):
        return sum(jnp.where(layer == i, value, 0) for i, value in enumerate(table))

    first = Exchange(sent, got, send_a, recv_a)
    second = Exchange(back, home, send_b, recv_b)
    early = ((layer, choose(1, 0, 3, 2)), (choose(2, 2, 1, 1), choose(3, 3, 0, 0)))
    late = ((layer, choose(2, 0, 0, 2)), (choose(1, 2, 1, 0), choose(3, 3, 3, 1)))
    loads[0].wait()
    turn_tokens(sz, n, rows, x_ref, work[0], work[1])
    pack_tokens(sz, work[1], sent)
    pl.semaphore_wait(barrier, n - 1)
    first.start(early[0] + early[1])
    for load in loads[1:]:
        load.wait()
    prepare(sz, row_weights, packed_row)
    place = lambda g, c: g * cols + c
    lines = Lines(sz, rows, length, place, block, cols, row_gain, packed_row, work, early)
    for part in range(2):
        lines.absorb(part, first.arrive(early[part]))
    lines.finish()
    pack_tokens(sz, work[1], back)
    second.start()
    prepare(sz, col_weights, packed_col)
    first.leave()
    height = n * rows
    place = lambda g, c: g
    lines = Lines(sz, cols, height, place, cols, 1, col_gain, packed_col, work, late)
    for part in range(2):
        lines.absorb(part, second.arrive(late[part]))
    ys = work[1]
    size = height // 4

    def emit(line, y, quarters):
        low = line * height
        for i, quarter in enumerate(quarters):
            spot = pl.multiple_of(low + quarter * size, size)
            for k in range(sz.chunks):
                piece = y[i * size : (i + 1) * size, k * LANES : (k + 1) * LANES]
                ys[k, pl.ds(spot, size), :] = piece
        y = jnp.concatenate([ys[k, low : low + height] for k in range(sz.chunks)], axis=1)
        result[line] = y[:, : sz.width].T.astype(BF16)

    lines.finish(emit)
    second.leave()


def swap_columns(sz, done, block, rows, cols):
    n = done.shape[0]
    parts = [done[:, k * block : (k + 1) * block] for k in range(sz.full)]
    if sz.rest:
        parts.append(done[:, sz.full * block :].reshape(n, block, sz.rest))
    whole = jnp.concatenate(parts, -1).reshape(rows, cols, sz.width)
    whole = lax.all_to_all(whole, "col", split_axis=1, concat_axis=0, tiled=True)
    whole = whole.reshape(n, block, sz.width)
    parts = [whole[..., k * LANES : (k + 1) * LANES] for k in range(sz.full)]
    if sz.rest:
        parts.append(whole[..., sz.full * LANES :].reshape(n, block // sz.side, LANES))
    return jnp.concatenate(parts, 1)


VMEM = pl.BlockSpec(memory_space=pltpu.VMEM)


def per_device(
    pair_map, row_gain, row_proj, row_gate_bias, row_out, col_gain, col_proj, col_gate_bias, col_out
):
    local_rows, local_cols, width = pair_map.shape
    n = lax.axis_size("row")
    sz = Sizes(width)
    rows = local_rows // n
    tokens = local_rows * local_cols
    block = rows * local_cols
    shape = (n, sz.packed_rows(block), LANES)
    turned = jnp.transpose(pair_map, (1, 2, 0))
    splits = lax.axis_size("col")
    folds = shape[1] % FOLD == 0 and block % (FOLD * sz.side) == 0
    even = rows % 2 == 0 and local_cols % 2 == 0 and n % 4 == 0
    if splits == 1 and folds and even and n * local_cols == local_rows == LANES:
        folded = (n, shape[1] // FOLD, FOLD, LANES)
        operands = (turned, row_gain, row_proj, row_gate_bias, row_out)
        operands += (col_gain, col_proj, col_gate_bias, col_out)
        operands = [pltpu.with_memory_space_constraint(a, pltpu.HBM) for a in operands]
        updated = pl.pallas_call(
            functools.partial(axial_kernel, sz, n, rows, local_cols),
            out_shape=jax.ShapeDtypeStruct(turned.shape, BF16),
            in_specs=[pl.BlockSpec(memory_space=pltpu.HBM)] * len(operands),
            out_specs=VMEM,
            scratch_shapes=[pltpu.VMEM(a.shape, a.dtype) for a in operands]
            + [pltpu.VMEM(folded, BF16)] * 4
            + [pltpu.VMEM(*spec) for spec in sz.packed_shapes()] * 2
            + sz.work_scratch(tokens, max(n * local_cols, local_rows))
            + [pltpu.SemaphoreType.DMA((len(operands),))]
            + [pltpu.SemaphoreType.DMA, pltpu.SemaphoreType.DMA((4,))] * 2,
            compiler_params=pltpu.CompilerParams(
                collective_id=0, has_side_effects=True, vmem_limit_bytes=VMEM_LIMIT
            ),
            name="axial_attention",
        )(*operands)
        return jnp.transpose(updated, (2, 0, 1))
    done, *packed = pl.pallas_call(
        functools.partial(row_kernel, sz, n, rows, local_cols),
        out_shape=[jax.ShapeDtypeStruct(shape, BF16)]
        + [jax.ShapeDtypeStruct(*spec) for spec in sz.packed_shapes()],
        in_specs=[VMEM] * 8,
        out_specs=[VMEM] * 7,
        scratch_shapes=[pltpu.VMEM(shape, BF16)] * 3
        + [pltpu.VMEM(*spec) for spec in sz.packed_shapes()]
        + sz.work_scratch(tokens, n * local_cols)
        + [pltpu.SemaphoreType.DMA((n,))] * 4
        + [pltpu.SemaphoreType.DMA],
        compiler_params=pltpu.CompilerParams(collective_id=0, has_side_effects=True),
        name="row_attention",
    )(turned, row_gain, row_proj, row_gate_bias, row_out, col_proj, col_gate_bias, col_out)
    if splits > 1:
        done = swap_columns(sz, done, block, local_rows, local_cols)
    cols = local_cols // splits
    full = tokens // cols
    updated = pl.pallas_call(
        functools.partial(col_kernel, sz, cols),
        out_shape=jax.ShapeDtypeStruct((cols, width, full), BF16),
        in_specs=[VMEM] * 8,
        out_specs=VMEM,
        scratch_shapes=sz.work_scratch(tokens, full),
        name="col_attention",
    )(done, col_gain, *packed)
    updated = jnp.transpose(updated, (2, 0, 1))
    if splits > 1:
        updated = lax.all_to_all(updated, "col", split_axis=0, concat_axis=1, tiled=True)
    return updated


def solution(mesh):
    return jax.shard_map(
        per_device,
        mesh=mesh,
        in_specs=(P(("groups", "col"), "row", None), P(), P(), P(), P(), P(), P(), P(), P()),
        out_specs=P(("groups", "col"), "row", None),
        check_vma=False,
    )
```
